128 devices in a mesh: ty: 8 (over x, core), tx: 16 (over z, y).
Axes of the slice: x: 4, y: 4, z: 4, core: 2. Of those that a mesh axis runs over, the one named last changes fastest.
Arguments:
- exposures: float32 [1024, 128, 128], P(('ty', 'tx')), may hold values from -70 to 70
- point_spread: float32 [1024, 31, 31], P(('ty', 'tx')), may hold values from 0.0001 to 1
- warp_steps: int32 [1024, 2], P(('ty', 'tx')), may hold values from 0 to 3
- column: int32 [1024, 1], P(('ty', 'tx')), may hold values from 0 to 15; in each aligned block of 8 rows (0 to 7, 8 to 15, ...) at most 2 rows name the same one
- block_cell: int32 [1024], P(('ty', 'tx')), may hold values from 0 to 15
Outputs:
- solution: float32 [4096, 8192], P('ty', 'tx')
- residual: float32 [4096, 8192], P('ty', 'tx')
The draws below stay inside these ranges and needn't reach their ends.
Inputs may be any that keep to these rules, and one draw needn't show every extreme that they name: `column`: among the 8 frame blocks of one device (aligned blocks of 8 rows) no value occurs more than 2 times, and in some such block one value occurs exactly 2 times.
All inputs are finite; a program needn't handle non-finite values.
Results may differ from the reference program's by a relative error of at most 0.0042.
Values may be sent and summed in bfloat16 or wider, within the bound.
No kernel may reach another device: no remote copies, remote signals or barrier semaphores. Data moves between devices by JAX's collectives and lax.ppermute only.
A program may use at most 192 MiB of HBM per device.

```python
import math
import jax
import jax.numpy as jnp
import numpy as np
from jax import lax

TILE = 512
FB_DEV = 8
BLOCK = 128
PSF = 31
SUB = 4
ITERS = 2
TAPS = 32
HALO = 16
WIN = 160
CELLS = 16
CAP = 2
FRAMES_ROW = 128
FRAMES = 1024
NY = 4096
NX = 8192
N_TX = 16


def draw_exposures(key, part):
    position = jnp.arange(FRAMES, dtype=jnp.float32) / max(FRAMES - 1, 1)
    scales = 1.0 + 2.0 * position
    noise_field = jnp.clip(jax.random.normal(jax.random.fold_in(key, 17), (FRAMES, BLOCK, BLOCK), jnp.float32), -6.0, 6.0)
    return noise_field * scales[:, None, None]


def plant(values, own_key, smallest, high):
    spot = [jax.random.randint(jax.random.fold_in(own_key, axis), (), 0, length) for axis, length in enumerate(values.shape)]
    longest = values.shape.index(max(values.shape))
    next_to = spot[:longest] + [(spot[longest] + 1) % values.shape[longest]] + spot[longest + 1:]
    return values.at[tuple(spot)].set(smallest).at[tuple(next_to)].set(high)


def shard_levels(rng, shape, shards, least, top_value):
    level, own = 1.0, jax.random.fold_in(rng, 6)
    for dim, blocks in shards:
        steps = jnp.exp(jax.random.uniform(jax.random.fold_in(own, dim), (blocks,), jnp.float32, least / len(shards), top_value / len(shards)))
        level = level * jnp.repeat(steps, shape[dim] // blocks).reshape([-1 if axis == dim else 1 for axis in range(len(shape))])
    return level


def assign_block(key, own, number, rows, number_of, top, most, lean):
    order = jax.random.permutation(key, number_of)
    crowded, common = shares(number_of, rows * top, most, lean, True), shares(number_of, rows * top, most, lean, False)
    places = jnp.arange(number_of)

    def named(lengths, rotation):
        used = int((lengths > 0).sum())
        fixed = max(1, used // 4)
        moved = fixed + (places - fixed + rotation * (used - fixed)) % max(1, number_of - fixed)
        return jnp.zeros((number_of,), jnp.int32).at[order[jnp.where(places < fixed, places, moved)]].set(jnp.asarray(lengths, jnp.int32))

    lengths = jnp.where(number % 4 == 0, named(crowded, number // 4), named(common, number - number // 4 - 1))
    mixed = jax.random.permutation(jax.random.fold_in(own, 3), number_of)
    giver, receiver = mixed[0:number_of // 2 * 2:2], mixed[1:number_of // 2 * 2:2]
    slack = jnp.minimum(lengths[giver] - 1, most - lengths[receiver]) // 2
    slack = jnp.where((giver == order[0]) | (receiver == order[0]) | (lengths[receiver] == 0), 0, jnp.maximum(slack, 0))
    moved = jax.random.randint(jax.random.fold_in(own, 4), (number_of // 2,), 0, 1 << 20) % (slack + 1)
    lengths = lengths.at[giver].add(-moved).at[receiver].add(moved)
    members = jnp.searchsorted(jnp.cumsum(lengths), jnp.arange(rows * top), side="right").astype(jnp.int32)
    table = members.reshape(top, rows).T
    table = table[jax.random.permutation(jax.random.fold_in(own, 1), rows)]
    rotation = jax.random.randint(jax.random.fold_in(own, 2), (rows, 1), 0, top)
    return jnp.take_along_axis(table, (jnp.arange(top)[None, :] + rotation) % top, axis=1)


def shares(number_of, total, bound, skew, full):
    weights = [(1 << 20) // math.isqrt(rank ** skew) + 1 for rank in range(1, number_of + 1)]
    largest = bound if full else min(bound, max(-(-total // number_of), total * weights[0] // sum(weights)))
    least = 1 if total - largest >= number_of - 1 else 0
    counts, spare = [largest] + [least] * (number_of - 1), total - largest - least * (number_of - 1)
    while spare > 0:
        candidates = [i for i in range(1, number_of) if counts[i] < largest] or [i for i in range(1, number_of) if counts[i] < bound]
        mass, left = sum([weights[i] for i in candidates]), spare
        for i in candidates:
            extra = min(bound - counts[i], max(1, left * weights[i] // mass), spare)
            counts[i] = counts[i] + extra
            spare = spare - extra
    return np.array(counts)


def setup_inputs(seed: int = 0) -> dict:
    arg_keys = jax.random.split(jax.random.key(seed), 6)
    exposures = draw_exposures(jax.random.fold_in(arg_keys[5], 71), 0)
    point_spread = jnp.clip(jnp.exp(math.log(1.0) - 9.2103404 * jax.random.uniform(arg_keys[1], (FRAMES, PSF, PSF), jnp.float32) ** shard_levels(arg_keys[1], (FRAMES, PSF, PSF), ((0, 128),), -0.2, 0.2)), 0.0001, 1.0)
    warp_steps = plant(jax.random.randint(arg_keys[2], (FRAMES, 2), 0, SUB), jax.random.fold_in(arg_keys[2], 1), 0, SUB - 1).astype(jnp.int32)
    column_keys = jax.random.split(jax.random.fold_in(arg_keys[3], 1), FRAMES // FB_DEV)
    column_turns = jax.random.permutation(jax.random.fold_in(arg_keys[3], 3), FRAMES // FB_DEV)
    column = jax.vmap(lambda own, number: assign_block(jax.random.fold_in(arg_keys[3], 2), own, number, FB_DEV, N_TX, 1, CAP, 2))(column_keys, column_turns).reshape((FRAMES, 1))
    block_cell = plant(jax.random.randint(arg_keys[4], (FRAMES,), 0, CELLS), jax.random.fold_in(arg_keys[4], 1), 0, CELLS - 1).astype(jnp.int32)
    return dict(exposures=exposures, point_spread=point_spread, warp_steps=warp_steps, column=column, block_cell=block_cell)


damping = 0.05


def make_kernels(point_spread, warp_steps):
    tap_count = point_spread.shape[-1] + 1
    totals = jnp.sum(point_spread, axis=(1, 2), keepdims=True)
    padded = jnp.pad(point_spread / totals, ((0, 0), (0, 1), (0, 1)))
    row_frac = (warp_steps[:, 0].astype(jnp.float32) / SUB)[:, None, None]
    col_frac = (warp_steps[:, 1].astype(jnp.float32) / SUB)[:, None, None]
    shifted = jnp.pad(padded, ((0, 0), (0, 0), (1, 0)))[:, :, :tap_count]
    blended = (1.0 - col_frac) * padded + col_frac * shifted
    lowered = jnp.pad(blended, ((0, 0), (1, 0), (0, 0)))[:, :tap_count, :]
    kernel = (1.0 - row_frac) * blended + row_frac * lowered
    return lax.optimization_barrier(kernel.astype(jnp.bfloat16)).astype(jnp.float32)


def rounded(values):
    return lax.optimization_barrier(values.astype(jnp.bfloat16)).astype(jnp.float32)


def window_anchors(column, block_cell):
    frame_index = jnp.arange(FRAMES, dtype=jnp.int32)
    per_row = TILE // BLOCK
    top_rows = (frame_index // FRAMES_ROW) * TILE + (block_cell.astype(jnp.int32) // per_row) * BLOCK
    left_cols = column[:, 0].astype(jnp.int32) * TILE + (block_cell.astype(jnp.int32) % per_row) * BLOCK
    return top_rows.astype(jnp.int32), left_cols.astype(jnp.int32)


def tap_table():
    taps_index = jnp.arange(TAPS)[:, None, None]
    positions = jnp.arange(WIN)[:, None]
    columns = jnp.arange(BLOCK)[None, :]
    table = jnp.where(positions - columns == taps_index, 1.0, 0.0).astype(jnp.float32)
    return table.reshape(TAPS, WIN * BLOCK)


def frame_bands(kernel_one, table):
    return jnp.dot(kernel_one, table, precision=lax.Precision.HIGHEST).reshape(TAPS, WIN, BLOCK)


def grouped(arrays):
    return tuple(member.reshape((FRAMES // FB_DEV, FB_DEV) + member.shape[1:]) for member in arrays)


def forward_all(field, kernels, top_rows, left_cols, table):
    padded = jnp.pad(field, HALO)

    def one_frame(kernel_one, top_row, left_col):
        framed = lax.dynamic_slice(padded, (top_row, left_col), (WIN, WIN))
        bands = frame_bands(kernel_one, table)
        stacked = jnp.stack([framed[offset:offset + BLOCK] for offset in range(TAPS)])
        return jnp.einsum('ayp,apx->yx', stacked, bands, precision=lax.Precision.HIGHEST)

    def one_group(operands):
        return jax.vmap(one_frame)(operands[0], operands[1], operands[2])

    result = lax.map(one_group, grouped((kernels, top_rows, left_cols)))
    return result.reshape(FRAMES, BLOCK, BLOCK)


def adjoint_all(images, kernels, top_rows, left_cols, table):
    def one_frame(frame_image, kernel_one):
        bands = frame_bands(kernel_one, table)
        spread = jnp.einsum('yx,apx->ayp', frame_image, bands, precision=lax.Precision.HIGHEST)
        summed = jnp.zeros((WIN, WIN), spread.dtype)
        for offset in range(TAPS):
            summed = summed + jnp.pad(spread[offset], ((offset, WIN - BLOCK - offset), (0, 0)))
        return summed

    def one_group(operands):
        return jax.vmap(one_frame)(operands[0], operands[1])

    patches = lax.map(one_group, grouped((images, kernels))).reshape(FRAMES, WIN, WIN)
    initial = jnp.zeros((NY + 2 * HALO, NX + 2 * HALO), patches.dtype)

    def place(slot_number, accumulated):
        current = lax.dynamic_slice(accumulated, (top_rows[slot_number], left_cols[slot_number]), (WIN, WIN))
        return lax.dynamic_update_slice(accumulated, current + patches[slot_number], (top_rows[slot_number], left_cols[slot_number]))

    accumulated = lax.fori_loop(0, FRAMES, place, initial)
    return accumulated[HALO:HALO + NY, HALO:HALO + NX]


def reference(exposures, point_spread, warp_steps, column, block_cell):
    kernels = make_kernels(point_spread, warp_steps)
    table = tap_table()
    top_rows, left_cols = window_anchors(column, block_cell)
    right_side = adjoint_all(rounded(exposures), kernels, top_rows, left_cols, table)
    solution = jnp.zeros_like(right_side)
    residual = right_side
    direction = right_side
    norm_now = jnp.sum(residual * residual)
    for iteration in range(ITERS):
        modelled = forward_all(rounded(direction), kernels, top_rows, left_cols, table)
        applied = adjoint_all(rounded(modelled), kernels, top_rows, left_cols, table) + damping * direction
        step_size = norm_now / jnp.sum(direction * applied)
        solution = solution + step_size * direction
        residual = residual - step_size * applied
        if iteration + 1 < ITERS:
            norm_next = jnp.sum(residual * residual)
            direction = residual + (norm_next / norm_now) * direction
            norm_now = norm_next
    return solution, residual
```

```python
import functools

import jax
import jax.numpy as jnp
from jax import lax
from jax.experimental import pallas as pl
from jax.experimental.pallas import tpu as pltpu
from jax.sharding import Mesh
from jax.sharding import PartitionSpec as P

TX = ("tx_0", "tx_1")
TY = ("ty_0", "ty_1")
TY_TX = TY + TX
N_TY, N_TX = 8, 16

SUB = 4
DAMPING = 0.05
FB = 8
CAP = 2
SLOTS = N_TX * CAP
TILE, BLOCK, HALO, TAPS, PSF = 512, 128, 16, 32, 31
EXT = TILE + 2 * HALO
LANES = 640
RIM = 2 * HALO
WIN = BLOCK + 2 * HALO
SLOT_ROWS = 160
F32, BF16 = jnp.float32, jnp.bfloat16
VMEM_BYTES = 48 << 20


def iota(shape, axis):
    return lax.broadcasted_iota(jnp.int32, shape, axis)


def by_group(lane, parts):
    low = jnp.where(lane < 32, parts[0], parts[1])
    high = jnp.where(lane < 96, parts[2], parts[3])
    return jnp.where(lane < 64, low, high)


def pack_kernel(column, cell, warp, spread_ref, exposures_ref, out_ref, pad, kern):
    pad[...] = jnp.zeros_like(pad)
    for f in range(FB):
        pad[f, 0:PSF, 0:PSF] = spread_ref[f]
    for f in range(FB):
        point = pad[f]
        point = point / jnp.sum(point, keepdims=True)
        row_frac = warp[f, 0].astype(F32) / SUB
        col_frac = warp[f, 1].astype(F32) / SUB
        blended = (1.0 - col_frac) * point + col_frac * pltpu.roll(point, 1, 1)
        lowered = pltpu.roll(blended, 1, 0)
        kern[32 * f : 32 * f + 32, :] = (
            (1.0 - row_frac) * blended + row_frac * lowered
        ).astype(BF16)
    row, lane = iota((128, 128), 0), iota((128, 128), 1)
    tall, wide = iota((32 * FB, 128), 0), iota((32 * FB, 128), 1)
    tap = tall & 31
    place = jnp.where((lane & 31) == 31 - row, 1.0, 0.0).astype(BF16)
    spread = jnp.dot(kern[...], place, preferred_element_type=F32)
    spread = jnp.where((wide >> 5) == ((tap >> 2) & 3), spread, 0.0).astype(BF16)
    target, source = iota((8 * FB, 32 * FB), 0), iota((8 * FB, 32 * FB), 1)
    s_tap = source & 31
    pick = ((source >> 5) == (target >> 3)) & (
        (target & 7) == 2 * (s_tap & 3) + (s_tap >> 4)
    )
    backward = jnp.dot(
        jnp.where(pick, 1.0, 0.0).astype(BF16), spread, preferred_element_type=F32
    )
    place = jnp.where((lane & 63) == row, 1.0, 0.0).astype(BF16)
    spread = jnp.dot(kern[...], place, preferred_element_type=F32)
    spread = jnp.where((wide >> 6) == (tap & 1), spread, 0.0).astype(BF16)
    target, source = iota((16 * FB, 32 * FB), 0), iota((16 * FB, 32 * FB), 1)
    pick = ((source >> 5) == (target >> 4)) & ((target & 15) == ((source & 31) >> 1))
    ahead = jnp.dot(
        jnp.where(pick, 1.0, 0.0).astype(BF16), spread, preferred_element_type=F32
    )
    for s in range(SLOTS):
        out_ref[s, 128:SLOT_ROWS, :] = jnp.zeros((SLOT_ROWS - 128, 128), BF16)
    for f in range(FB):
        standing = jnp.int32(0)
        for g in range(f):
            standing = standing + jnp.where(column[g] == column[f], 1, 0)
        slot = CAP * column[f] + jnp.minimum(standing, CAP - 1)
        out_ref[slot, 0:BLOCK, :] = exposures_ref[f].astype(BF16)
        tail = jnp.concatenate(
            [
                backward[8 * f : 8 * f + 8],
                ahead[16 * f : 16 * f + 16],
                jnp.broadcast_to((cell[f] + 1).astype(F32), (8, 128)),
            ],
            axis=0,
        )
        out_ref[slot, 128:SLOT_ROWS, :] = tail.astype(BF16)


def pack(column, cell, warp, spread, exposures):
    smem = pl.BlockSpec(memory_space=pltpu.SMEM)
    vmem = pl.BlockSpec(memory_space=pltpu.VMEM)
    return pl.pallas_call(
        pack_kernel,
        out_shape=jax.ShapeDtypeStruct((SLOTS, SLOT_ROWS, 128), BF16),
        in_specs=[smem, smem, smem, vmem, vmem],
        out_specs=vmem,
        scratch_shapes=[pltpu.VMEM((FB, 32, 128), F32), pltpu.VMEM((32 * FB, 128), BF16)],
        compiler_params=pltpu.CompilerParams(vmem_limit_bytes=VMEM_BYTES),
        name="pack",
    )(column, cell, warp, spread, exposures)


def list_frames(cells, frames):
    count = jnp.int32(0)
    for s in range(SLOTS):
        frames[count] = s
        count = count + jnp.where(cells[s] > 0, 1, 0)
    return count


def build_taps(taps, taps_out):
    row, lane = iota((64, 128), 0), iota((64, 128), 1)
    offset = (lane & 31) + 31 - row
    inside = (offset >= 0) & (offset < 32)
    for a2 in range(4):
        for h in range(2):
            line = jnp.broadcast_to(taps[2 * a2 + h : 2 * a2 + h + 1], (64, 128))
            line = pltpu.roll(line, 97, 1, stride=1, stride_axis=0)
            taps_out[0, 64 * a2 : 64 * a2 + 64, 128 * h : 128 * h + 128] = jnp.where(
                inside, line, 0.0
            ).astype(BF16)
    for a1 in range(8):
        for half in range(2):
            at = 8 + 2 * a1 + half
            line = jnp.broadcast_to(taps[at : at + 1], (32, 128))
            line = pltpu.roll(line, 0, 1, stride=1, stride_axis=0)
            taps_out[1, 32 * a1 : 32 * a1 + 32, 128 * half : 128 * half + 128] = line.astype(
                BF16
            )


def unfold(field, doubled, stack):
    rows = 32

    def columns(at, carry):
        left = pl.ds(pl.multiple_of(128 * at, 128), 128)
        right = pl.ds(pl.multiple_of(128 * at + 128, 128), 128)
        for r in range(0, EXT + 8, 24):
            lane = iota((24, 128), 1)
            here, there = field[r : r + 24, left], field[r : r + 24, right]
            turned = pltpu.roll(here, 64, 1)
            odd = pltpu.roll(here, 96, 1)
            odd_turned = pltpu.roll(odd, 64, 1)
            last = jnp.where(lane < 96, odd, pltpu.roll(there, 96, 1))
            last_turned = pltpu.roll(last, 64, 1)
            doubled[0, r : r + 24] = jnp.where(lane < 64, here, turned)
            doubled[1, r : r + 24] = jnp.where(lane < 64, odd, odd_turned)
            doubled[2, r : r + 24] = jnp.where(lane < 64, turned, here)
            doubled[3, r : r + 24] = jnp.where(lane < 64, last_turned, last)
        lane = iota((rows, 128), 1)
        for k in range(4):
            for r in range(0, EXT, rows):
                part = [doubled[k, r + a : r + a + rows] for a in range(4)]
                stack[4 * at + k, r : r + rows, 0:128] = jnp.where(
                    lane < 64, part[0], part[1]
                ).astype(BF16)
                stack[4 * at + k, r : r + rows, 128:256] = jnp.where(
                    lane < 64, part[2], part[3]
                ).astype(BF16)
        return carry

    lax.fori_loop(0, TILE // 128, columns, 0)


def fold(total, field):
    rows = 32
    lane = iota((rows, 128), 1)

    def block(b, r):
        even = total[b, r + 8 : r + 8 + rows, 0:128] + total[b, r + 6 : r + 6 + rows, 128:256]
        odd = total[b, r + 7 : r + 7 + rows, 0:128] + total[b, r + 5 : r + 5 + rows, 128:256]
        return jnp.where(lane < 64, even, odd)

    def columns(at, carry):
        here = pl.ds(pl.multiple_of(128 * at, 128), 128)
        for r in range(0, EXT, rows):
            before = block(4 * at, r)
            b0, b1, b2, b3 = [block(4 * at + 1 + k, r) for k in range(4)]
            even = jnp.where(lane < 64, b0, b2) + pltpu.roll(jnp.where(lane < 64, b2, b0), 64, 1)
            direct = jnp.where(lane < 64, b1, jnp.where(lane < 96, b3, before))
            turned = jnp.where(lane < 64, jnp.where(lane < 32, b3, before), b1)
            odd = direct + pltpu.roll(turned, 64, 1)
            field[r : r + rows, here] = even + pltpu.roll(odd, 32, 1)
        return carry

    lax.fori_loop(0, TILE // 128, columns, 0)
    for r in range(0, EXT, rows):
        before = block(TILE // 32, r)
        before = pltpu.roll(before + pltpu.roll(before, 64, 1), 32, 1)
        field[r : r + rows, TILE:LANES] = jnp.where(lane < RIM, before, 0.0)


def clear_total(total):
    def clear(b, carry):
        total[b] = jnp.zeros(total.shape[1:], F32)
        return carry

    lax.fori_loop(0, total.shape[0], clear, 0)


def expand_and_add(image_chunks, turned, spread, taps, total, lx, top):
    for c in range(4):
        for d in range(4):
            moved = image_chunks[c] if d == 0 else pltpu.roll(image_chunks[c], 32 * d, 1)
            turned[d, 16 + 32 * c : 48 + 32 * c] = moved
    lane = iota((48, 128), 1)
    for xb in range(4):
        for q in range(0, 144, 48):
            parts = [turned[(j - xb) % 4, 16 - 4 * j + q : 64 - 4 * j + q] for j in range(4)]
            spread[xb, 16 + q : 64 + q] = by_group(lane, parts).astype(BF16)
    both = jnp.concatenate([spread[:, 16:176], spread[:, 0:160]], axis=2).reshape(640, 256)
    window = jnp.dot(both, taps, preferred_element_type=F32).reshape(4, WIN, 256)
    at = pl.ds(pl.multiple_of(8 + top, 8), WIN)
    total[pl.ds(1 + lx, 4), at, :] += window


def clear_margins(turned, spread):
    turned[:, 0:16] = jnp.zeros((4, 16, 128), F32)
    turned[:, 144:160] = jnp.zeros((4, 16, 128), F32)
    spread[:, 0:16] = jnp.zeros((4, 16, 128), BF16)
    spread[:, 160:176] = jnp.zeros((4, 16, 128), BF16)


def write_rims(field, left_ref, right_ref, top_ref, bottom_ref):
    left_ref[...] = jnp.zeros_like(left_ref)
    right_ref[...] = jnp.zeros_like(right_ref)
    for r in range(0, TILE, 128):
        left_ref[:, r : r + 128] = field[r : r + 128, 0:128].T[0:RIM]
        right_ref[:, r : r + 128] = field[r : r + 128, TILE : TILE + 128].T[0:RIM]
    left_ref[:, TILE:EXT] = field[TILE:EXT, 0:128].T[0:RIM]
    right_ref[:, TILE:EXT] = field[TILE:EXT, TILE : TILE + 128].T[0:RIM]
    top_ref[...] = field[0:RIM, :]
    bottom_ref[...] = field[TILE:EXT, :]


def complete(place, own, rims, field):
    from_left, from_right, from_above, from_below = rims
    field[0:EXT, :] = own[...]
    field[EXT:, :] = jnp.zeros((field.shape[0] - EXT, LANES), F32)
    for r in range(0, TILE, 128):
        field[r : r + 128, 0:RIM] += from_left[:, r : r + 128].T
        field[r : r + 128, TILE:EXT] += from_right[:, r : r + 128].T
    field[TILE:EXT, 0:RIM] += from_left[:, TILE:LANES].T[0:RIM]
    field[TILE:EXT, TILE:EXT] += from_right[:, TILE:LANES].T[0:RIM]
    field[0:RIM, :] += from_above[...]
    field[TILE:EXT, :] += from_below[...]

    @pl.when(place[0] == 0)
    def _():
        field[0:HALO, :] = jnp.zeros((HALO, LANES), F32)

    @pl.when(place[0] == N_TY - 1)
    def _():
        field[EXT - HALO : EXT, :] = jnp.zeros((HALO, LANES), F32)

    @pl.when(place[1] == 0)
    def _():
        field[0:EXT, 0:HALO] = jnp.zeros((EXT, HALO), F32)

    @pl.when(place[1] == N_TX - 1)
    def _():
        field[0:EXT, EXT - HALO : EXT] = jnp.zeros((EXT, HALO), F32)


def inner_sum(chunk_of):
    sums = jnp.zeros((1, 128), F32)
    lane = iota((32, LANES), 1)
    inside = (lane >= HALO) & (lane < HALO + TILE)
    for r in range(HALO, HALO + TILE, 32):
        chunk = jnp.where(inside, chunk_of(r, 32), 0.0)
        by_lane = jnp.sum(chunk, axis=0, keepdims=True)
        for x in range(0, LANES, 128):
            sums = sums + by_lane[:, x : x + 128]
    return sums


def first_kernel(
    cells, slots_ref, own_ref, left_ref, right_ref, top_ref, bottom_ref, taps_out,
    frames, taps, total, turned, spread, sems,
):
    count = list_frames(cells, frames)
    clear_total(total)
    clear_margins(turned, spread)

    def frame(i, carry):
        s = frames[i]
        cell = cells[s] - 1
        lx, top = 4 * (cell & 3), BLOCK * (cell >> 2)
        build_taps(slots_ref[s, 128:SLOT_ROWS].astype(F32), taps.at[i])
        pltpu.make_async_copy(taps.at[i], taps_out.at[i], sems.at[i]).start()
        chunks = [slots_ref[s, r : r + 32].astype(F32) for r in range(0, BLOCK, 32)]
        expand_and_add(chunks, turned, spread, taps[i, 1], total, lx, top)
        return carry

    lax.fori_loop(0, count, frame, 0)
    fold(total, own_ref)
    write_rims(own_ref, left_ref, right_ref, top_ref, bottom_ref)

    def wait(i, carry):
        pltpu.make_async_copy(taps.at[i], taps_out.at[i], sems.at[i]).wait()
        return carry

    lax.fori_loop(0, count, wait, 0)


def frame_pass(cells, frames, count, taps_in, field, scratch):
    taps, total, turned, spread, stack, doubled, product, paired, sems = scratch
    unfold(field, doubled, stack)
    clear_total(total)
    clear_margins(turned, spread)

    def frame(i, sums):
        cell = cells[frames[i]] - 1
        lx, top = 4 * (cell & 3), BLOCK * (cell >> 2)
        pltpu.make_async_copy(taps_in.at[i], taps.at[i], sems.at[i]).wait()
        window = stack[pl.ds(lx, 4), pl.ds(pl.multiple_of(top, 128), WIN), :]
        product[...] = jnp.dot(
            window.reshape(4 * WIN, 256), taps[i, 0], preferred_element_type=F32
        ).reshape(4, WIN, 256)
        for xb in range(4):
            paired[xb] = product[xb, 0:144, 0:128] + product[xb, 16:160, 128:256]
        lane = iota((32, 128), 1)
        chunks = []
        for r in range(0, BLOCK, 32):
            modelled = None
            for d in range(4):
                parts = [paired[(j + d) % 4, r + 4 * j : r + 4 * j + 32] for j in range(4)]
                moved = by_group(lane, parts)
                moved = moved if d == 0 else pltpu.roll(moved, 32 * d, 1)
                modelled = moved if d == 0 else modelled + moved
            low = modelled.astype(BF16).astype(F32)
            sums = sums + jnp.sum(modelled * low, axis=0, keepdims=True)
            chunks.append(low)
        expand_and_add(chunks, turned, spread, taps[i, 1], total, lx, top)
        return sums

    return lax.fori_loop(0, count, frame, jnp.zeros((1, 128), F32))


def start_taps(cells, frames, taps_in, taps, sems):
    count = list_frames(cells, frames)

    def start(i, carry):
        pltpu.make_async_copy(taps_in.at[i], taps.at[i], sems.at[i]).start()
        return carry

    lax.fori_loop(0, count, start, 0)
    return count


def second_kernel(
    cells, place, own_in, rim_l, rim_r, rim_a, rim_b, taps_in,
    own_ref, left_ref, right_ref, top_ref, bottom_ref, residual_ref, sums_ref,
    frames, field, *scratch,
):
    count = start_taps(cells, frames, taps_in, scratch[0], scratch[-1])
    complete(place, own_in, (rim_l, rim_r, rim_a, rim_b), field)
    residual_ref[...] = field[0:EXT, :]
    square = inner_sum(lambda r, n: field[r : r + n, :] * field[r : r + n, :])
    curve = frame_pass(cells, frames, count, taps_in, field, scratch)
    fold(scratch[1], own_ref)
    write_rims(own_ref, left_ref, right_ref, top_ref, bottom_ref)
    sums_ref[...] = jnp.zeros_like(sums_ref)
    sums_ref[0:1] = square
    sums_ref[1:2] = curve


def first_step(sums):
    square = jnp.sum(sums[0:1], axis=1, keepdims=True)
    curve = jnp.sum(sums[1:2], axis=1, keepdims=True) + DAMPING * square
    return square, curve, square / curve


def third_kernel(
    cells, place, sums_in, own_in, rim_l, rim_r, rim_a, rim_b, start_ref, taps_in,
    own_ref, left_ref, right_ref, top_ref, bottom_ref, residual_ref, applied_ref, sums_ref,
    frames, field, *scratch,
):
    count = start_taps(cells, frames, taps_in, scratch[0], scratch[-1])
    complete(place, own_in, (rim_l, rim_r, rim_a, rim_b), field)
    step = first_step(sums_in[...])[2]
    for r in range(0, EXT, 32):
        start = start_ref[r : r + 32]
        applied = field[r : r + 32, :] + DAMPING * start
        residual = start - step * applied
        applied_ref[r : r + 32] = applied
        residual_ref[r : r + 32] = residual
        field[r : r + 32, :] = residual
    square = inner_sum(lambda r, n: field[r : r + n, :] * field[r : r + n, :])
    cross = inner_sum(lambda r, n: field[r : r + n, :] * applied_ref[r : r + n, :])
    curve = frame_pass(cells, frames, count, taps_in, field, scratch)
    fold(scratch[1], own_ref)
    write_rims(own_ref, left_ref, right_ref, top_ref, bottom_ref)
    sums_ref[...] = jnp.zeros_like(sums_ref)
    sums_ref[0:1] = square
    sums_ref[1:2] = cross
    sums_ref[2:3] = curve


def last_kernel(
    place, sums_one, sums_two, own_in, rim_l, rim_r, rim_a, rim_b, start_ref, applied_ref,
    residual_ref, solution_out, residual_out, field,
):
    complete(place, own_in, (rim_l, rim_r, rim_a, rim_b), field)
    square_one, curve_one, step_one = first_step(sums_one[...])
    sums = sums_two[...]
    square_two = jnp.sum(sums[0:1], axis=1, keepdims=True)
    cross = jnp.sum(sums[1:2], axis=1, keepdims=True)
    curve = jnp.sum(sums[2:3], axis=1, keepdims=True) + DAMPING * square_two
    ratio = square_two / square_one
    curve_two = curve + 2.0 * ratio * cross + ratio * ratio * curve_one
    step_two = square_two / curve_two
    lane = iota((32, 128), 1)
    for r in range(0, TILE, 32):
        rows = slice(r + HALO, r + HALO + 32)
        start, residual = start_ref[rows], residual_ref[rows]
        applied = field[rows, :] + DAMPING * residual + ratio * applied_ref[rows]
        total = step_one * start + step_two * (residual + ratio * start)
        left = residual - step_two * applied
        for value, out in ((total, solution_out), (left, residual_out)):
            parts = [
                pltpu.roll(value[:, x : x + 128], 128 - HALO, 1) for x in range(0, LANES, 128)
            ]
            for x in range(TILE // 128):
                out[r : r + 32, 128 * x : 128 * x + 128] = jnp.where(
                    lane < 128 - HALO, parts[x], parts[x + 1]
                )


def corner_kernel(top_ref, bottom_ref, from_left, from_right, top_out, bottom_out):
    top_out[...] = top_ref[...]
    bottom_out[...] = bottom_ref[...]
    for rim, at in ((from_left, 0), (from_right, TILE)):
        top_out[:, at : at + RIM] += rim[:, 0:128].T[0:RIM]
        bottom_out[:, at : at + RIM] += rim[:, TILE:LANES].T[0:RIM]


def call(kernel, outs, spaces, operands, scratch, name, out_spaces=None):
    specs = {
        "s": pl.BlockSpec(memory_space=pltpu.SMEM),
        "v": pl.BlockSpec(memory_space=pltpu.VMEM),
        "a": pl.BlockSpec(memory_space=pl.ANY),
    }
    return pl.pallas_call(
        kernel,
        out_shape=[jax.ShapeDtypeStruct(shape, kind) for shape, kind in outs],
        in_specs=[specs[space] for space in spaces],
        out_specs=[specs[space] for space in (out_spaces or "v" * len(outs))],
        scratch_shapes=scratch,
        compiler_params=pltpu.CompilerParams(vmem_limit_bytes=VMEM_BYTES),
        name=name,
    )(*operands)


FIELD = ((EXT, LANES), F32)
RIM_ARRAY = ((RIM, LANES), F32)
SUMS = ((8, 128), F32)
FRAME_LIST = pltpu.SMEM((SLOTS + 1,), jnp.int32)
TAPS_SCRATCH = pltpu.VMEM((SLOTS, 2, 256, 256), BF16)
TOTAL = pltpu.VMEM((TILE // 32 + 1, 8 + EXT, 256), F32)
TURNED = pltpu.VMEM((4, WIN, 128), F32)
SPREAD = pltpu.VMEM((4, WIN + 16, 128), BF16)
FIELD_SCRATCH = pltpu.VMEM((EXT + 8, LANES), F32)
PASS_SCRATCH = [
    FRAME_LIST,
    FIELD_SCRATCH,
    TAPS_SCRATCH,
    TOTAL,
    TURNED,
    SPREAD,
    pltpu.VMEM((TILE // 32, EXT, 256), BF16),
    pltpu.VMEM((4, EXT + 8, 128), F32),
    pltpu.VMEM((4, WIN, 256), F32),
    pltpu.VMEM((4, 144, 128), F32),
    pltpu.SemaphoreType.DMA((SLOTS,)),
]


def shift(value, axes, size, step):
    pairs = [(i, i + step) for i in range(size) if 0 <= i + step < size]
    return lax.ppermute(value, axes, pairs)


def trade_rims(left, right, top, bottom):
    from_left = shift(right, TX, N_TX, 1)
    from_right = shift(left, TX, N_TX, -1)
    top, bottom = call(
        corner_kernel,
        [RIM_ARRAY, RIM_ARRAY],
        "vvvv",
        (top, bottom, from_left, from_right),
        [],
        "corners",
    )
    from_above = shift(bottom, TY, N_TY, 1)
    from_below = shift(top, TY, N_TY, -1)
    return from_left, from_right, from_above, from_below


def total_sum(value):
    value = value + lax.ppermute(value, "ty_1", [(0, 1), (1, 0)])
    for axis in ("tx_1", "tx_0", "ty_0"):
        value = value + lax.ppermute(value, axis, [(0, 1), (1, 0), (2, 3), (3, 2)])
        value = value + lax.ppermute(value, axis, [(1, 2), (2, 1), (3, 0), (0, 3)])
    return value


def body(exposures, point_spread, warp_steps, column, block_cell):
    place = jnp.stack([lax.axis_index(TY), lax.axis_index(TX)]).astype(jnp.int32)
    sent = pack(column[:, 0], block_cell, warp_steps, point_spread, exposures)
    slots = lax.all_to_all(
        sent.reshape(N_TX, CAP, SLOT_ROWS, 128), TX, split_axis=0, concat_axis=0, tiled=True
    ).reshape(SLOTS, SLOT_ROWS, 128)
    cells = slots[:, SLOT_ROWS - 8, 0].astype(jnp.int32)
    rims_out = [RIM_ARRAY] * 4

    own, left, right, top, bottom, taps = call(
        first_kernel,
        [FIELD] + rims_out + [((SLOTS, 2, 256, 256), BF16)],
        "sv",
        (cells, slots),
        [FRAME_LIST, TAPS_SCRATCH, TOTAL, TURNED, SPREAD, pltpu.SemaphoreType.DMA((SLOTS,))],
        "right_side",
        "vvvvva",
    )
    rims = trade_rims(left, right, top, bottom)
    own, left, right, top, bottom, start, sums_one = call(
        second_kernel,
        [FIELD] + rims_out + [FIELD, SUMS],
        "ssvvvvva",
        (cells, place, own, *rims, taps),
        PASS_SCRATCH,
        "first_pass",
    )
    rims = trade_rims(left, right, top, bottom)
    sums_one = total_sum(sums_one)
    own, left, right, top, bottom, residual, applied, sums_two = call(
        third_kernel,
        [FIELD] + rims_out + [FIELD, FIELD, SUMS],
        "ssvvvvvvva",
        (cells, place, sums_one, own, *rims, start, taps),
        PASS_SCRATCH,
        "second_pass",
    )
    rims = trade_rims(left, right, top, bottom)
    sums_two = total_sum(sums_two)
    tile = ((TILE, TILE), F32)
    return tuple(
        call(
            last_kernel,
            [tile, tile],
            "svvvvvvvvvv",
            (place, sums_one, sums_two, own, *rims, start, applied, residual),
            [FIELD_SCRATCH],
            "finish",
        )
    )


def solution(mesh):
    torus = Mesh(mesh.devices.reshape(4, 2, 4, 4), TY_TX)
    in_specs = (
        P(TY_TX, None, None),
        P(TY_TX, None, None),
        P(TY_TX, None),
        P(TY_TX, None),
        P(TY_TX),
    )
    out_specs = (P(TY, TX), P(TY, TX))
    return jax.shard_map(body, mesh=torus, in_specs=in_specs, out_specs=out_specs, check_vma=False)
```

```python
import jax
import jax.numpy as jnp
from jax import lax
from jax.experimental import pallas as pl
from jax.experimental.pallas import tpu as pltpu
from jax.sharding import Mesh
from jax.sharding import PartitionSpec as P

TX = ("tx_0", "tx_1")
TY = ("ty_0", "ty_1")
TY_TX = TY + TX
N_TY, N_TX = 8, 16

SUB = 4
DAMPING = 0.05
FB = 8
CAP = 2
SLOTS = N_TX * CAP
TILE, BLOCK, HALO, TAPS, PSF = 512, 128, 16, 32, 31
EXT = TILE + 2 * HALO
LANES = 640
RIM = 2 * HALO
WIN = BLOCK + 2 * HALO
SLOT_ROWS = 160
GROUP = 4
F32, BF16 = jnp.float32, jnp.bfloat16
VMEM_BYTES = 48 << 20


def iota(shape, axis):
    return lax.broadcasted_iota(jnp.int32, shape, axis)


def by_group(lane, parts):
    low = jnp.where(lane < 32, parts[0], parts[1])
    high = jnp.where(lane < 96, parts[2], parts[3])
    return jnp.where(lane < 64, low, high)


def pack_kernel(column, cell, warp, spread_ref, exposures_ref, out_ref, pad, kern):
    pad[...] = jnp.zeros_like(pad)
    for f in range(FB):
        pad[f, 0:PSF, 0:PSF] = spread_ref[f]
    for f in range(FB):
        point = pad[f]
        point = point / jnp.sum(point, keepdims=True)
        row_frac = warp[f, 0].astype(F32) / SUB
        col_frac = warp[f, 1].astype(F32) / SUB
        blended = (1.0 - col_frac) * point + col_frac * pltpu.roll(point, 1, 1)
        lowered = pltpu.roll(blended, 1, 0)
        kern[32 * f : 32 * f + 32, :] = (
            (1.0 - row_frac) * blended + row_frac * lowered
        ).astype(BF16)
    row, lane = iota((128, 128), 0), iota((128, 128), 1)
    tall, wide = iota((32 * FB, 128), 0), iota((32 * FB, 128), 1)
    tap = tall & 31
    place = jnp.where((lane & 31) == 31 - row, 1.0, 0.0).astype(BF16)
    spread = jnp.dot(kern[...], place, preferred_element_type=F32)
    spread = jnp.where((wide >> 5) == ((tap >> 2) & 3), spread, 0.0).astype(BF16)
    target, source = iota((8 * FB, 32 * FB), 0), iota((8 * FB, 32 * FB), 1)
    s_tap = source & 31
    pick = ((source >> 5) == (target >> 3)) & (
        (target & 7) == 2 * (s_tap & 3) + (s_tap >> 4)
    )
    backward = jnp.dot(
        jnp.where(pick, 1.0, 0.0).astype(BF16), spread, preferred_element_type=F32
    )
    place = jnp.where((lane & 63) == row, 1.0, 0.0).astype(BF16)
    spread = jnp.dot(kern[...], place, preferred_element_type=F32)
    spread = jnp.where((wide >> 6) == (tap & 1), spread, 0.0).astype(BF16)
    target, source = iota((16 * FB, 32 * FB), 0), iota((16 * FB, 32 * FB), 1)
    pick = ((source >> 5) == (target >> 4)) & ((target & 15) == ((source & 31) >> 1))
    ahead = jnp.dot(
        jnp.where(pick, 1.0, 0.0).astype(BF16), spread, preferred_element_type=F32
    )
    for s in range(SLOTS):
        out_ref[s, 128:SLOT_ROWS, :] = jnp.zeros((SLOT_ROWS - 128, 128), BF16)
    for f in range(FB):
        standing = jnp.int32(0)
        for g in range(f):
            standing = standing + jnp.where(column[g] == column[f], 1, 0)
        slot = CAP * column[f] + jnp.minimum(standing, CAP - 1)
        out_ref[slot, 0:BLOCK, :] = exposures_ref[f].astype(BF16)
        tail = jnp.concatenate(
            [
                backward[8 * f : 8 * f + 8],
                ahead[16 * f : 16 * f + 16],
                jnp.broadcast_to((cell[f] + 1).astype(F32), (8, 128)),
            ],
            axis=0,
        )
        out_ref[slot, 128:SLOT_ROWS, :] = tail.astype(BF16)


def pack(column, cell, warp, spread, exposures):
    smem = pl.BlockSpec(memory_space=pltpu.SMEM)
    vmem = pl.BlockSpec(memory_space=pltpu.VMEM)
    return pl.pallas_call(
        pack_kernel,
        out_shape=jax.ShapeDtypeStruct((SLOTS, SLOT_ROWS, 128), BF16),
        in_specs=[smem, smem, smem, vmem, vmem],
        out_specs=vmem,
        scratch_shapes=[pltpu.VMEM((FB, 32, 128), F32), pltpu.VMEM((32 * FB, 128), BF16)],
        compiler_params=pltpu.CompilerParams(vmem_limit_bytes=VMEM_BYTES),
        name="pack",
    )(column, cell, warp, spread, exposures)


def list_frames(cells, frames):
    count = jnp.int32(0)
    for s in range(SLOTS):
        frames[count] = s
        count = count + jnp.where(cells[s] > 0, 1, 0)
    return count


def build_taps(taps, taps_out):
    row, lane = iota((64, 128), 0), iota((64, 128), 1)
    offset = (lane & 31) + 31 - row
    inside = (offset >= 0) & (offset < 32)
    for a2 in range(4):
        for h in range(2):
            line = jnp.broadcast_to(taps[2 * a2 + h : 2 * a2 + h + 1], (64, 128))
            line = pltpu.roll(line, 97, 1, stride=1, stride_axis=0)
            taps_out[0, 64 * a2 : 64 * a2 + 64, 128 * h : 128 * h + 128] = jnp.where(
                inside, line, 0.0
            ).astype(BF16)
    for a1 in range(8):
        for half in range(2):
            at = 8 + 2 * a1 + half
            line = jnp.broadcast_to(taps[at : at + 1], (32, 128))
            line = pltpu.roll(line, 0, 1, stride=1, stride_axis=0)
            taps_out[1, 32 * a1 : 32 * a1 + 32, 128 * half : 128 * half + 128] = line.astype(
                BF16
            )


def unfold(field, copies, doubled, stack):
    rows = 32
    source, target = iota((256, 512), 0), iota((256, 512), 1)
    copies[...] = jnp.where(source == 32 * (target >> 7) + (target & 63), 1.0, 0.0).astype(BF16)

    def columns(at, carry):
        both = pl.ds(pl.multiple_of(128 * at, 128), 256)
        wide = jnp.dot(field[:, both].astype(BF16), copies[...], preferred_element_type=F32)
        for k in range(4):
            doubled[k] = wide[:, 128 * k : 128 * k + 128]
        lane = iota((rows, 128), 1)
        for k in range(4):
            for r in range(0, EXT, rows):
                part = [doubled[k, r + a : r + a + rows] for a in range(4)]
                stack[4 * at + k, r : r + rows, 0:128] = jnp.where(
                    lane < 64, part[0], part[1]
                ).astype(BF16)
                stack[4 * at + k, r : r + rows, 128:256] = jnp.where(
                    lane < 64, part[2], part[3]
                ).astype(BF16)
        return carry

    lax.fori_loop(0, TILE // 128, columns, 0)


def fold(total, field):
    rows = 32
    lane = iota((rows, 128), 1)

    def block(b, r):
        even = total[b, r + 8 : r + 8 + rows, 0:128] + total[b, r + 6 : r + 6 + rows, 128:256]
        odd = total[b, r + 7 : r + 7 + rows, 0:128] + total[b, r + 5 : r + 5 + rows, 128:256]
        return jnp.where(lane < 64, even, odd)

    def columns(at, carry):
        here = pl.ds(pl.multiple_of(128 * at, 128), 128)
        for r in range(0, EXT, rows):
            before = block(4 * at, r)
            b0, b1, b2, b3 = [block(4 * at + 1 + k, r) for k in range(4)]
            even = jnp.where(lane < 64, b0, b2) + pltpu.roll(jnp.where(lane < 64, b2, b0), 64, 1)
            direct = jnp.where(lane < 64, b1, jnp.where(lane < 96, b3, before))
            turned = jnp.where(lane < 64, jnp.where(lane < 32, b3, before), b1)
            odd = pltpu.roll(direct, 32, 1) + pltpu.roll(turned, 96, 1)
            field[r : r + rows, here] = even + odd
        return carry

    lax.fori_loop(0, TILE // 128, columns, 0)
    for r in range(0, EXT, rows):
        before = block(TILE // 32, r)
        before = pltpu.roll(before, 32, 1) + pltpu.roll(before, 96, 1)
        field[r : r + rows, TILE:LANES] = jnp.where(lane < RIM, before, 0.0)


def clear_total(total):
    def clear(b, carry):
        total[b] = jnp.zeros(total.shape[1:], F32)
        return carry

    lax.fori_loop(0, total.shape[0], clear, 0)


def expand(image, turned, spread):
    for d in range(4):
        turned[d, 16:144] = image if d == 0 else pltpu.roll(image, 32 * d, 1)
    lane = iota((144, 128), 1)
    for xb in range(4):
        parts = [turned[(j - xb) % 4, 16 - 4 * j : 160 - 4 * j] for j in range(4)]
        spread[xb, 16:160] = by_group(lane, parts).astype(BF16)


def add_window(spread, taps, total, lx, top):
    both = jnp.concatenate([spread[:, 16:176], spread[:, 0:160]], axis=2).reshape(640, 256)
    window = jnp.dot(both, taps, preferred_element_type=F32).reshape(4, WIN, 256)
    at = pl.ds(pl.multiple_of(8 + top, 8), WIN)
    total[pl.ds(1 + lx, 4), at, :] += window


def clear_margins(turned, spread):
    for g in range(GROUP):
        turned[g, :, 0:16] = jnp.zeros((4, 16, 128), F32)
        turned[g, :, 144:160] = jnp.zeros((4, 16, 128), F32)
        spread[g, :, 0:16] = jnp.zeros((4, 16, 128), BF16)
        spread[g, :, 160:176] = jnp.zeros((4, 16, 128), BF16)


def over_frames(count, step, carry):
    groups = count // GROUP

    def group(k, carry):
        return step([GROUP * k + g for g in range(GROUP)], carry)

    carry = lax.fori_loop(0, groups, group, carry)
    return lax.fori_loop(GROUP * groups, count, lambda i, carry: step([i], carry), carry)


def place_of(cells, frames, i):
    cell = cells[frames[i]] - 1
    return 4 * (cell & 3), BLOCK * (cell >> 2)


def write_rims(field, left_ref, right_ref, top_ref, bottom_ref):
    left_ref[...] = jnp.zeros_like(left_ref)
    right_ref[...] = jnp.zeros_like(right_ref)
    for r in range(0, TILE, 128):
        left_ref[:, r : r + 128] = field[r : r + 128, 0:128].T[0:RIM]
        right_ref[:, r : r + 128] = field[r : r + 128, TILE : TILE + 128].T[0:RIM]
    left_ref[:, TILE:EXT] = field[TILE:EXT, 0:128].T[0:RIM]
    right_ref[:, TILE:EXT] = field[TILE:EXT, TILE : TILE + 128].T[0:RIM]
    top_ref[...] = field[0:RIM, :]
    bottom_ref[...] = field[TILE:EXT, :]


def complete(place, own, rims, field):
    from_left, from_right, from_above, from_below = rims
    field[0:EXT, :] = own[...]
    field[EXT:, :] = jnp.zeros((field.shape[0] - EXT, LANES), F32)
    for r in range(0, TILE, 128):
        field[r : r + 128, 0:RIM] += from_left[:, r : r + 128].T
        field[r : r + 128, TILE:EXT] += from_right[:, r : r + 128].T
    field[TILE:EXT, 0:RIM] += from_left[:, TILE:LANES].T[0:RIM]
    field[TILE:EXT, TILE:EXT] += from_right[:, TILE:LANES].T[0:RIM]
    field[0:RIM, :] += from_above[...]
    field[TILE:EXT, :] += from_below[...]

    @pl.when(place[0] == 0)
    def _():
        field[0:HALO, :] = jnp.zeros((HALO, LANES), F32)

    @pl.when(place[0] == N_TY - 1)
    def _():
        field[EXT - HALO : EXT, :] = jnp.zeros((HALO, LANES), F32)

    @pl.when(place[1] == 0)
    def _():
        field[0:EXT, 0:HALO] = jnp.zeros((EXT, HALO), F32)

    @pl.when(place[1] == N_TX - 1)
    def _():
        field[0:EXT, EXT - HALO : EXT] = jnp.zeros((EXT, HALO), F32)


def inner_sum(chunk_of):
    sums = jnp.zeros((1, 128), F32)
    lane = iota((32, LANES), 1)
    inside = (lane >= HALO) & (lane < HALO + TILE)
    for r in range(HALO, HALO + TILE, 32):
        chunk = jnp.where(inside, chunk_of(r, 32), 0.0)
        by_lane = jnp.sum(chunk, axis=0, keepdims=True)
        for x in range(0, LANES, 128):
            sums = sums + by_lane[:, x : x + 128]
    return sums


def first_kernel(
    cells, slots_ref, own_ref, left_ref, right_ref, top_ref, bottom_ref, taps_out,
    frames, taps, total, turned, spread, sems,
):
    count = list_frames(cells, frames)
    clear_total(total)
    clear_margins(turned, spread)

    def step(group, carry):
        for i in group:
            build_taps(slots_ref[frames[i], 128:SLOT_ROWS].astype(F32), taps.at[i])
            pltpu.make_async_copy(taps.at[i], taps_out.at[i], sems.at[i]).start()
        for g, i in enumerate(group):
            image = slots_ref[frames[i], 0:BLOCK].astype(F32)
            expand(image, turned.at[g], spread.at[g])
        for g, i in enumerate(group):
            add_window(spread.at[g], taps[i, 1], total, *place_of(cells, frames, i))
        return carry

    over_frames(count, step, 0)
    fold(total, own_ref)
    write_rims(own_ref, left_ref, right_ref, top_ref, bottom_ref)

    def wait(i, carry):
        pltpu.make_async_copy(taps.at[i], taps_out.at[i], sems.at[i]).wait()
        return carry

    lax.fori_loop(0, count, wait, 0)


def frame_pass(cells, frames, count, taps_in, field, scratch):
    taps, total, turned, spread, stack, copies, doubled, product, paired, sems = scratch
    unfold(field, copies, doubled, stack)
    clear_total(total)
    clear_margins(turned, spread)

    def step(group, sums):
        for i in group:
            pltpu.make_async_copy(taps_in.at[i], taps.at[i], sems.at[i]).wait()
        for g, i in enumerate(group):
            lx, top = place_of(cells, frames, i)
            window = stack[pl.ds(lx, 4), pl.ds(pl.multiple_of(top, 128), WIN), :]
            product[g] = jnp.dot(
                window.reshape(4 * WIN, 256), taps[i, 0], preferred_element_type=F32
            ).reshape(4, WIN, 256)
        images = []
        for g in range(len(group)):
            for xb in range(4):
                paired[g, xb] = product[g, xb, 0:144, 0:128] + product[g, xb, 16:160, 128:256]
            lane = iota((BLOCK, 128), 1)
            modelled = None
            for d in range(4):
                parts = [paired[g, (j + d) % 4, 4 * j : 4 * j + BLOCK] for j in range(4)]
                moved = by_group(lane, parts)
                moved = moved if d == 0 else pltpu.roll(moved, 32 * d, 1)
                modelled = moved if d == 0 else modelled + moved
            image = modelled.astype(BF16).astype(F32)
            sums = sums + jnp.sum(modelled * image, axis=0, keepdims=True)
            images.append(image)
        for g, image in enumerate(images):
            expand(image, turned.at[g], spread.at[g])
        for g, i in enumerate(group):
            add_window(spread.at[g], taps[i, 1], total, *place_of(cells, frames, i))
        return sums

    return over_frames(count, step, jnp.zeros((1, 128), F32))


def start_taps(cells, frames, taps_in, taps, sems):
    count = list_frames(cells, frames)

    def start(i, carry):
        pltpu.make_async_copy(taps_in.at[i], taps.at[i], sems.at[i]).start()
        return carry

    lax.fori_loop(0, count, start, 0)
    return count


def second_kernel(
    cells, place, own_in, rim_l, rim_r, rim_a, rim_b, taps_in,
    own_ref, left_ref, right_ref, top_ref, bottom_ref, residual_ref, sums_ref,
    frames, field, *scratch,
):
    count = start_taps(cells, frames, taps_in, scratch[0], scratch[-1])
    complete(place, own_in, (rim_l, rim_r, rim_a, rim_b), field)
    residual_ref[...] = field[0:EXT, :]
    square = inner_sum(lambda r, n: field[r : r + n, :] * field[r : r + n, :])
    curve = frame_pass(cells, frames, count, taps_in, field, scratch)
    fold(scratch[1], own_ref)
    write_rims(own_ref, left_ref, right_ref, top_ref, bottom_ref)
    sums_ref[...] = jnp.zeros_like(sums_ref)
    sums_ref[0:1] = square
    sums_ref[1:2] = curve


def first_step(sums):
    square = jnp.sum(sums[0:1], axis=1, keepdims=True)
    curve = jnp.sum(sums[1:2], axis=1, keepdims=True) + DAMPING * square
    return square, curve, square / curve


def third_kernel(
    cells, place, sums_in, own_in, rim_l, rim_r, rim_a, rim_b, start_ref, taps_in,
    own_ref, left_ref, right_ref, top_ref, bottom_ref, residual_ref, applied_ref, sums_ref,
    frames, field, *scratch,
):
    count = start_taps(cells, frames, taps_in, scratch[0], scratch[-1])
    complete(place, own_in, (rim_l, rim_r, rim_a, rim_b), field)
    step = first_step(sums_in[...])[2]
    for r in range(0, EXT, 32):
        start = start_ref[r : r + 32]
        applied = field[r : r + 32, :] + DAMPING * start
        residual = start - step * applied
        applied_ref[r : r + 32] = applied
        residual_ref[r : r + 32] = residual
        field[r : r + 32, :] = residual
    square = inner_sum(lambda r, n: field[r : r + n, :] * field[r : r + n, :])
    cross = inner_sum(lambda r, n: field[r : r + n, :] * applied_ref[r : r + n, :])
    curve = frame_pass(cells, frames, count, taps_in, field, scratch)
    fold(scratch[1], own_ref)
    write_rims(own_ref, left_ref, right_ref, top_ref, bottom_ref)
    sums_ref[...] = jnp.zeros_like(sums_ref)
    sums_ref[0:1] = square
    sums_ref[1:2] = cross
    sums_ref[2:3] = curve


def last_kernel(
    place, sums_one, sums_two, own_in, rim_l, rim_r, rim_a, rim_b, start_ref, applied_ref,
    residual_ref, solution_out, residual_out, field,
):
    complete(place, own_in, (rim_l, rim_r, rim_a, rim_b), field)
    square_one, curve_one, step_one = first_step(sums_one[...])
    sums = sums_two[...]
    square_two = jnp.sum(sums[0:1], axis=1, keepdims=True)
    cross = jnp.sum(sums[1:2], axis=1, keepdims=True)
    curve = jnp.sum(sums[2:3], axis=1, keepdims=True) + DAMPING * square_two
    ratio = square_two / square_one
    curve_two = curve + 2.0 * ratio * cross + ratio * ratio * curve_one
    step_two = square_two / curve_two
    lane = iota((32, 128), 1)
    for r in range(0, TILE, 32):
        rows = slice(r + HALO, r + HALO + 32)
        start, residual = start_ref[rows], residual_ref[rows]
        applied = field[rows, :] + DAMPING * residual + ratio * applied_ref[rows]
        total = step_one * start + step_two * (residual + ratio * start)
        left = residual - step_two * applied
        for value, out in ((total, solution_out), (left, residual_out)):
            parts = [
                pltpu.roll(value[:, x : x + 128], 128 - HALO, 1) for x in range(0, LANES, 128)
            ]
            for x in range(TILE // 128):
                out[r : r + 32, 128 * x : 128 * x + 128] = jnp.where(
                    lane < 128 - HALO, parts[x], parts[x + 1]
                )


def corner_kernel(top_ref, bottom_ref, from_left, from_right, top_out, bottom_out):
    top_out[...] = top_ref[...]
    bottom_out[...] = bottom_ref[...]
    for rim, at in ((from_left, 0), (from_right, TILE)):
        top_out[:, at : at + RIM] += rim[:, 0:128].T[0:RIM]
        bottom_out[:, at : at + RIM] += rim[:, TILE:LANES].T[0:RIM]


def call(kernel, outs, spaces, operands, scratch, name, out_spaces=None):
    specs = {
        "s": pl.BlockSpec(memory_space=pltpu.SMEM),
        "v": pl.BlockSpec(memory_space=pltpu.VMEM),
        "a": pl.BlockSpec(memory_space=pl.ANY),
    }
    return pl.pallas_call(
        kernel,
        out_shape=[jax.ShapeDtypeStruct(shape, kind) for shape, kind in outs],
        in_specs=[specs[space] for space in spaces],
        out_specs=[specs[space] for space in (out_spaces or "v" * len(outs))],
        scratch_shapes=scratch,
        compiler_params=pltpu.CompilerParams(vmem_limit_bytes=VMEM_BYTES),
        name=name,
    )(*operands)


FIELD = ((EXT, LANES), F32)
RIM_ARRAY = ((RIM, LANES), F32)
SUMS = ((8, 128), F32)
FRAME_LIST = pltpu.SMEM((SLOTS + 1,), jnp.int32)
TAPS_SCRATCH = pltpu.VMEM((SLOTS, 2, 256, 256), BF16)
TOTAL = pltpu.VMEM((TILE // 32 + 1, 8 + EXT, 256), F32)
TURNED = pltpu.VMEM((GROUP, 4, WIN, 128), F32)
SPREAD = pltpu.VMEM((GROUP, 4, WIN + 16, 128), BF16)
FIELD_SCRATCH = pltpu.VMEM((EXT + 8, LANES), F32)
PASS_SCRATCH = [
    FRAME_LIST,
    FIELD_SCRATCH,
    TAPS_SCRATCH,
    TOTAL,
    TURNED,
    SPREAD,
    pltpu.VMEM((TILE // 32, EXT, 256), BF16),
    pltpu.VMEM((256, 512), BF16),
    pltpu.VMEM((4, EXT + 8, 128), F32),
    pltpu.VMEM((GROUP, 4, WIN, 256), F32),
    pltpu.VMEM((GROUP, 4, 144, 128), F32),
    pltpu.SemaphoreType.DMA((SLOTS,)),
]


def shift(value, axes, size, step):
    pairs = [(i, i + step) for i in range(size) if 0 <= i + step < size]
    return lax.ppermute(value, axes, pairs)


def trade_rims(left, right, top, bottom):
    from_left = shift(right, TX, N_TX, 1)
    from_right = shift(left, TX, N_TX, -1)
    top, bottom = call(
        corner_kernel,
        [RIM_ARRAY, RIM_ARRAY],
        "vvvv",
        (top, bottom, from_left, from_right),
        [],
        "corners",
    )
    from_above = shift(bottom, TY, N_TY, 1)
    from_below = shift(top, TY, N_TY, -1)
    return from_left, from_right, from_above, from_below


def total_sum(value):
    value = value + lax.ppermute(value, "ty_1", [(0, 1), (1, 0)])
    for axis in ("tx_1", "tx_0", "ty_0"):
        value = value + lax.ppermute(value, axis, [(0, 1), (1, 0), (2, 3), (3, 2)])
        value = value + lax.ppermute(value, axis, [(1, 2), (2, 1), (3, 0), (0, 3)])
    return value


def body(exposures, point_spread, warp_steps, column, block_cell):
    place = jnp.stack([lax.axis_index(TY), lax.axis_index(TX)]).astype(jnp.int32)
    sent = pack(column[:, 0], block_cell, warp_steps, point_spread, exposures)
    slots = lax.all_to_all(
        sent.reshape(N_TX, CAP, SLOT_ROWS, 128), TX, split_axis=0, concat_axis=0, tiled=True
    ).reshape(SLOTS, SLOT_ROWS, 128)
    cells = slots[:, SLOT_ROWS - 8, 0].astype(jnp.int32)
    rims_out = [RIM_ARRAY] * 4

    own, left, right, top, bottom, taps = call(
        first_kernel,
        [FIELD] + rims_out + [((SLOTS, 2, 256, 256), BF16)],
        "sv",
        (cells, slots),
        [FRAME_LIST, TAPS_SCRATCH, TOTAL, TURNED, SPREAD, pltpu.SemaphoreType.DMA((SLOTS,))],
        "right_side",
        "vvvvva",
    )
    rims = trade_rims(left, right, top, bottom)
    own, left, right, top, bottom, start, sums_one = call(
        second_kernel,
        [FIELD] + rims_out + [FIELD, SUMS],
        "ssvvvvva",
        (cells, place, own, *rims, taps),
        PASS_SCRATCH,
        "first_pass",
    )
    rims = trade_rims(left, right, top, bottom)
    sums_one = total_sum(sums_one)
    own, left, right, top, bottom, residual, applied, sums_two = call(
        third_kernel,
        [FIELD] + rims_out + [FIELD, FIELD, SUMS],
        "ssvvvvvvva",
        (cells, place, sums_one, own, *rims, start, taps),
        PASS_SCRATCH,
        "second_pass",
    )
    rims = trade_rims(left, right, top, bottom)
    sums_two = total_sum(sums_two)
    tile = ((TILE, TILE), F32)
    return tuple(
        call(
            last_kernel,
            [tile, tile],
            "svvvvvvvvvv",
            (place, sums_one, sums_two, own, *rims, start, applied, residual),
            [FIELD_SCRATCH],
            "finish",
        )
    )


def solution(mesh):
    torus = Mesh(mesh.devices.reshape(4, 2, 4, 4), TY_TX)
    in_specs = (
        P(TY_TX, None, None),
        P(TY_TX, None, None),
        P(TY_TX, None),
        P(TY_TX, None),
        P(TY_TX),
    )
    out_specs = (P(TY, TX), P(TY, TX))
    return jax.shard_map(body, mesh=torus, in_specs=in_specs, out_specs=out_specs, check_vma=False)
```

```python
import jax
import jax.numpy as jnp
from jax import lax
from jax.experimental import pallas as pl
from jax.experimental.pallas import tpu as pltpu
from jax.sharding import Mesh
from jax.sharding import PartitionSpec as P

TX = ("tx_0", "tx_1")
TY = ("ty_0", "ty_1")
TY_TX = TY + TX
N_TY, N_TX = 8, 16

SUB = 4
DAMPING = 0.05
FB = 8
CAP = 2
SLOTS = N_TX * CAP
TILE, BLOCK, HALO, TAPS, PSF = 512, 128, 16, 32, 31
EXT = TILE + 2 * HALO
LANES = 640
RIM = 2 * HALO
WIN = BLOCK + 2 * HALO
SLOT_ROWS = 160
GROUP = 4
F32, BF16 = jnp.float32, jnp.bfloat16
VMEM_BYTES = 38 << 20


def iota(shape, axis):
    return lax.broadcasted_iota(jnp.int32, shape, axis)


def by_group(lane, parts):
    low = jnp.where(lane < 32, parts[0], parts[1])
    high = jnp.where(lane < 96, parts[2], parts[3])
    return jnp.where(lane < 64, low, high)


def pack_kernel(labels, spread_ref, exposures_ref, out_ref, pad, kern):
    pad[...] = jnp.zeros_like(pad)
    for f in range(FB):
        pad[f, 0:PSF, 0:PSF] = spread_ref[:, f, :]
    for f in range(FB):
        point = pad[f]
        point = point / jnp.sum(point, keepdims=True)
        row_frac = labels[0, f].astype(F32) / SUB
        col_frac = labels[1, f].astype(F32) / SUB
        blended = (1.0 - col_frac) * point + col_frac * pltpu.roll(point, 1, 1)
        lowered = pltpu.roll(blended, 1, 0)
        kern[32 * f : 32 * f + 32, :] = (
            (1.0 - row_frac) * blended + row_frac * lowered
        ).astype(BF16)
    row, lane = iota((128, 128), 0), iota((128, 128), 1)
    tall, wide = iota((32 * FB, 128), 0), iota((32 * FB, 128), 1)
    tap = tall & 31
    place = jnp.where((lane & 31) == 31 - row, 1.0, 0.0).astype(BF16)
    spread = jnp.dot(kern[...], place, preferred_element_type=F32)
    spread = jnp.where((wide >> 5) == ((tap >> 2) & 3), spread, 0.0).astype(BF16)
    target, source = iota((8 * FB, 32 * FB), 0), iota((8 * FB, 32 * FB), 1)
    s_tap = source & 31
    pick = ((source >> 5) == (target >> 3)) & (
        (target & 7) == 2 * (s_tap & 3) + (s_tap >> 4)
    )
    backward = jnp.dot(
        jnp.where(pick, 1.0, 0.0).astype(BF16), spread, preferred_element_type=F32
    )
    place = jnp.where((lane & 63) == row, 1.0, 0.0).astype(BF16)
    spread = jnp.dot(kern[...], place, preferred_element_type=F32)
    spread = jnp.where((wide >> 6) == (tap & 1), spread, 0.0).astype(BF16)
    target, source = iota((16 * FB, 32 * FB), 0), iota((16 * FB, 32 * FB), 1)
    pick = ((source >> 5) == (target >> 4)) & ((target & 15) == ((source & 31) >> 1))
    ahead = jnp.dot(
        jnp.where(pick, 1.0, 0.0).astype(BF16), spread, preferred_element_type=F32
    )
    for s in range(SLOTS):
        out_ref[s, 128:SLOT_ROWS, :] = jnp.zeros((SLOT_ROWS - 128, 128), BF16)
    for f in range(FB):
        standing = jnp.int32(0)
        for g in range(f):
            standing = standing + jnp.where(labels[2, g] == labels[2, f], 1, 0)
        slot = CAP * labels[2, f] + jnp.minimum(standing, CAP - 1)
        out_ref[slot, 0:BLOCK, :] = exposures_ref[f].astype(BF16)
        tail = jnp.concatenate(
            [
                backward[8 * f : 8 * f + 8],
                ahead[16 * f : 16 * f + 16],
                jnp.broadcast_to((labels[3, f] + 1).astype(F32), (8, 128)),
            ],
            axis=0,
        )
        out_ref[slot, 128:SLOT_ROWS, :] = tail.astype(BF16)


def pack(labels, spread, exposures):
    smem = pl.BlockSpec(memory_space=pltpu.SMEM)
    vmem = pl.BlockSpec(memory_space=pltpu.VMEM)
    return pl.pallas_call(
        pack_kernel,
        out_shape=jax.ShapeDtypeStruct((SLOTS, SLOT_ROWS, 128), BF16),
        in_specs=[smem, vmem, vmem],
        out_specs=vmem,
        scratch_shapes=[pltpu.VMEM((FB, 32, 128), F32), pltpu.VMEM((32 * FB, 128), BF16)],
        compiler_params=pltpu.CompilerParams(vmem_limit_bytes=VMEM_BYTES),
        name="pack",
    )(labels, spread, exposures)


def list_frames(cells, frames):
    count = jnp.int32(0)
    for s in range(SLOTS):
        frames[count] = s
        count = count + jnp.where(cells[s] > 0, 1, 0)
    return count


def build_taps(taps, taps_out):
    row, lane = iota((64, 128), 0), iota((64, 128), 1)
    offset = (lane & 31) + 31 - row
    inside = (offset >= 0) & (offset < 32)
    for a2 in range(4):
        for h in range(2):
            line = jnp.broadcast_to(taps[2 * a2 + h : 2 * a2 + h + 1], (64, 128))
            line = pltpu.roll(line, 97, 1, stride=1, stride_axis=0)
            taps_out[0, 64 * a2 : 64 * a2 + 64, 128 * h : 128 * h + 128] = jnp.where(
                inside, line, 0.0
            ).astype(BF16)
    for a1 in range(8):
        for half in range(2):
            at = 8 + 2 * a1 + half
            line = jnp.broadcast_to(taps[at : at + 1], (32, 128))
            line = pltpu.roll(line, 0, 1, stride=1, stride_axis=0)
            taps_out[1, 32 * a1 : 32 * a1 + 32, 128 * half : 128 * half + 128] = line.astype(
                BF16
            )


def unfold(field, copies, doubled, stack):
    rows = 32
    source, target = iota((256, 512), 0), iota((256, 512), 1)
    copies[...] = jnp.where(source == 32 * (target >> 7) + (target & 63), 1.0, 0.0).astype(BF16)

    def columns(at, carry):
        both = pl.ds(pl.multiple_of(128 * at, 128), 256)
        wide = jnp.dot(field[:, both].astype(BF16), copies[...], preferred_element_type=F32)
        for k in range(4):
            doubled[k] = wide[:, 128 * k : 128 * k + 128]
        lane = iota((rows, 128), 1)
        for k in range(4):
            for r in range(0, EXT, rows):
                part = [doubled[k, r + a : r + a + rows] for a in range(4)]
                stack[4 * at + k, r : r + rows, 0:128] = jnp.where(
                    lane < 64, part[0], part[1]
                ).astype(BF16)
                stack[4 * at + k, r : r + rows, 128:256] = jnp.where(
                    lane < 64, part[2], part[3]
                ).astype(BF16)
        return carry

    lax.fori_loop(0, TILE // 128, columns, 0)


def fold(total, field):
    rows = 32
    lane = iota((rows, 128), 1)

    def block(b, r):
        even = total[b, r + 8 : r + 8 + rows, 0:128] + total[b, r + 6 : r + 6 + rows, 128:256]
        odd = total[b, r + 7 : r + 7 + rows, 0:128] + total[b, r + 5 : r + 5 + rows, 128:256]
        return jnp.where(lane < 64, even, odd)

    def columns(at, carry):
        here = pl.ds(pl.multiple_of(128 * at, 128), 128)
        for r in range(0, EXT, rows):
            before = block(4 * at, r)
            b0, b1, b2, b3 = [block(4 * at + 1 + k, r) for k in range(4)]
            even = jnp.where(lane < 64, b0, b2) + pltpu.roll(jnp.where(lane < 64, b2, b0), 64, 1)
            direct = jnp.where(lane < 64, b1, jnp.where(lane < 96, b3, before))
            turned = jnp.where(lane < 64, jnp.where(lane < 32, b3, before), b1)
            odd = pltpu.roll(direct, 32, 1) + pltpu.roll(turned, 96, 1)
            field[r : r + rows, here] = even + odd
        return carry

    lax.fori_loop(0, TILE // 128, columns, 0)
    for r in range(0, EXT, rows):
        before = block(TILE // 32, r)
        before = pltpu.roll(before, 32, 1) + pltpu.roll(before, 96, 1)
        field[r : r + rows, TILE:LANES] = jnp.where(lane < RIM, before, 0.0)


def clear_total(total):
    def clear(b, carry):
        total[b] = jnp.zeros(total.shape[1:], F32)
        return carry

    lax.fori_loop(0, total.shape[0], clear, 0)


def expand(image, turned, spread):
    for d in range(4):
        turned[d, 16:144] = image if d == 0 else pltpu.roll(image, 32 * d, 1)
    lane = iota((144, 128), 1)
    for xb in range(4):
        parts = [turned[(j - xb) % 4, 16 - 4 * j : 160 - 4 * j] for j in range(4)]
        spread[xb, 16:160] = by_group(lane, parts).astype(BF16)


def add_window(spread, taps, total, lx, top):
    both = jnp.concatenate([spread[:, 16:176], spread[:, 0:160]], axis=2).reshape(640, 256)
    window = jnp.dot(both, taps, preferred_element_type=F32).reshape(4, WIN, 256)
    at = pl.ds(pl.multiple_of(8 + top, 8), WIN)
    total[pl.ds(1 + lx, 4), at, :] += window


def clear_margins(turned, spread):
    for g in range(GROUP):
        turned[g, :, 0:16] = jnp.zeros((4, 16, 128), F32)
        turned[g, :, 144:160] = jnp.zeros((4, 16, 128), F32)
        spread[g, :, 0:16] = jnp.zeros((4, 16, 128), BF16)
        spread[g, :, 160:176] = jnp.zeros((4, 16, 128), BF16)


def over_frames(count, step, carry):
    groups = count // GROUP

    def group(k, carry):
        return step([GROUP * k + g for g in range(GROUP)], carry)

    carry = lax.fori_loop(0, groups, group, carry)
    return lax.fori_loop(GROUP * groups, count, lambda i, carry: step([i], carry), carry)


def place_of(cells, frames, i):
    cell = cells[frames[i]] - 1
    return 4 * (cell & 3), BLOCK * (cell >> 2)


def write_rims(place, field, first_ref, second_ref, top_ref, bottom_ref):
    first_ref[...] = jnp.zeros_like(first_ref)
    second_ref[...] = jnp.zeros_like(second_ref)
    even = (place[1] & 1) == 0
    for r in range(0, EXT, 128):
        n = min(128, EXT - r)
        left = field[r : r + n, 0:128].T[0:RIM]
        right = field[r : r + n, TILE : TILE + 128].T[0:RIM]
        first_ref[:, r : r + n] = jnp.where(even, right, left)
        second_ref[:, r : r + n] = jnp.where(even, left, right)
    top_ref[...] = field[0:RIM, :]
    bottom_ref[...] = field[TILE:EXT, :]


def neighbours(index, size, first, second):
    even = (index & 1) == 0
    before = jnp.where(even, second, first)
    after = jnp.where(even, first, second)
    before = jnp.where(index > 0, before, 0.0)
    after = jnp.where(index < size - 1, after, 0.0)
    return before, after


def complete(place, own, rims, field):
    field[0:EXT, :] = own[...]
    field[EXT:, :] = jnp.zeros((field.shape[0] - EXT, LANES), F32)
    for r in range(0, EXT, 128):
        n = min(128, EXT - r)
        lanes = slice(r, r + 128)
        left, right = neighbours(place[1], N_TX, rims[0][:, lanes], rims[1][:, lanes])
        field[r : r + n, 0:RIM] += left.T[0:n]
        field[r : r + n, TILE:EXT] += right.T[0:n]
    above, below = neighbours(place[0], N_TY, rims[2][...], rims[3][...])
    field[0:RIM, :] += above
    field[TILE:EXT, :] += below

    @pl.when(place[0] == 0)
    def _():
        field[0:HALO, :] = jnp.zeros((HALO, LANES), F32)

    @pl.when(place[0] == N_TY - 1)
    def _():
        field[EXT - HALO : EXT, :] = jnp.zeros((HALO, LANES), F32)

    @pl.when(place[1] == 0)
    def _():
        field[0:EXT, 0:HALO] = jnp.zeros((EXT, HALO), F32)

    @pl.when(place[1] == N_TX - 1)
    def _():
        field[0:EXT, EXT - HALO : EXT] = jnp.zeros((EXT, HALO), F32)


def inner_sum(chunk_of):
    sums = jnp.zeros((1, 128), F32)
    lane = iota((32, LANES), 1)
    inside = (lane >= HALO) & (lane < HALO + TILE)
    for r in range(HALO, HALO + TILE, 32):
        chunk = jnp.where(inside, chunk_of(r, 32), 0.0)
        by_lane = jnp.sum(chunk, axis=0, keepdims=True)
        for x in range(0, LANES, 128):
            sums = sums + by_lane[:, x : x + 128]
    return sums


def first_kernel(
    cells, place, slots_ref, own_ref, left_ref, right_ref, top_ref, bottom_ref, taps_out,
    frames, taps, total, turned, spread, sems,
):
    count = list_frames(cells, frames)
    clear_total(total)
    clear_margins(turned, spread)

    def step(group, carry):
        for i in group:
            build_taps(slots_ref[frames[i], 128:SLOT_ROWS].astype(F32), taps.at[i])
            pltpu.make_async_copy(taps.at[i], taps_out.at[i], sems.at[i]).start()
        for g, i in enumerate(group):
            image = slots_ref[frames[i], 0:BLOCK].astype(F32)
            expand(image, turned.at[g], spread.at[g])
        for g, i in enumerate(group):
            add_window(spread.at[g], taps[i, 1], total, *place_of(cells, frames, i))
        return carry

    over_frames(count, step, 0)
    fold(total, own_ref)
    write_rims(place, own_ref, left_ref, right_ref, top_ref, bottom_ref)

    def wait(i, carry):
        pltpu.make_async_copy(taps.at[i], taps_out.at[i], sems.at[i]).wait()
        return carry

    lax.fori_loop(0, count, wait, 0)


def frame_pass(cells, frames, count, taps_in, field, scratch):
    taps, total, turned, spread, stack, copies, doubled, product, paired, sems = scratch
    unfold(field, copies, doubled, stack)
    clear_total(total)
    clear_margins(turned, spread)

    def step(group, sums):
        for i in group:
            pltpu.make_async_copy(taps_in.at[i], taps.at[i], sems.at[i]).wait()
        for g, i in enumerate(group):
            lx, top = place_of(cells, frames, i)
            window = stack[pl.ds(lx, 4), pl.ds(pl.multiple_of(top, 128), WIN), :]
            product[g] = jnp.dot(
                window.reshape(4 * WIN, 256), taps[i, 0], preferred_element_type=F32
            ).reshape(4, WIN, 256)
        images = []
        for g in range(len(group)):
            for xb in range(4):
                paired[g, xb] = product[g, xb, 0:144, 0:128] + product[g, xb, 16:160, 128:256]
            lane = iota((BLOCK, 128), 1)
            modelled = None
            for d in range(4):
                parts = [paired[g, (j + d) % 4, 4 * j : 4 * j + BLOCK] for j in range(4)]
                moved = by_group(lane, parts)
                moved = moved if d == 0 else pltpu.roll(moved, 32 * d, 1)
                modelled = moved if d == 0 else modelled + moved
            image = modelled.astype(BF16).astype(F32)
            sums = sums + jnp.sum(modelled * image, axis=0, keepdims=True)
            images.append(image)
        for g, image in enumerate(images):
            expand(image, turned.at[g], spread.at[g])
        for g, i in enumerate(group):
            add_window(spread.at[g], taps[i, 1], total, *place_of(cells, frames, i))
        return sums

    return over_frames(count, step, jnp.zeros((1, 128), F32))


def start_taps(cells, frames, taps_in, taps, sems):
    count = list_frames(cells, frames)

    def start(i, carry):
        pltpu.make_async_copy(taps_in.at[i], taps.at[i], sems.at[i]).start()
        return carry

    lax.fori_loop(0, count, start, 0)
    return count


def second_kernel(
    cells, place, own_in, rim_l, rim_r, rim_a, rim_b, taps_in,
    own_ref, left_ref, right_ref, top_ref, bottom_ref, residual_ref, sums_ref,
    frames, field, *scratch,
):
    count = start_taps(cells, frames, taps_in, scratch[0], scratch[-1])
    complete(place, own_in, (rim_l, rim_r, rim_a, rim_b), field)
    residual_ref[...] = field[0:EXT, :]
    square = inner_sum(lambda r, n: field[r : r + n, :] * field[r : r + n, :])
    curve = frame_pass(cells, frames, count, taps_in, field, scratch)
    fold(scratch[1], own_ref)
    write_rims(place, own_ref, left_ref, right_ref, top_ref, bottom_ref)
    sums_ref[...] = jnp.zeros_like(sums_ref)
    sums_ref[0:1] = square
    sums_ref[1:2] = curve


def first_step(sums):
    square = jnp.sum(sums[0:1], axis=1, keepdims=True)
    curve = jnp.sum(sums[1:2], axis=1, keepdims=True) + DAMPING * square
    return square, curve, square / curve


def third_kernel(
    cells, place, sums_in, own_in, rim_l, rim_r, rim_a, rim_b, start_ref, taps_in,
    own_ref, left_ref, right_ref, top_ref, bottom_ref, residual_ref, applied_ref, sums_ref,
    frames, field, *scratch,
):
    count = start_taps(cells, frames, taps_in, scratch[0], scratch[-1])
    complete(place, own_in, (rim_l, rim_r, rim_a, rim_b), field)
    step = first_step(sums_in[...])[2]
    for r in range(0, EXT, 32):
        start = start_ref[r : r + 32]
        applied = field[r : r + 32, :] + DAMPING * start
        residual = start - step * applied
        applied_ref[r : r + 32] = applied
        residual_ref[r : r + 32] = residual
        field[r : r + 32, :] = residual
    square = inner_sum(lambda r, n: field[r : r + n, :] * field[r : r + n, :])
    cross = inner_sum(lambda r, n: field[r : r + n, :] * applied_ref[r : r + n, :])
    curve = frame_pass(cells, frames, count, taps_in, field, scratch)
    fold(scratch[1], own_ref)
    write_rims(place, own_ref, left_ref, right_ref, top_ref, bottom_ref)
    sums_ref[...] = jnp.zeros_like(sums_ref)
    sums_ref[0:1] = square
    sums_ref[1:2] = cross
    sums_ref[2:3] = curve


def last_kernel(
    place, sums_one, sums_two, own_in, rim_l, rim_r, rim_a, rim_b, start_ref, applied_ref,
    residual_ref, solution_out, residual_out, field,
):
    complete(place, own_in, (rim_l, rim_r, rim_a, rim_b), field)
    square_one, curve_one, step_one = first_step(sums_one[...])
    sums = sums_two[...]
    square_two = jnp.sum(sums[0:1], axis=1, keepdims=True)
    cross = jnp.sum(sums[1:2], axis=1, keepdims=True)
    curve = jnp.sum(sums[2:3], axis=1, keepdims=True) + DAMPING * square_two
    ratio = square_two / square_one
    curve_two = curve + 2.0 * ratio * cross + ratio * ratio * curve_one
    step_two = square_two / curve_two
    lane = iota((32, 128), 1)
    for r in range(0, TILE, 32):
        rows = slice(r + HALO, r + HALO + 32)
        start, residual = start_ref[rows], residual_ref[rows]
        applied = field[rows, :] + DAMPING * residual + ratio * applied_ref[rows]
        total = step_one * start + step_two * (residual + ratio * start)
        left = residual - step_two * applied
        for value, out in ((total, solution_out), (left, residual_out)):
            parts = [
                pltpu.roll(value[:, x : x + 128], 128 - HALO, 1) for x in range(0, LANES, 128)
            ]
            for x in range(TILE // 128):
                out[r : r + 32, 128 * x : 128 * x + 128] = jnp.where(
                    lane < 128 - HALO, parts[x], parts[x + 1]
                )


def corner_kernel(place, top_ref, bottom_ref, first_in, second_in, *rest):
    first_out, second_out, top, bottom = rest[-4:]
    top[...] = top_ref[...]
    bottom[...] = bottom_ref[...]
    left, right = neighbours(place[1], N_TX, first_in[...], second_in[...])
    for rim, at in ((left, 0), (right, TILE)):
        top[:, at : at + RIM] += rim[:, 0:128].T[0:RIM]
        bottom[:, at : at + RIM] += rim[:, TILE:LANES].T[0:RIM]
    even = (place[0] & 1) == 0
    first_out[...] = jnp.where(even, bottom[...], top[...])
    second_out[...] = jnp.where(even, top[...], bottom[...])


def call(kernel, outs, spaces, operands, scratch, name, out_spaces=None):
    specs = {
        "s": pl.BlockSpec(memory_space=pltpu.SMEM),
        "v": pl.BlockSpec(memory_space=pltpu.VMEM),
        "a": pl.BlockSpec(memory_space=pl.ANY),
    }
    return pl.pallas_call(
        kernel,
        out_shape=[jax.ShapeDtypeStruct(shape, kind) for shape, kind in outs],
        in_specs=[specs[space] for space in spaces],
        out_specs=[specs[space] for space in (out_spaces or "v" * len(outs))],
        scratch_shapes=scratch,
        compiler_params=pltpu.CompilerParams(vmem_limit_bytes=VMEM_BYTES),
        name=name,
    )(*operands)


FIELD = ((EXT, LANES), F32)
RIM_ARRAY = ((RIM, LANES), F32)
SUMS = ((8, 128), F32)
FRAME_LIST = pltpu.SMEM((SLOTS + 1,), jnp.int32)
TAPS_SCRATCH = pltpu.VMEM((SLOTS, 2, 256, 256), BF16)
TOTAL = pltpu.VMEM((TILE // 32 + 1, 8 + EXT, 256), F32)
TURNED = pltpu.VMEM((GROUP, 4, WIN, 128), F32)
SPREAD = pltpu.VMEM((GROUP, 4, WIN + 16, 128), BF16)
FIELD_SCRATCH = pltpu.VMEM((EXT + 8, LANES), F32)
PASS_SCRATCH = [
    FRAME_LIST,
    FIELD_SCRATCH,
    TAPS_SCRATCH,
    TOTAL,
    TURNED,
    SPREAD,
    pltpu.VMEM((TILE // 32, EXT, 256), BF16),
    pltpu.VMEM((256, 512), BF16),
    pltpu.VMEM((4, EXT + 8, 128), F32),
    pltpu.VMEM((GROUP, 4, WIN, 256), F32),
    pltpu.VMEM((GROUP, 4, 144, 128), F32),
    pltpu.SemaphoreType.DMA((SLOTS,)),
]


def trade(first, second, axes, size):
    near = [(i, i ^ 1) for i in range(size)]
    far = [(i, ((i + 1) ^ 1) - 1) for i in range(1, size - 1)] + [(0, size - 1), (size - 1, 0)]
    return lax.ppermute(first, axes, near), lax.ppermute(second, axes, far)


def sum_pairs(value, axis):
    value = value + lax.ppermute(value, axis, [(0, 1), (1, 0), (2, 3), (3, 2)])
    return value + lax.ppermute(value, axis, [(1, 2), (2, 1), (3, 0), (0, 3)])


def trade_rims(place, left, right, top, bottom, sums=None):
    rims = trade(left, right, TX, N_TX)
    ahead = ()
    if sums is not None:
        sums = sum_pairs(sums, "tx_1")
        ahead = (sums,)
    rows = call(
        corner_kernel,
        [RIM_ARRAY, RIM_ARRAY],
        "svvvv" + "a" * len(ahead),
        (place, top, bottom, *rims, *ahead),
        [pltpu.VMEM((RIM, LANES), F32)] * 2,
        "corners",
    )
    rims = (*rims, *trade(*rows, TY, N_TY))
    if sums is not None:
        sums = sums + lax.ppermute(sums, "ty_1", [(0, 1), (1, 0)])
        sums = sum_pairs(sum_pairs(sums, "tx_0"), "ty_0")
    return rims, sums


def body(exposures, point_spread, warp_steps, column, block_cell):
    place = jnp.stack([lax.axis_index(TY), lax.axis_index(TX)]).astype(jnp.int32)
    labels = jnp.concatenate([warp_steps.T, column.T, block_cell[None]])
    sent = pack(labels, point_spread.transpose(1, 0, 2), exposures)
    slots = lax.all_to_all(
        sent.reshape(N_TX, CAP, SLOT_ROWS, 128), TX, split_axis=0, concat_axis=0, tiled=True
    ).reshape(SLOTS, SLOT_ROWS, 128)
    cells = slots[:, SLOT_ROWS - 8, 0].astype(jnp.int32)
    rims_out = [RIM_ARRAY] * 4

    own, left, right, top, bottom, taps = call(
        first_kernel,
        [FIELD] + rims_out + [((SLOTS, 2, 256, 256), BF16)],
        "ssv",
        (cells, place, slots),
        [FRAME_LIST, TAPS_SCRATCH, TOTAL, TURNED, SPREAD, pltpu.SemaphoreType.DMA((SLOTS,))],
        "right_side",
        "vvvvva",
    )
    rims, _ = trade_rims(place, left, right, top, bottom)
    own, left, right, top, bottom, start, sums_one = call(
        second_kernel,
        [FIELD] + rims_out + [FIELD, SUMS],
        "ssvvvvva",
        (cells, place, own, *rims, taps),
        PASS_SCRATCH,
        "first_pass",
    )
    rims, sums_one = trade_rims(place, left, right, top, bottom, sums_one)
    own, left, right, top, bottom, residual, applied, sums_two = call(
        third_kernel,
        [FIELD] + rims_out + [FIELD, FIELD, SUMS],
        "ssvvvvvvva",
        (cells, place, sums_one, own, *rims, start, taps),
        PASS_SCRATCH,
        "second_pass",
    )
    rims, sums_two = trade_rims(place, left, right, top, bottom, sums_two)
    tile = ((TILE, TILE), F32)
    return tuple(
        call(
            last_kernel,
            [tile, tile],
            "svvvvvvvvvv",
            (place, sums_one, sums_two, own, *rims, start, applied, residual),
            [FIELD_SCRATCH],
            "finish",
        )
    )


def solution(mesh):
    torus = Mesh(mesh.devices.reshape(4, 2, 4, 4), TY_TX)
    in_specs = (
        P(TY_TX, None, None),
        P(TY_TX, None, None),
        P(TY_TX, None),
        P(TY_TX, None),
        P(TY_TX),
    )
    out_specs = (P(TY, TX), P(TY, TX))
    return jax.shard_map(body, mesh=torus, in_specs=in_specs, out_specs=out_specs, check_vma=False)
```

```python
import jax
import jax.numpy as jnp
from jax import lax
from jax.experimental import pallas as pl
from jax.experimental.pallas import tpu as pltpu
from jax.sharding import Mesh
from jax.sharding import PartitionSpec as P

TX = ("tx_0", "tx_1")
TY = ("ty_0", "ty_1")
TY_TX = TY + TX
N_TY, N_TX = 8, 16

SUB = 4
DAMPING = 0.05
FB = 8
CAP = 2
SLOTS = N_TX * CAP
TILE, BLOCK, HALO, TAPS, PSF = 512, 128, 16, 32, 31
EXT = TILE + 2 * HALO
LANES = 640
RIM = 2 * HALO
WIN = BLOCK + 2 * HALO
SLOT_ROWS = 160
GROUP = 8
F32, BF16 = jnp.float32, jnp.bfloat16
VMEM_BYTES = 36 << 20


def iota(shape, axis):
    return lax.broadcasted_iota(jnp.int32, shape, axis)


def by_group(lane, parts):
    low = jnp.where(lane < 32, parts[0], parts[1])
    high = jnp.where(lane < 96, parts[2], parts[3])
    return jnp.where(lane < 64, low, high)


def pack_kernel(labels, spread_hbm, exposures_hbm, out_ref, points, images, pad, kern, sems):
    copies = [
        pltpu.make_async_copy(spread_hbm, points, sems.at[0]),
        pltpu.make_async_copy(exposures_hbm, images, sems.at[1]),
    ]
    for copy in copies:
        copy.start()
    for s in range(SLOTS):
        out_ref[s, 128:SLOT_ROWS, :] = jnp.zeros((SLOT_ROWS - 128, 128), BF16)
    pad[...] = jnp.zeros_like(pad)
    frame = iota((FB, 128), 0)
    row_frac, col_frac = jnp.zeros((FB, 128), F32), jnp.zeros((FB, 128), F32)
    for f in range(FB):
        row_frac = jnp.where(frame == f, labels[0, f].astype(F32) / SUB, row_frac)
        col_frac = jnp.where(frame == f, labels[1, f].astype(F32) / SUB, col_frac)
    copies[0].wait()
    pad[0:PSF, :, 0:PSF] = points[...]
    total = jnp.sum(jnp.sum(pad[...], axis=0), axis=1, keepdims=True)
    before = jnp.zeros((FB, 128), F32)
    for a in range(TAPS):
        point = pad[a] / total
        blended = (1.0 - col_frac) * point + col_frac * pltpu.roll(point, 1, 1)
        kern[FB * a : FB * a + FB, :] = (1.0 - row_frac) * blended + row_frac * before
        before = blended
    taps = kern[...].astype(BF16)
    row, lane = iota((128, 128), 0), iota((128, 128), 1)
    tall, wide = iota((32 * FB, 128), 0), iota((32 * FB, 128), 1)
    tap = tall >> 3
    place = jnp.where((lane & 31) == 31 - row, 1.0, 0.0).astype(BF16)
    spread = jnp.dot(taps, place, preferred_element_type=F32)
    spread = jnp.where((wide >> 5) == ((tap >> 2) & 3), spread, 0.0).astype(BF16)
    target, source = iota((8 * FB, 32 * FB), 0), iota((8 * FB, 32 * FB), 1)
    s_tap = source >> 3
    pick = ((source & 7) == (target >> 3)) & (
        (target & 7) == 2 * (s_tap & 3) + (s_tap >> 4)
    )
    backward = jnp.dot(
        jnp.where(pick, 1.0, 0.0).astype(BF16), spread, preferred_element_type=F32
    )
    place = jnp.where((lane & 63) == row, 1.0, 0.0).astype(BF16)
    spread = jnp.dot(taps, place, preferred_element_type=F32)
    spread = jnp.where((wide >> 6) == (tap & 1), spread, 0.0).astype(BF16)
    target, source = iota((16 * FB, 32 * FB), 0), iota((16 * FB, 32 * FB), 1)
    pick = ((source & 7) == (target >> 4)) & ((target & 15) == (source >> 4))
    ahead = jnp.dot(
        jnp.where(pick, 1.0, 0.0).astype(BF16), spread, preferred_element_type=F32
    )
    copies[1].wait()
    for f in range(FB):
        standing = jnp.int32(0)
        for g in range(f):
            standing = standing + jnp.where(labels[2, g] == labels[2, f], 1, 0)
        slot = CAP * labels[2, f] + jnp.minimum(standing, CAP - 1)
        out_ref[slot, 0:BLOCK, :] = images[f].astype(BF16)
        tail = jnp.concatenate(
            [
                backward[8 * f : 8 * f + 8],
                ahead[16 * f : 16 * f + 16],
                jnp.broadcast_to((labels[3, f] + 1).astype(F32), (8, 128)),
            ],
            axis=0,
        )
        out_ref[slot, 128:SLOT_ROWS, :] = tail.astype(BF16)


def list_frames(cells, frames):
    count = jnp.int32(0)
    for s in range(SLOTS):
        frames[count] = s
        count = count + jnp.where(cells[s] > 0, 1, 0)
    return count


def build_taps(taps, taps_out):
    row, lane = iota((64, 128), 0), iota((64, 128), 1)
    offset = (lane & 31) + 31 - row
    inside = (offset >= 0) & (offset < 32)
    for a2 in range(4):
        for h in range(2):
            line = jnp.broadcast_to(taps[2 * a2 + h : 2 * a2 + h + 1], (64, 128))
            line = pltpu.roll(line, 97, 1, stride=1, stride_axis=0)
            taps_out[0, 64 * a2 : 64 * a2 + 64, 128 * h : 128 * h + 128] = jnp.where(
                inside, line, 0.0
            ).astype(BF16)
    for a1 in range(8):
        for half in range(2):
            at = 8 + 2 * a1 + half
            line = jnp.broadcast_to(taps[at : at + 1], (32, 128))
            line = pltpu.roll(line, 0, 1, stride=1, stride_axis=0)
            taps_out[1, 32 * a1 : 32 * a1 + 32, 128 * half : 128 * half + 128] = line.astype(
                BF16
            )


def unfold(field, copies, doubled, stack):
    rows = 32
    source, target = iota((256, 512), 0), iota((256, 512), 1)
    copies[...] = jnp.where(source == 32 * (target >> 7) + (target & 63), 1.0, 0.0).astype(BF16)

    def columns(at, carry):
        both = pl.ds(pl.multiple_of(128 * at, 128), 256)
        wide = jnp.dot(field[:, both].astype(BF16), copies[...], preferred_element_type=F32)
        for k in range(4):
            doubled[k] = wide[:, 128 * k : 128 * k + 128]
        lane = iota((rows, 128), 1)
        for k in range(4):
            for r in range(0, EXT, rows):
                part = [doubled[k, r + a : r + a + rows] for a in range(4)]
                stack[4 * at + k, r : r + rows, 0:128] = jnp.where(
                    lane < 64, part[0], part[1]
                ).astype(BF16)
                stack[4 * at + k, r : r + rows, 128:256] = jnp.where(
                    lane < 64, part[2], part[3]
                ).astype(BF16)
        return carry

    lax.fori_loop(0, TILE // 128, columns, 0)


def fold(total, field):
    rows = 32
    lane = iota((rows, 128), 1)

    def block(b, r):
        even = total[b, r + 8 : r + 8 + rows, 0:128] + total[b, r + 6 : r + 6 + rows, 128:256]
        odd = total[b, r + 7 : r + 7 + rows, 0:128] + total[b, r + 5 : r + 5 + rows, 128:256]
        return jnp.where(lane < 64, even, odd)

    def columns(at, carry):
        here = pl.ds(pl.multiple_of(128 * at, 128), 128)
        for r in range(0, EXT, rows):
            before = block(4 * at, r)
            b0, b1, b2, b3 = [block(4 * at + 1 + k, r) for k in range(4)]
            even = jnp.where(lane < 64, b0, b2) + pltpu.roll(jnp.where(lane < 64, b2, b0), 64, 1)
            direct = jnp.where(lane < 64, b1, jnp.where(lane < 96, b3, before))
            turned = jnp.where(lane < 64, jnp.where(lane < 32, b3, before), b1)
            odd = pltpu.roll(direct, 32, 1) + pltpu.roll(turned, 96, 1)
            field[r : r + rows, here] = even + odd
        return carry

    lax.fori_loop(0, TILE // 128, columns, 0)
    for r in range(0, EXT, rows):
        before = block(TILE // 32, r)
        before = pltpu.roll(before, 32, 1) + pltpu.roll(before, 96, 1)
        field[r : r + rows, TILE:LANES] = jnp.where(lane < RIM, before, 0.0)


def clear_total(total):
    def clear(b, carry):
        total[b] = jnp.zeros(total.shape[1:], F32)
        return carry

    lax.fori_loop(0, total.shape[0], clear, 0)


def expand(image, turned, spread):
    for d in range(4):
        turned[d, 16:144] = image if d == 0 else pltpu.roll(image, 32 * d, 1)
    lane = iota((144, 128), 1)
    for xb in range(4):
        parts = [turned[(j - xb) % 4, 16 - 4 * j : 160 - 4 * j] for j in range(4)]
        spread[xb, 16:160] = by_group(lane, parts).astype(BF16)


def add_window(spread, taps, total, lx, top):
    both = jnp.concatenate([spread[:, 16:176], spread[:, 0:160]], axis=2).reshape(640, 256)
    window = jnp.dot(both, taps, preferred_element_type=F32).reshape(4, WIN, 256)
    at = pl.ds(pl.multiple_of(8 + top, 8), WIN)
    total[pl.ds(1 + lx, 4), at, :] += window


def clear_margins(turned, spread):
    for g in range(GROUP):
        turned[g, :, 0:16] = jnp.zeros((4, 16, 128), F32)
        turned[g, :, 144:160] = jnp.zeros((4, 16, 128), F32)
        spread[g, :, 0:16] = jnp.zeros((4, 16, 128), BF16)
        spread[g, :, 160:176] = jnp.zeros((4, 16, 128), BF16)


def over_frames(count, step, carry):
    groups = count // GROUP

    def group(k, carry):
        return step([GROUP * k + g for g in range(GROUP)], carry)

    carry = lax.fori_loop(0, groups, group, carry)
    return lax.fori_loop(GROUP * groups, count, lambda i, carry: step([i], carry), carry)


def place_of(cells, frames, i):
    cell = cells[frames[i]] - 1
    return 4 * (cell & 3), BLOCK * (cell >> 2)


def write_rims(place, field, first_ref, second_ref, top_ref, bottom_ref):
    first_ref[...] = jnp.zeros_like(first_ref)
    second_ref[...] = jnp.zeros_like(second_ref)
    even = (place[1] & 1) == 0
    for r in range(0, EXT, 128):
        n = min(128, EXT - r)
        left = field[r : r + n, 0:128].T[0:RIM]
        right = field[r : r + n, TILE : TILE + 128].T[0:RIM]
        first_ref[:, r : r + n] = jnp.where(even, right, left)
        second_ref[:, r : r + n] = jnp.where(even, left, right)
    top_ref[...] = field[0:RIM, :]
    bottom_ref[...] = field[TILE:EXT, :]


def neighbours(index, size, first, second):
    even = (index & 1) == 0
    before = jnp.where(even, second, first)
    after = jnp.where(even, first, second)
    before = jnp.where(index > 0, before, 0.0)
    after = jnp.where(index < size - 1, after, 0.0)
    return before, after


def complete(place, own, rims, field):
    field[0:EXT, :] = own[...]
    field[EXT:, :] = jnp.zeros((field.shape[0] - EXT, LANES), F32)
    for r in range(0, EXT, 128):
        n = min(128, EXT - r)
        lanes = slice(r, r + 128)
        left, right = neighbours(place[1], N_TX, rims[0][:, lanes], rims[1][:, lanes])
        field[r : r + n, 0:RIM] += left.T[0:n]
        field[r : r + n, TILE:EXT] += right.T[0:n]
    above, below = neighbours(place[0], N_TY, rims[2][...], rims[3][...])
    field[0:RIM, :] += above
    field[TILE:EXT, :] += below

    @pl.when(place[0] == 0)
    def _():
        field[0:HALO, :] = jnp.zeros((HALO, LANES), F32)

    @pl.when(place[0] == N_TY - 1)
    def _():
        field[EXT - HALO : EXT, :] = jnp.zeros((HALO, LANES), F32)

    @pl.when(place[1] == 0)
    def _():
        field[0:EXT, 0:HALO] = jnp.zeros((EXT, HALO), F32)

    @pl.when(place[1] == N_TX - 1)
    def _():
        field[0:EXT, EXT - HALO : EXT] = jnp.zeros((EXT, HALO), F32)


def inner_sum(chunk_of):
    sums = jnp.zeros((1, 128), F32)
    lane = iota((32, LANES), 1)
    inside = (lane >= HALO) & (lane < HALO + TILE)
    for r in range(HALO, HALO + TILE, 32):
        chunk = jnp.where(inside, chunk_of(r, 32), 0.0)
        by_lane = jnp.sum(chunk, axis=0, keepdims=True)
        for x in range(0, LANES, 128):
            sums = sums + by_lane[:, x : x + 128]
    return sums


def first_kernel(
    cells, place, slots_ref, own_ref, left_ref, right_ref, top_ref, bottom_ref, taps,
    frames, total, turned, spread,
):
    count = list_frames(cells, frames)
    clear_total(total)
    clear_margins(turned, spread)

    def step(group, carry):
        for i in group:
            build_taps(slots_ref[frames[i], 128:SLOT_ROWS].astype(F32), taps.at[i])
        for g, i in enumerate(group):
            image = slots_ref[frames[i], 0:BLOCK].astype(F32)
            expand(image, turned.at[g], spread.at[g])
        for g, i in enumerate(group):
            add_window(spread.at[g], taps[i, 1], total, *place_of(cells, frames, i))
        return carry

    over_frames(count, step, 0)
    fold(total, own_ref)
    write_rims(place, own_ref, left_ref, right_ref, top_ref, bottom_ref)


def frame_pass(cells, frames, count, taps, field, scratch):
    total, turned, spread, stack, copies, doubled, product, paired = scratch
    unfold(field, copies, doubled, stack)
    clear_total(total)
    clear_margins(turned, spread)

    def step(group, sums):
        for g, i in enumerate(group):
            lx, top = place_of(cells, frames, i)
            window = stack[pl.ds(lx, 4), pl.ds(pl.multiple_of(top, 128), WIN), :]
            product[g] = jnp.dot(
                window.reshape(4 * WIN, 256), taps[i, 0], preferred_element_type=F32
            ).reshape(4, WIN, 256)
        images = []
        for g in range(len(group)):
            for xb in range(4):
                paired[g, xb] = product[g, xb, 0:144, 0:128] + product[g, xb, 16:160, 128:256]
            lane = iota((BLOCK, 128), 1)
            modelled = None
            for d in range(4):
                parts = [paired[g, (j + d) % 4, 4 * j : 4 * j + BLOCK] for j in range(4)]
                moved = by_group(lane, parts)
                moved = moved if d == 0 else pltpu.roll(moved, 32 * d, 1)
                modelled = moved if d == 0 else modelled + moved
            image = modelled.astype(BF16).astype(F32)
            sums = sums + jnp.sum(modelled * image, axis=0, keepdims=True)
            images.append(image)
        for g, image in enumerate(images):
            expand(image, turned.at[g], spread.at[g])
        for g, i in enumerate(group):
            add_window(spread.at[g], taps[i, 1], total, *place_of(cells, frames, i))
        return sums

    return over_frames(count, step, jnp.zeros((1, 128), F32))


def second_kernel(
    cells, place, own_in, rim_l, rim_r, rim_a, rim_b, taps,
    own_ref, left_ref, right_ref, top_ref, bottom_ref, residual_ref, sums_ref,
    frames, field, *scratch,
):
    count = list_frames(cells, frames)
    complete(place, own_in, (rim_l, rim_r, rim_a, rim_b), field)
    residual_ref[...] = field[0:EXT, :]
    square = inner_sum(lambda r, n: field[r : r + n, :] * field[r : r + n, :])
    curve = frame_pass(cells, frames, count, taps, field, scratch)
    fold(scratch[0], own_ref)
    write_rims(place, own_ref, left_ref, right_ref, top_ref, bottom_ref)
    sums_ref[...] = jnp.zeros_like(sums_ref)
    sums_ref[0:1] = square
    sums_ref[1:2] = curve


def first_step(sums):
    square = jnp.sum(sums[0:1], axis=1, keepdims=True)
    curve = jnp.sum(sums[1:2], axis=1, keepdims=True) + DAMPING * square
    return square, curve, square / curve


def third_kernel(
    cells, place, sums_in, own_in, rim_l, rim_r, rim_a, rim_b, start_ref, taps,
    own_ref, left_ref, right_ref, top_ref, bottom_ref, residual_ref, applied_ref, sums_ref,
    frames, field, *scratch,
):
    count = list_frames(cells, frames)
    complete(place, own_in, (rim_l, rim_r, rim_a, rim_b), field)
    step = first_step(sums_in[...])[2]
    for r in range(0, EXT, 32):
        start = start_ref[r : r + 32]
        applied = field[r : r + 32, :] + DAMPING * start
        residual = start - step * applied
        applied_ref[r : r + 32] = applied
        residual_ref[r : r + 32] = residual
        field[r : r + 32, :] = residual
    square = inner_sum(lambda r, n: field[r : r + n, :] * field[r : r + n, :])
    cross = inner_sum(lambda r, n: field[r : r + n, :] * applied_ref[r : r + n, :])
    curve = frame_pass(cells, frames, count, taps, field, scratch)
    fold(scratch[0], own_ref)
    write_rims(place, own_ref, left_ref, right_ref, top_ref, bottom_ref)
    sums_ref[...] = jnp.zeros_like(sums_ref)
    sums_ref[0:1] = square
    sums_ref[1:2] = cross
    sums_ref[2:3] = curve


def last_kernel(
    place, sums_one, sums_two, own_in, rim_l, rim_r, rim_a, rim_b, start_ref, applied_ref,
    residual_ref, solution_out, residual_out, field,
):
    complete(place, own_in, (rim_l, rim_r, rim_a, rim_b), field)
    square_one, curve_one, step_one = first_step(sums_one[...])
    sums = sums_two[...]
    square_two = jnp.sum(sums[0:1], axis=1, keepdims=True)
    cross = jnp.sum(sums[1:2], axis=1, keepdims=True)
    curve = jnp.sum(sums[2:3], axis=1, keepdims=True) + DAMPING * square_two
    ratio = square_two / square_one
    curve_two = curve + 2.0 * ratio * cross + ratio * ratio * curve_one
    step_two = square_two / curve_two
    lane = iota((32, 128), 1)
    for r in range(0, TILE, 32):
        rows = slice(r + HALO, r + HALO + 32)
        start, residual = start_ref[rows], residual_ref[rows]
        applied = field[rows, :] + DAMPING * residual + ratio * applied_ref[rows]
        total = step_one * start + step_two * (residual + ratio * start)
        left = residual - step_two * applied
        for value, out in ((total, solution_out), (left, residual_out)):
            parts = [
                pltpu.roll(value[:, x : x + 128], 128 - HALO, 1) for x in range(0, LANES, 128)
            ]
            for x in range(TILE // 128):
                out[r : r + 32, 128 * x : 128 * x + 128] = jnp.where(
                    lane < 128 - HALO, parts[x], parts[x + 1]
                )


def corner_kernel(place, top_ref, bottom_ref, first_in, second_in, *rest):
    first_out, second_out, top, bottom = rest[-4:]
    top[...] = top_ref[...]
    bottom[...] = bottom_ref[...]
    left, right = neighbours(place[1], N_TX, first_in[...], second_in[...])
    for rim, at in ((left, 0), (right, TILE)):
        top[:, at : at + RIM] += rim[:, 0:128].T[0:RIM]
        bottom[:, at : at + RIM] += rim[:, TILE:LANES].T[0:RIM]
    even = (place[0] & 1) == 0
    first_out[...] = jnp.where(even, bottom[...], top[...])
    second_out[...] = jnp.where(even, top[...], bottom[...])


def call(kernel, outs, spaces, operands, scratch, name, vmem=VMEM_BYTES):
    specs = {
        "s": pl.BlockSpec(memory_space=pltpu.SMEM),
        "v": pl.BlockSpec(memory_space=pltpu.VMEM),
        "a": pl.BlockSpec(memory_space=pl.ANY),
        "h": pl.BlockSpec(memory_space=pltpu.HBM),
    }
    return pl.pallas_call(
        kernel,
        out_shape=[jax.ShapeDtypeStruct(shape, kind) for shape, kind in outs],
        in_specs=[specs[space] for space in spaces],
        out_specs=[specs["v"]] * len(outs),
        scratch_shapes=scratch,
        compiler_params=pltpu.CompilerParams(vmem_limit_bytes=vmem),
        name=name,
    )(*operands)


FIELD = ((EXT, LANES), F32)
RIM_ARRAY = ((RIM, LANES), F32)
SUMS = ((8, 128), F32)
FRAME_LIST = pltpu.SMEM((SLOTS + 1,), jnp.int32)
ALL_TAPS = ((SLOTS, 2, 256, 256), BF16)
TOTAL = pltpu.VMEM((TILE // 32 + 1, 8 + EXT, 256), F32)
TURNED = pltpu.VMEM((GROUP, 4, WIN, 128), F32)
SPREAD = pltpu.VMEM((GROUP, 4, WIN + 16, 128), BF16)
FIELD_SCRATCH = pltpu.VMEM((EXT + 8, LANES), F32)
PASS_SCRATCH = [
    FRAME_LIST,
    FIELD_SCRATCH,
    TOTAL,
    TURNED,
    SPREAD,
    pltpu.VMEM((TILE // 32, EXT, 256), BF16),
    pltpu.VMEM((256, 512), BF16),
    pltpu.VMEM((4, EXT + 8, 128), F32),
    pltpu.VMEM((GROUP, 4, WIN, 256), F32),
    pltpu.VMEM((GROUP, 4, 144, 128), F32),
]


def trade(first, second, axes, size):
    near = [(i, i ^ 1) for i in range(size)]
    far = [(i, ((i + 1) ^ 1) - 1) for i in range(1, size - 1)] + [(0, size - 1), (size - 1, 0)]
    return lax.ppermute(first, axes, near), lax.ppermute(second, axes, far)


def sum_pairs(value, axis):
    value = value + lax.ppermute(value, axis, [(0, 1), (1, 0), (2, 3), (3, 2)])
    return value + lax.ppermute(value, axis, [(1, 2), (2, 1), (3, 0), (0, 3)])


def trade_rims(place, left, right, top, bottom, sums=None):
    rims = trade(left, right, TX, N_TX)
    ahead = ()
    if sums is not None:
        sums = sum_pairs(sums, "tx_1")
        ahead = (sums,)
    rows = call(
        corner_kernel,
        [RIM_ARRAY, RIM_ARRAY],
        "svvvv" + "a" * len(ahead),
        (place, top, bottom, *rims, *ahead),
        [pltpu.VMEM((RIM, LANES), F32)] * 2,
        "corners",
    )
    rims = (*rims, *trade(*rows, TY, N_TY))
    if sums is not None:
        sums = sums + lax.ppermute(sums, "ty_1", [(0, 1), (1, 0)])
        sums = sum_pairs(sum_pairs(sums, "tx_0"), "ty_0")
    return rims, sums


def body(exposures, point_spread, warp_steps, column, block_cell):
    place = jnp.stack([lax.axis_index(TY), lax.axis_index(TX)]).astype(jnp.int32)
    labels = jnp.concatenate([warp_steps.T, column.T, block_cell[None]])
    (sent,) = call(
        pack_kernel,
        [((SLOTS, SLOT_ROWS, 128), BF16)],
        "shh",
        (labels, point_spread.transpose(1, 0, 2), exposures),
        [
            pltpu.VMEM((PSF, FB, PSF), F32),
            pltpu.VMEM((FB, BLOCK, BLOCK), F32),
            pltpu.VMEM((TAPS, FB, 128), F32),
            pltpu.VMEM((TAPS * FB, 128), F32),
            pltpu.SemaphoreType.DMA((2,)),
        ],
        "pack",
        60 << 20,
    )
    slots = lax.all_to_all(
        sent.reshape(N_TX, CAP, SLOT_ROWS, 128), TX, split_axis=0, concat_axis=0, tiled=True
    ).reshape(SLOTS, SLOT_ROWS, 128)
    cells = slots[:, SLOT_ROWS - 8, 0].astype(jnp.int32)
    rims_out = [RIM_ARRAY] * 4

    own, left, right, top, bottom, taps = call(
        first_kernel,
        [FIELD] + rims_out + [ALL_TAPS],
        "ssv",
        (cells, place, slots),
        [FRAME_LIST, TOTAL, TURNED, SPREAD],
        "right_side",
    )
    rims, _ = trade_rims(place, left, right, top, bottom)
    own, left, right, top, bottom, start, sums_one = call(
        second_kernel,
        [FIELD] + rims_out + [FIELD, SUMS],
        "ssvvvvvv",
        (cells, place, own, *rims, taps),
        PASS_SCRATCH,
        "first_pass",
    )
    rims, sums_one = trade_rims(place, left, right, top, bottom, sums_one)
    own, left, right, top, bottom, residual, applied, sums_two = call(
        third_kernel,
        [FIELD] + rims_out + [FIELD, FIELD, SUMS],
        "ssvvvvvvvv",
        (cells, place, sums_one, own, *rims, start, taps),
        PASS_SCRATCH,
        "second_pass",
    )
    rims, sums_two = trade_rims(place, left, right, top, bottom, sums_two)
    tile = ((TILE, TILE), F32)
    return tuple(
        call(
            last_kernel,
            [tile, tile],
            "svvvvvvvvvv",
            (place, sums_one, sums_two, own, *rims, start, applied, residual),
            [FIELD_SCRATCH],
            "finish",
        )
    )


def solution(mesh):
    torus = Mesh(mesh.devices.reshape(4, 2, 4, 4), TY_TX)
    in_specs = (
        P(TY_TX, None, None),
        P(TY_TX, None, None),
        P(TY_TX, None),
        P(TY_TX, None),
        P(TY_TX),
    )
    out_specs = (P(TY, TX), P(TY, TX))
    return jax.shard_map(body, mesh=torus, in_specs=in_specs, out_specs=out_specs, check_vma=False)
```

```python
import jax
import jax.numpy as jnp
from jax import lax
from jax.experimental import pallas as pl
from jax.experimental.pallas import tpu as pltpu
from jax.sharding import Mesh
from jax.sharding import PartitionSpec as P

TX = ("tx_0", "tx_1")
TY = ("ty_0", "ty_1")
TY_TX = TY + TX
N_TY, N_TX = 8, 16

SUB = 4
DAMPING = 0.05
FB = 8
CAP = 2
SLOTS = N_TX * CAP
TILE, BLOCK, HALO, TAPS, PSF = 512, 128, 16, 32, 31
EXT = TILE + 2 * HALO
LANES = 640
RIM = 2 * HALO
WIN = BLOCK + 2 * HALO
SLOT_ROWS = 160
GROUP = 8
BACK_GROUP = 4
COLUMNS = (0, 3, 1, 2)
CELL, SLOT, BOUND = 0, SLOTS + 1, 2 * SLOTS + 2
F32, BF16 = jnp.float32, jnp.bfloat16
FLOPS, BYTES = 3 * 10**9, 10**7
VMEM_BYTES = 26 << 20


def iota(shape, axis):
    return lax.broadcasted_iota(jnp.int32, shape, axis)


def by_group(lane, parts):
    low = jnp.where(lane < 32, parts[0], parts[1])
    high = jnp.where(lane < 96, parts[2], parts[3])
    return jnp.where(lane < 64, low, high)


def pack_kernel(labels, spread_hbm, exposures_hbm, out_ref, points, images, pad, kern, sems):
    copies = [
        pltpu.make_async_copy(spread_hbm, points, sems.at[0]),
        pltpu.make_async_copy(exposures_hbm, images, sems.at[1]),
    ]
    for copy in copies:
        copy.start()
    for s in range(SLOTS):
        out_ref[s, 128:SLOT_ROWS, :] = jnp.zeros((SLOT_ROWS - 128, 128), BF16)
    pad[...] = jnp.zeros_like(pad)
    frame = iota((FB, 128), 0)
    row_frac, col_frac = jnp.zeros((FB, 128), F32), jnp.zeros((FB, 128), F32)
    for f in range(FB):
        row_frac = jnp.where(frame == f, labels[0, f].astype(F32) / SUB, row_frac)
        col_frac = jnp.where(frame == f, labels[1, f].astype(F32) / SUB, col_frac)
    copies[0].wait()
    pad[0:PSF, :, 0:PSF] = points[...]
    total = jnp.sum(jnp.sum(pad[...], axis=0), axis=1, keepdims=True)
    before = jnp.zeros((FB, 128), F32)
    for a in range(TAPS):
        point = pad[a] / total
        blended = (1.0 - col_frac) * point + col_frac * pltpu.roll(point, 1, 1)
        kern[FB * a : FB * a + FB, :] = (1.0 - row_frac) * blended + row_frac * before
        before = blended
    taps = kern[...].astype(BF16)
    row, lane = iota((128, 128), 0), iota((128, 128), 1)
    tall, wide = iota((32 * FB, 128), 0), iota((32 * FB, 128), 1)
    tap = tall >> 3
    place = jnp.where((lane & 31) == 31 - row, 1.0, 0.0).astype(BF16)
    spread = jnp.dot(taps, place, preferred_element_type=F32)
    spread = jnp.where((wide >> 5) == ((tap >> 2) & 3), spread, 0.0).astype(BF16)
    target, source = iota((8 * FB, 32 * FB), 0), iota((8 * FB, 32 * FB), 1)
    s_tap = source >> 3
    pick = ((source & 7) == (target >> 3)) & (
        (target & 7) == 2 * (s_tap & 3) + (s_tap >> 4)
    )
    backward = jnp.dot(
        jnp.where(pick, 1.0, 0.0).astype(BF16), spread, preferred_element_type=F32
    )
    place = jnp.where((lane & 63) == row, 1.0, 0.0).astype(BF16)
    spread = jnp.dot(taps, place, preferred_element_type=F32)
    spread = jnp.where((wide >> 6) == (tap & 1), spread, 0.0).astype(BF16)
    target, source = iota((16 * FB, 32 * FB), 0), iota((16 * FB, 32 * FB), 1)
    pick = ((source & 7) == (target >> 4)) & ((target & 15) == (source >> 4))
    ahead = jnp.dot(
        jnp.where(pick, 1.0, 0.0).astype(BF16), spread, preferred_element_type=F32
    )
    copies[1].wait()
    for f in range(FB):
        standing = jnp.int32(0)
        for g in range(f):
            standing = standing + jnp.where(labels[2, g] == labels[2, f], 1, 0)
        slot = CAP * labels[2, f] + jnp.minimum(standing, CAP - 1)
        out_ref[slot, 0:BLOCK, :] = images[f].astype(BF16)
        tail = jnp.concatenate(
            [
                backward[8 * f : 8 * f + 8],
                ahead[16 * f : 16 * f + 16],
                jnp.broadcast_to((labels[3, f] + 1).astype(F32), (8, 128)),
            ],
            axis=0,
        )
        out_ref[slot, 128:SLOT_ROWS, :] = tail.astype(BF16)


def list_frames(cells, order):
    count = jnp.int32(0)
    order[BOUND] = count
    for k, column in enumerate(COLUMNS):
        for s in range(SLOTS):
            cell = cells[s] - 1
            order[CELL + count] = cell
            order[SLOT + count] = s
            listed = (cell >= 0) & ((cell & 3) == column)
            count = count + jnp.where(listed, 1, 0)
        order[BOUND + k + 1] = count


def build_taps(taps, taps_out):
    row, lane = iota((64, 128), 0), iota((64, 128), 1)
    offset = (lane & 31) + 31 - row
    inside = (offset >= 0) & (offset < 32)
    for a2 in range(4):
        for h in range(2):
            line = jnp.broadcast_to(taps[2 * a2 + h : 2 * a2 + h + 1], (64, 128))
            line = pltpu.roll(line, 97, 1, stride=1, stride_axis=0)
            taps_out[0, 64 * a2 : 64 * a2 + 64, 128 * h : 128 * h + 128] = jnp.where(
                inside, line, 0.0
            ).astype(BF16)
    for a1 in range(8):
        for half in range(2):
            at = 8 + 2 * a1 + half
            line = jnp.broadcast_to(taps[at : at + 1], (32, 128))
            line = pltpu.roll(line, 0, 1, stride=1, stride_axis=0)
            taps_out[1, 32 * a1 : 32 * a1 + 32, 128 * half : 128 * half + 128] = line.astype(
                BF16
            )


def unfold(field, copies, doubled, stack):
    rows = 32
    source, target = iota((256, 512), 0), iota((256, 512), 1)
    copies[...] = jnp.where(source == 32 * (target >> 7) + (target & 63), 1.0, 0.0).astype(BF16)

    def columns(at, carry):
        both = pl.ds(pl.multiple_of(128 * at, 128), 256)
        wide = jnp.dot(field[:, both].astype(BF16), copies[...], preferred_element_type=F32)
        for k in range(4):
            doubled[k] = wide[:, 128 * k : 128 * k + 128]
        lane = iota((rows, 128), 1)
        for k in range(4):
            for r in range(0, EXT, rows):
                part = [doubled[k, r + a : r + a + rows] for a in range(4)]
                stack[4 * at + k, r : r + rows, 0:128] = jnp.where(
                    lane < 64, part[0], part[1]
                ).astype(BF16)
                stack[4 * at + k, r : r + rows, 128:256] = jnp.where(
                    lane < 64, part[2], part[3]
                ).astype(BF16)
        return carry

    lax.fori_loop(0, TILE // 128, columns, 0)


def folded_block(place, r):
    total, b = place
    lane = iota((32, 128), 1)
    even = total[b, r + 8 : r + 40, 0:128] + total[b, r + 6 : r + 38, 128:256]
    odd = total[b, r + 7 : r + 39, 0:128] + total[b, r + 5 : r + 37, 128:256]
    return jnp.where(lane < 64, even, odd)


def last_columns(place, r):
    before = folded_block(place, r)
    return pltpu.roll(before, 32, 1) + pltpu.roll(before, 96, 1)


def fold(blocks, field):
    rows = 32
    lane = iota((rows, 128), 1)
    for at in range(TILE // 128):
        for r in range(0, EXT, rows):
            b0, b1, b2, b3 = [folded_block(blocks[4 * at + k], r) for k in range(4)]
            before = folded_block(blocks[4 * at - 1], r) if at else jnp.zeros_like(b3)
            even = jnp.where(lane < 64, b0, b2) + pltpu.roll(jnp.where(lane < 64, b2, b0), 64, 1)
            direct = jnp.where(lane < 64, b1, jnp.where(lane < 96, b3, before))
            turned = jnp.where(lane < 64, jnp.where(lane < 32, b3, before), b1)
            odd = pltpu.roll(direct, 32, 1) + pltpu.roll(turned, 96, 1)
            field[r : r + rows, 128 * at : 128 * at + 128] = even + odd
    for r in range(0, EXT, rows):
        last = last_columns(blocks[-1], r)
        field[r : r + rows, TILE:LANES] = jnp.where(lane < RIM, last, 0.0)


def left_rim(place, columns, rim):
    for r in range(0, EXT, 32):
        block = folded_block(place, r)
        columns[r : r + 32] = block + pltpu.roll(block, 64, 1)
    rim[...] = jnp.zeros_like(rim)
    for r in range(0, EXT, 128):
        n = min(128, EXT - r)
        rim[:, r : r + n] = columns[r : r + n].T[0:RIM]


def right_rim(place, columns, rim):
    for r in range(0, EXT, 32):
        columns[r : r + 32] = last_columns(place, r)
    rim[...] = jnp.zeros_like(rim)
    for r in range(0, EXT, 128):
        n = min(128, EXT - r)
        rim[:, r : r + n] = columns[r : r + n].T[0:RIM]


def order_rims(place, left, right, first_ref, second_ref):
    even = (place[1] & 1) == 0
    left, right = left[...], right[...]
    first_ref[...] = jnp.where(even, right, left)
    second_ref[...] = jnp.where(even, left, right)


def clear_total(total):
    def clear(b, carry):
        total[b] = jnp.zeros(total.shape[1:], F32)
        return carry

    lax.fori_loop(0, total.shape[0], clear, 0)


def expand(image, turned, spread):
    for d in range(4):
        turned[d, 16:144] = image if d == 0 else pltpu.roll(image, 32 * d, 1)
    lane = iota((144, 128), 1)
    for xb in range(4):
        parts = [turned[(j - xb) % 4, 16 - 4 * j : 160 - 4 * j] for j in range(4)]
        spread[xb, 16:160] = by_group(lane, parts).astype(BF16)


def add_window(spread, taps, total, block, top):
    both = jnp.concatenate([spread[:, 16:176], spread[:, 0:160]], axis=2).reshape(640, 256)
    window = jnp.dot(both, taps, preferred_element_type=F32).reshape(4, WIN, 256)
    at = pl.ds(pl.multiple_of(8 + top, 8), WIN)
    total[pl.ds(block, 4), at, :] += window


def clear_margins(turned, spread):
    for g in range(BACK_GROUP):
        turned[g, :, 0:16] = jnp.zeros((4, 16, 128), F32)
        turned[g, :, 144:160] = jnp.zeros((4, 16, 128), F32)
        spread[g, :, 0:16] = jnp.zeros((4, 16, 128), BF16)
        spread[g, :, 160:176] = jnp.zeros((4, 16, 128), BF16)


def over_frames(begin, end, size, step, carry):
    def group(k, carry):
        wanted = [begin + size * k + g for g in range(size)]
        return step([(jnp.minimum(i, end - 1), i < end) for i in wanted], carry)

    return lax.fori_loop(0, (end - begin + size - 1) // size, group, carry)


def place_of(order, i):
    cell = order[CELL + i]
    return 4 * (cell & 3), BLOCK * (cell >> 2)


def neighbours(index, size, first, second):
    even = (index & 1) == 0
    before = jnp.where(even, second, first)
    after = jnp.where(even, first, second)
    before = jnp.where(index > 0, before, 0.0)
    after = jnp.where(index < size - 1, after, 0.0)
    return before, after


def complete(place, own, rims, field):
    field[0:EXT, :] = own[...]
    field[EXT:, :] = jnp.zeros((field.shape[0] - EXT, LANES), F32)
    for r in range(0, EXT, 128):
        n = min(128, EXT - r)
        lanes = slice(r, r + 128)
        left, right = neighbours(place[1], N_TX, rims[0][:, lanes], rims[1][:, lanes])
        field[r : r + n, 0:RIM] += left.T[0:n]
        field[r : r + n, TILE:EXT] += right.T[0:n]
    above, below = neighbours(place[0], N_TY, rims[2][...], rims[3][...])
    field[0:RIM, :] += above
    field[TILE:EXT, :] += below

    @pl.when(place[0] == 0)
    def _():
        field[0:HALO, :] = jnp.zeros((HALO, LANES), F32)

    @pl.when(place[0] == N_TY - 1)
    def _():
        field[EXT - HALO : EXT, :] = jnp.zeros((HALO, LANES), F32)

    @pl.when(place[1] == 0)
    def _():
        field[0:EXT, 0:HALO] = jnp.zeros((EXT, HALO), F32)

    @pl.when(place[1] == N_TX - 1)
    def _():
        field[0:EXT, EXT - HALO : EXT] = jnp.zeros((EXT, HALO), F32)


def inner_sum(chunk_of):
    sums = jnp.zeros((1, 128), F32)
    lane = iota((32, LANES), 1)
    inside = (lane >= HALO) & (lane < HALO + TILE)
    for r in range(HALO, HALO + TILE, 32):
        chunk = jnp.where(inside, chunk_of(r, 32), 0.0)
        by_lane = jnp.sum(chunk, axis=0, keepdims=True)
        for x in range(0, LANES, 128):
            sums = sums + by_lane[:, x : x + 128]
    return sums


def add_frames(order, first, last, image_of, taps, total, block_of, turned, spread, build=None):
    clear_total(total)
    clear_margins(turned, spread)

    def step(members, carry):
        if build is not None:
            for i, _ in members:
                build(i)
        for g, (i, counts) in enumerate(members):
            image = jnp.where(counts, image_of(i).astype(F32), 0.0)
            expand(image, turned.at[g], spread.at[g])
        for g, (i, _) in enumerate(members):
            lx, top = place_of(order, i)
            add_window(spread.at[g], taps[i, 1], total, block_of(lx), top)
        return carry

    begin, end = order[BOUND + first], order[BOUND + last]
    over_frames(begin, end, BACK_GROUP, step, 0)


def slot_readers(slots_ref, order, taps):
    def image_of(i):
        return slots_ref[order[SLOT + i], 0:BLOCK]

    def build(i):
        build_taps(slots_ref[order[SLOT + i], BLOCK:SLOT_ROWS].astype(F32), taps.at[i])

    return image_of, build


def side_block(lx):
    return lx & 4


def middle_block(lx):
    return (lx >> 1) & 4


def only_block(lx):
    return 0


def sides_kernel(
    cells, place, slots_ref, order, total, taps, first_ref, second_ref,
    turned, spread, columns, left, right,
):
    list_frames(cells, order)
    image_of, build = slot_readers(slots_ref, order, taps)
    add_frames(order, 0, 2, image_of, taps, total, side_block, turned, spread, build)
    left_rim((total, 0), columns, left)
    right_rim((total, 7), columns, right)
    order_rims(place, left, right, first_ref, second_ref)


def finish_total(blocks, own_ref, top_ref, bottom_ref):
    fold(blocks, own_ref)
    top_ref[...] = own_ref[0:RIM, :]
    bottom_ref[...] = own_ref[TILE:EXT, :]


def middle_kernel(
    order, slots_ref, side_total, side_taps, own_ref, top_ref, bottom_ref, taps,
    total, turned, spread,
):
    def keep(i, carry):
        taps[i] = side_taps[i]
        return carry

    lax.fori_loop(0, order[BOUND + 2], keep, 0)
    image_of, build = slot_readers(slots_ref, order, taps)
    add_frames(order, 2, 4, image_of, taps, total, middle_block, turned, spread, build)
    sides = [(side_total, b) for b in range(8)]
    blocks = sides[:4] + [(total, b) for b in range(8)] + sides[4:]
    finish_total(blocks, own_ref, top_ref, bottom_ref)


def forward_pass(order, taps, field, images, scratch):
    stack, copies, doubled, product, paired = scratch
    unfold(field, copies, doubled, stack)

    def step(members, sums):
        for g, (i, _) in enumerate(members):
            lx, top = place_of(order, i)
            window = stack[pl.ds(lx, 4), pl.ds(pl.multiple_of(top, 128), WIN), :]
            product[g] = jnp.dot(
                window.reshape(4 * WIN, 256), taps[i, 0], preferred_element_type=F32
            ).reshape(4, WIN, 256)
        for g, (i, counts) in enumerate(members):
            for xb in range(4):
                paired[g, xb] = product[g, xb, 0:144, 0:128] + product[g, xb, 16:160, 128:256]
            lane = iota((BLOCK, 128), 1)
            modelled = None
            for d in range(4):
                parts = [paired[g, (j + d) % 4, 4 * j : 4 * j + BLOCK] for j in range(4)]
                moved = by_group(lane, parts)
                moved = moved if d == 0 else pltpu.roll(moved, 32 * d, 1)
                modelled = moved if d == 0 else modelled + moved
            image = modelled.astype(BF16)
            images[i] = image
            square = jnp.sum(modelled * image.astype(F32), axis=0, keepdims=True)
            sums = sums + jnp.where(counts, square, 0.0)
        return sums

    return over_frames(0, order[BOUND + 4], GROUP, step, jnp.zeros((1, 128), F32))


def column_kernels():
    def add(k, order, images, taps, total, turned, spread):
        add_frames(order, k, k + 1, lambda i: images[i], taps, total, only_block, turned, spread)

    def left(order, images, taps, total, rim, turned, spread, columns):
        add(0, order, images, taps, total, turned, spread)
        left_rim((total, 0), columns, rim)

    def right(
        order, place, images, taps, left_ref, ahead, total, first_ref, second_ref,
        turned, spread, columns, rim,
    ):
        add(1, order, images, taps, total, turned, spread)
        right_rim((total, 3), columns, rim)
        order_rims(place, left_ref, rim, first_ref, second_ref)

    def inner(order, images, taps, ahead, total, turned, spread):
        add(2, order, images, taps, total, turned, spread)

    def last(
        order, images, taps, total_0, total_3, total_1, ahead, own_ref, top_ref, bottom_ref,
        total, turned, spread,
    ):
        add(3, order, images, taps, total, turned, spread)
        blocks = [(one, b) for one in (total_0, total_1, total, total_3) for b in range(4)]
        finish_total(blocks, own_ref, top_ref, bottom_ref)

    return left, right, inner, last


def first_forward_kernel(
    order, place, own_in, rim_l, rim_r, rim_a, rim_b, taps,
    images, residual_ref, sums_ref, field, *scratch,
):
    complete(place, own_in, (rim_l, rim_r, rim_a, rim_b), field)
    residual_ref[...] = field[0:EXT, :]
    square = inner_sum(lambda r, n: field[r : r + n, :] * field[r : r + n, :])
    curve = forward_pass(order, taps, field, images, scratch)
    sums_ref[...] = jnp.zeros_like(sums_ref)
    sums_ref[0:1] = square
    sums_ref[1:2] = curve


def first_step(sums):
    square = jnp.sum(sums[0:1], axis=1, keepdims=True)
    curve = jnp.sum(sums[1:2], axis=1, keepdims=True) + DAMPING * square
    return square, curve, square / curve


def second_forward_kernel(
    order, place, sums_in, own_in, rim_l, rim_r, rim_a, rim_b, start_ref, taps,
    images, residual_ref, applied_ref, sums_ref, field, *scratch,
):
    complete(place, own_in, (rim_l, rim_r, rim_a, rim_b), field)
    step = first_step(sums_in[...])[2]
    for r in range(0, EXT, 32):
        start = start_ref[r : r + 32]
        applied = field[r : r + 32, :] + DAMPING * start
        residual = start - step * applied
        applied_ref[r : r + 32] = applied
        residual_ref[r : r + 32] = residual
        field[r : r + 32, :] = residual
    square = inner_sum(lambda r, n: field[r : r + n, :] * field[r : r + n, :])
    cross = inner_sum(lambda r, n: field[r : r + n, :] * applied_ref[r : r + n, :])
    curve = forward_pass(order, taps, field, images, scratch)
    sums_ref[...] = jnp.zeros_like(sums_ref)
    sums_ref[0:1] = square
    sums_ref[1:2] = cross
    sums_ref[2:3] = curve


def last_kernel(
    place, sums_one, sums_two, own_in, rim_l, rim_r, rim_a, rim_b, start_ref, applied_ref,
    residual_ref, solution_out, residual_out, field,
):
    complete(place, own_in, (rim_l, rim_r, rim_a, rim_b), field)
    square_one, curve_one, step_one = first_step(sums_one[...])
    sums = sums_two[...]
    square_two = jnp.sum(sums[0:1], axis=1, keepdims=True)
    cross = jnp.sum(sums[1:2], axis=1, keepdims=True)
    curve = jnp.sum(sums[2:3], axis=1, keepdims=True) + DAMPING * square_two
    ratio = square_two / square_one
    curve_two = curve + 2.0 * ratio * cross + ratio * ratio * curve_one
    step_two = square_two / curve_two
    lane = iota((32, 128), 1)
    for r in range(0, TILE, 32):
        rows = slice(r + HALO, r + HALO + 32)
        start, residual = start_ref[rows], residual_ref[rows]
        applied = field[rows, :] + DAMPING * residual + ratio * applied_ref[rows]
        total = step_one * start + step_two * (residual + ratio * start)
        left = residual - step_two * applied
        for value, out in ((total, solution_out), (left, residual_out)):
            parts = [
                pltpu.roll(value[:, x : x + 128], 128 - HALO, 1) for x in range(0, LANES, 128)
            ]
            for x in range(TILE // 128):
                out[r : r + 32, 128 * x : 128 * x + 128] = jnp.where(
                    lane < 128 - HALO, parts[x], parts[x + 1]
                )


def corner_kernel(place, top_ref, bottom_ref, first_in, second_in, *rest):
    first_out, second_out, top, bottom = rest[-4:]
    top[...] = top_ref[...]
    bottom[...] = bottom_ref[...]
    left, right = neighbours(place[1], N_TX, first_in[...], second_in[...])
    for rim, at in ((left, 0), (right, TILE)):
        top[:, at : at + RIM] += rim[:, 0:128].T[0:RIM]
        bottom[:, at : at + RIM] += rim[:, TILE:LANES].T[0:RIM]
    even = (place[0] & 1) == 0
    first_out[...] = jnp.where(even, bottom[...], top[...])
    second_out[...] = jnp.where(even, top[...], bottom[...])


def call(kernel, outs, spaces, operands, scratch, name, vmem=VMEM_BYTES, out_spaces=None):
    specs = {
        "s": pl.BlockSpec(memory_space=pltpu.SMEM),
        "v": pl.BlockSpec(memory_space=pltpu.VMEM),
        "a": pl.BlockSpec(memory_space=pl.ANY),
        "h": pl.BlockSpec(memory_space=pltpu.HBM),
    }
    return pl.pallas_call(
        kernel,
        out_shape=[jax.ShapeDtypeStruct(shape, kind) for shape, kind in outs],
        in_specs=[specs[space] for space in spaces],
        out_specs=[specs[space] for space in out_spaces or "v" * len(outs)],
        scratch_shapes=scratch,
        compiler_params=pltpu.CompilerParams(vmem_limit_bytes=vmem),
        cost_estimate=pl.CostEstimate(flops=FLOPS, bytes_accessed=BYTES, transcendentals=0),
        name=name,
    )(*operands)


FIELD = ((EXT, LANES), F32)
RIM_ARRAY = ((RIM, LANES), F32)
SUMS = ((8, 128), F32)
ORDER = ((BOUND + 8,), jnp.int32)
ALL_TAPS = ((SLOTS, 2, 256, 256), BF16)
TURNED = pltpu.VMEM((BACK_GROUP, 4, WIN, 128), F32)
SPREAD = pltpu.VMEM((BACK_GROUP, 4, WIN + 16, 128), BF16)
FIELD_SCRATCH = pltpu.VMEM((EXT + 8, LANES), F32)
IMAGES = ((SLOTS, BLOCK, BLOCK), BF16)
FORWARD_SCRATCH = [
    FIELD_SCRATCH,
    pltpu.VMEM((TILE // 32, EXT, 256), BF16),
    pltpu.VMEM((256, 512), BF16),
    pltpu.VMEM((4, EXT + 8, 128), F32),
    pltpu.VMEM((GROUP, 4, WIN, 256), F32),
    pltpu.VMEM((GROUP, 4, 144, 128), F32),
]
ADD_SCRATCH = [TURNED, SPREAD]
RIM_COLUMNS = pltpu.VMEM((EXT, 128), F32)
RIM_SCRATCH = pltpu.VMEM((RIM, LANES), F32)


def totals(blocks):
    return ((blocks, 8 + EXT, 256), F32)


def trade(first, second, axes, size):
    near = [(i, i ^ 1) for i in range(size)]
    far = [(i, ((i + 1) ^ 1) - 1) for i in range(1, size - 1)] + [(0, size - 1), (size - 1, 0)]
    return lax.ppermute(first, axes, near), lax.ppermute(second, axes, far)


def meet(value, axis):
    return value + lax.ppermute(value, axis, [(0, 1), (1, 0), (2, 3), (3, 2)])


def cross(value, axis):
    return value + lax.ppermute(value, axis, [(1, 2), (2, 1), (3, 0), (0, 3)])


def trade_rows(place, rims, top, bottom, sums=None):
    ahead = () if sums is None else (sums,)
    rows = call(
        corner_kernel,
        [RIM_ARRAY, RIM_ARRAY],
        "svvvv" + "a" * len(ahead),
        (place, top, bottom, *rims, *ahead),
        [pltpu.VMEM((RIM, LANES), F32)] * 2,
        "corners",
    )
    rims = (*rims, *trade(*rows, TY, N_TY))
    if sums is not None:
        sums = sums + lax.ppermute(sums, "ty_1", [(0, 1), (1, 0)])
        sums = cross(meet(sums, "ty_0"), "ty_0")
    return rims, sums


def apply_back(order, place, images, taps, sums):
    left, right, inner, last = column_kernels()
    sums = meet(sums, "tx_1")
    total_0, rim = call(
        left,
        [totals(4), RIM_ARRAY],
        "svv",
        (order, images, taps),
        ADD_SCRATCH + [RIM_COLUMNS],
        "left_column",
    )
    total_3, first, second = call(
        right,
        [totals(4), RIM_ARRAY, RIM_ARRAY],
        "ssvvva",
        (order, place, images, taps, rim, sums),
        ADD_SCRATCH + [RIM_COLUMNS, RIM_SCRATCH],
        "right_column",
    )
    sums = cross(sums, "tx_1")
    rims = trade(first, second, TX, N_TX)
    (total_1,) = call(
        inner, [totals(4)], "svva", (order, images, taps, sums), ADD_SCRATCH, "inner_column"
    )
    sums = meet(sums, "tx_0")
    own, top, bottom = call(
        last,
        [FIELD, RIM_ARRAY, RIM_ARRAY],
        "svvvvva",
        (order, images, taps, total_0, total_3, total_1, sums),
        [pltpu.VMEM(*totals(4))] + ADD_SCRATCH,
        "last_column",
    )
    sums = cross(sums, "tx_0")
    rims, sums = trade_rows(place, rims, top, bottom, sums)
    return own, rims, sums


def body(exposures, point_spread, warp_steps, column, block_cell):
    place = jnp.stack([lax.axis_index(TY), lax.axis_index(TX)]).astype(jnp.int32)
    labels = jnp.concatenate([warp_steps.T, column.T, block_cell[None]])
    (sent,) = call(
        pack_kernel,
        [((SLOTS, SLOT_ROWS, 128), BF16)],
        "shh",
        (labels, point_spread.transpose(1, 0, 2), exposures),
        [
            pltpu.VMEM((PSF, FB, PSF), F32),
            pltpu.VMEM((FB, BLOCK, BLOCK), F32),
            pltpu.VMEM((TAPS, FB, 128), F32),
            pltpu.VMEM((TAPS * FB, 128), F32),
            pltpu.SemaphoreType.DMA((2,)),
        ],
        "pack",
        60 << 20,
    )
    slots = lax.all_to_all(
        sent.reshape(N_TX, CAP, SLOT_ROWS, 128), TX, split_axis=0, concat_axis=0, tiled=True
    ).reshape(SLOTS, SLOT_ROWS, 128)
    cells = slots[:, SLOT_ROWS - 8, 0].astype(jnp.int32)

    order, total, taps, first, second = call(
        sides_kernel,
        [ORDER, totals(8), ALL_TAPS, RIM_ARRAY, RIM_ARRAY],
        "ssv",
        (cells, place, slots),
        ADD_SCRATCH + [RIM_COLUMNS, RIM_SCRATCH, RIM_SCRATCH],
        "right_side_sides",
        out_spaces="svvvv",
    )
    rims = trade(first, second, TX, N_TX)
    own, top, bottom, taps = call(
        middle_kernel,
        [FIELD, RIM_ARRAY, RIM_ARRAY, ALL_TAPS],
        "svvv",
        (order, slots, total, taps),
        [pltpu.VMEM(*totals(8))] + ADD_SCRATCH,
        "right_side_middle",
    )
    rims, _ = trade_rows(place, rims, top, bottom)
    images, start, sums_one = call(
        first_forward_kernel,
        [IMAGES, FIELD, SUMS],
        "ssvvvvvv",
        (order, place, own, *rims, taps),
        FORWARD_SCRATCH,
        "first_forward",
    )
    own, rims, sums_one = apply_back(order, place, images, taps, sums_one)
    images, residual, applied, sums_two = call(
        second_forward_kernel,
        [IMAGES, FIELD, FIELD, SUMS],
        "ssvvvvvvvv",
        (order, place, sums_one, own, *rims, start, taps),
        FORWARD_SCRATCH,
        "second_forward",
    )
    own, rims, sums_two = apply_back(order, place, images, taps, sums_two)
    tile = ((TILE, TILE), F32)
    return tuple(
        call(
            last_kernel,
            [tile, tile],
            "svvvvvvvvvv",
            (place, sums_one, sums_two, own, *rims, start, applied, residual),
            [FIELD_SCRATCH],
            "finish",
        )
    )


def solution(mesh):
    torus = Mesh(mesh.devices.reshape(4, 2, 4, 4), TY_TX)
    in_specs = (
        P(TY_TX, None, None),
        P(TY_TX, None, None),
        P(TY_TX, None),
        P(TY_TX, None),
        P(TY_TX),
    )
    out_specs = (P(TY, TX), P(TY, TX))
    return jax.shard_map(body, mesh=torus, in_specs=in_specs, out_specs=out_specs, check_vma=False)
```

```python
import jax
import jax.numpy as jnp
from jax import lax
from jax.experimental import pallas as pl
from jax.experimental.pallas import tpu as pltpu
from jax.sharding import Mesh
from jax.sharding import PartitionSpec as P

TX = ("tx_0", "tx_1")
TY = ("ty_0", "ty_1")
TY_TX = TY + TX
N_TY, N_TX = 8, 16

SUB = 4
DAMPING = 0.05
FB = 8
CAP = 2
SLOTS = N_TX * CAP
TILE, BLOCK, HALO, TAPS, PSF = 512, 128, 16, 32, 31
EXT = TILE + 2 * HALO
LANES = 640
RIM = 2 * HALO
WIN = BLOCK + 2 * HALO
SLOT_ROWS = 160
GROUP = 8
BACK_GROUP = 4
COLUMNS = (0, 3, 1, 2)
CELL, SLOT, BOUND = 0, SLOTS + 1, 2 * SLOTS + 2
F32, BF16 = jnp.float32, jnp.bfloat16
FLOPS, BYTES = 3 * 10**9, 10**7
VMEM_BYTES = 26 << 20


def iota(shape, axis):
    return lax.broadcasted_iota(jnp.int32, shape, axis)


def by_group(lane, parts):
    low = jnp.where(lane < 32, parts[0], parts[1])
    high = jnp.where(lane < 96, parts[2], parts[3])
    return jnp.where(lane < 64, low, high)


def pack_kernel(warp, column, cell, spread_hbm, exposures_hbm, out_ref, points, images, pad, kern, sems):
    copies = [
        pltpu.make_async_copy(spread_hbm, points, sems.at[0]),
        pltpu.make_async_copy(exposures_hbm, images, sems.at[1]),
    ]
    for copy in copies:
        copy.start()
    for s in range(SLOTS):
        out_ref[s, 128:SLOT_ROWS, :] = jnp.zeros((SLOT_ROWS - 128, 128), BF16)
    pad[...] = jnp.zeros_like(pad)
    frame = iota((FB, 128), 0)
    row_frac, col_frac = jnp.zeros((FB, 128), F32), jnp.zeros((FB, 128), F32)
    for f in range(FB):
        row_frac = jnp.where(frame == f, warp[0, f].astype(F32) / SUB, row_frac)
        col_frac = jnp.where(frame == f, warp[1, f].astype(F32) / SUB, col_frac)
    copies[0].wait()
    pad[0:PSF, :, 0:PSF] = points[...]
    total = jnp.sum(jnp.sum(pad[...], axis=0), axis=1, keepdims=True)
    before = jnp.zeros((FB, 128), F32)
    for a in range(TAPS):
        point = pad[a] / total
        blended = (1.0 - col_frac) * point + col_frac * pltpu.roll(point, 1, 1)
        kern[FB * a : FB * a + FB, :] = (1.0 - row_frac) * blended + row_frac * before
        before = blended
    taps = kern[...].astype(BF16)
    row, lane = iota((128, 128), 0), iota((128, 128), 1)
    tall, wide = iota((32 * FB, 128), 0), iota((32 * FB, 128), 1)
    tap = tall >> 3
    place = jnp.where((lane & 31) == 31 - row, 1.0, 0.0).astype(BF16)
    spread = jnp.dot(taps, place, preferred_element_type=F32)
    spread = jnp.where((wide >> 5) == ((tap >> 2) & 3), spread, 0.0).astype(BF16)
    target, source = iota((8 * FB, 32 * FB), 0), iota((8 * FB, 32 * FB), 1)
    s_tap = source >> 3
    pick = ((source & 7) == (target >> 3)) & (
        (target & 7) == 2 * (s_tap & 3) + (s_tap >> 4)
    )
    backward = jnp.dot(
        jnp.where(pick, 1.0, 0.0).astype(BF16), spread, preferred_element_type=F32
    )
    place = jnp.where((lane & 63) == row, 1.0, 0.0).astype(BF16)
    spread = jnp.dot(taps, place, preferred_element_type=F32)
    spread = jnp.where((wide >> 6) == (tap & 1), spread, 0.0).astype(BF16)
    target, source = iota((16 * FB, 32 * FB), 0), iota((16 * FB, 32 * FB), 1)
    pick = ((source & 7) == (target >> 4)) & ((target & 15) == (source >> 4))
    ahead = jnp.dot(
        jnp.where(pick, 1.0, 0.0).astype(BF16), spread, preferred_element_type=F32
    )
    copies[1].wait()
    for f in range(FB):
        standing = jnp.int32(0)
        for g in range(f):
            standing = standing + jnp.where(column[g] == column[f], 1, 0)
        slot = CAP * column[f] + jnp.minimum(standing, CAP - 1)
        out_ref[slot, 0:BLOCK, :] = images[f].astype(BF16)
        tail = jnp.concatenate(
            [
                backward[8 * f : 8 * f + 8],
                ahead[16 * f : 16 * f + 16],
                jnp.broadcast_to((cell[f] + 1).astype(F32), (8, 128)),
            ],
            axis=0,
        )
        out_ref[slot, 128:SLOT_ROWS, :] = tail.astype(BF16)


def list_frames(cells, order):
    count = jnp.int32(0)
    order[BOUND] = count
    for k, column in enumerate(COLUMNS):
        for s in range(SLOTS):
            cell = cells[s] - 1
            order[CELL + count] = cell
            order[SLOT + count] = s
            listed = (cell >= 0) & ((cell & 3) == column)
            count = count + jnp.where(listed, 1, 0)
        order[BOUND + k + 1] = count


def build_ahead(taps, out):
    row, lane = iota((64, 128), 0), iota((64, 128), 1)
    offset = (lane & 31) + 31 - row
    inside = (offset >= 0) & (offset < 32)
    for a2 in range(4):
        for h in range(2):
            line = jnp.broadcast_to(taps[2 * a2 + h : 2 * a2 + h + 1], (64, 128))
            line = pltpu.roll(line, 97, 1, stride=1, stride_axis=0)
            out[64 * a2 : 64 * a2 + 64, 128 * h : 128 * h + 128] = jnp.where(
                inside, line, 0.0
            ).astype(BF16)


def build_back(taps, out):
    for a1 in range(8):
        for half in range(2):
            at = 8 + 2 * a1 + half
            line = jnp.broadcast_to(taps[at : at + 1], (32, 128))
            line = pltpu.roll(line, 0, 1, stride=1, stride_axis=0)
            out[32 * a1 : 32 * a1 + 32, 128 * half : 128 * half + 128] = line.astype(BF16)


def unfold(field, copies, doubled, stack):
    rows = 32
    source, target = iota((256, 512), 0), iota((256, 512), 1)
    copies[...] = jnp.where(source == 32 * (target >> 7) + (target & 63), 1.0, 0.0).astype(BF16)

    def columns(at, carry):
        both = pl.ds(pl.multiple_of(128 * at, 128), 256)
        wide = jnp.dot(field[:, both].astype(BF16), copies[...], preferred_element_type=F32)
        for k in range(4):
            doubled[k] = wide[:, 128 * k : 128 * k + 128]
        lane = iota((rows, 128), 1)
        for k in range(4):
            for r in range(0, EXT, rows):
                part = [doubled[k, r + a : r + a + rows] for a in range(4)]
                stack[4 * at + k, r : r + rows, 0:128] = jnp.where(
                    lane < 64, part[0], part[1]
                ).astype(BF16)
                stack[4 * at + k, r : r + rows, 128:256] = jnp.where(
                    lane < 64, part[2], part[3]
                ).astype(BF16)
        return carry

    lax.fori_loop(0, TILE // 128, columns, 0)


def folded_block(place, r):
    total, b = place
    lane = iota((32, 128), 1)
    even = total[b, r + 8 : r + 40, 0:128] + total[b, r + 6 : r + 38, 128:256]
    odd = total[b, r + 7 : r + 39, 0:128] + total[b, r + 5 : r + 37, 128:256]
    return jnp.where(lane < 64, even, odd)


def last_columns(place, r):
    before = folded_block(place, r)
    return pltpu.roll(before, 32, 1) + pltpu.roll(before, 96, 1)


def fold_rows(blocks, r, field, to):
    lane = iota((32, 128), 1)
    for at in range(TILE // 128):
        b0, b1, b2, b3 = [folded_block(blocks[4 * at + k], r) for k in range(4)]
        before = folded_block(blocks[4 * at - 1], r) if at else jnp.zeros_like(b3)
        even = jnp.where(lane < 64, b0, b2) + pltpu.roll(jnp.where(lane < 64, b2, b0), 64, 1)
        direct = jnp.where(lane < 64, b1, jnp.where(lane < 96, b3, before))
        turned = jnp.where(lane < 64, jnp.where(lane < 32, b3, before), b1)
        odd = pltpu.roll(direct, 32, 1) + pltpu.roll(turned, 96, 1)
        field[to : to + 32, 128 * at : 128 * at + 128] = even + odd
    field[to : to + 32, TILE:LANES] = jnp.where(lane < RIM, last_columns(blocks[-1], r), 0.0)


def left_rim(place, columns, rim):
    for r in range(0, EXT, 32):
        block = folded_block(place, r)
        columns[r : r + 32] = block + pltpu.roll(block, 64, 1)
    rim[...] = jnp.zeros_like(rim)
    for r in range(0, EXT, 128):
        n = min(128, EXT - r)
        rim[:, r : r + n] = columns[r : r + n].T[0:RIM]


def right_rim(place, columns, rim):
    for r in range(0, EXT, 32):
        columns[r : r + 32] = last_columns(place, r)
    rim[...] = jnp.zeros_like(rim)
    for r in range(0, EXT, 128):
        n = min(128, EXT - r)
        rim[:, r : r + n] = columns[r : r + n].T[0:RIM]


def order_rims(place, left, right, first_ref, second_ref):
    even = (place[1] & 1) == 0
    left, right = left[...], right[...]
    first_ref[...] = jnp.where(even, right, left)
    second_ref[...] = jnp.where(even, left, right)


def clear_total(total):
    def clear(b, carry):
        total[b] = jnp.zeros(total.shape[1:], F32)
        return carry

    lax.fori_loop(0, total.shape[0], clear, 0)


def expand(image, turned, spread):
    for d in range(4):
        turned[d, 16:144] = image if d == 0 else pltpu.roll(image, 32 * d, 1)
    lane = iota((144, 128), 1)
    for xb in range(4):
        parts = [turned[(j - xb) % 4, 16 - 4 * j : 160 - 4 * j] for j in range(4)]
        spread[xb, 16:160] = by_group(lane, parts).astype(BF16)


def add_window(spread, taps, total, block, top):
    both = jnp.concatenate([spread[:, 16:176], spread[:, 0:160]], axis=2).reshape(640, 256)
    window = jnp.dot(both, taps, preferred_element_type=F32).reshape(4, WIN, 256)
    at = pl.ds(pl.multiple_of(8 + top, 8), WIN)
    total[pl.ds(block, 4), at, :] += window


def clear_margins(turned, spread):
    for g in range(BACK_GROUP):
        turned[g, :, 0:16] = jnp.zeros((4, 16, 128), F32)
        turned[g, :, 144:160] = jnp.zeros((4, 16, 128), F32)
        spread[g, :, 0:16] = jnp.zeros((4, 16, 128), BF16)
        spread[g, :, 160:176] = jnp.zeros((4, 16, 128), BF16)


def over_frames(begin, end, size, step, carry):
    def group(k, carry):
        wanted = [begin + size * k + g for g in range(size)]
        return step([(jnp.minimum(i, end - 1), i < end) for i in wanted], carry)

    return lax.fori_loop(0, (end - begin + size - 1) // size, group, carry)


def place_of(order, i):
    cell = order[CELL + i]
    return 4 * (cell & 3), BLOCK * (cell >> 2)


def neighbours(index, size, first, second):
    even = (index & 1) == 0
    before = jnp.where(even, second, first)
    after = jnp.where(even, first, second)
    before = jnp.where(index > 0, before, 0.0)
    after = jnp.where(index < size - 1, after, 0.0)
    return before, after


def complete(place, own, rims, field):
    field[0:EXT, :] = own[...]
    field[EXT:, :] = jnp.zeros((field.shape[0] - EXT, LANES), F32)
    for r in range(0, EXT, 128):
        n = min(128, EXT - r)
        lanes = slice(r, r + 128)
        left, right = neighbours(place[1], N_TX, rims[0][:, lanes], rims[1][:, lanes])
        field[r : r + n, 0:RIM] += left.T[0:n]
        field[r : r + n, TILE:EXT] += right.T[0:n]
    above, below = neighbours(place[0], N_TY, rims[2][...], rims[3][...])
    field[0:RIM, :] += above
    field[TILE:EXT, :] += below

    @pl.when(place[0] == 0)
    def _():
        field[0:HALO, :] = jnp.zeros((HALO, LANES), F32)

    @pl.when(place[0] == N_TY - 1)
    def _():
        field[EXT - HALO : EXT, :] = jnp.zeros((HALO, LANES), F32)

    @pl.when(place[1] == 0)
    def _():
        field[0:EXT, 0:HALO] = jnp.zeros((EXT, HALO), F32)

    @pl.when(place[1] == N_TX - 1)
    def _():
        field[0:EXT, EXT - HALO : EXT] = jnp.zeros((EXT, HALO), F32)


def inner_sum(chunk_of):
    sums = jnp.zeros((1, 128), F32)
    lane = iota((32, LANES), 1)
    inside = (lane >= HALO) & (lane < HALO + TILE)
    for r in range(HALO, HALO + TILE, 32):
        chunk = jnp.where(inside, chunk_of(r, 32), 0.0)
        by_lane = jnp.sum(chunk, axis=0, keepdims=True)
        for x in range(0, LANES, 128):
            sums = sums + by_lane[:, x : x + 128]
    return sums


def add_frames(order, first, last, image_of, taps, total, block_of, turned, spread, build=None):
    clear_total(total)
    clear_margins(turned, spread)

    def step(members, carry):
        if build is not None:
            for i, _ in members:
                build(i)
        for g, (i, counts) in enumerate(members):
            image = jnp.where(counts, image_of(i).astype(F32), 0.0)
            expand(image, turned.at[g], spread.at[g])
        for g, (i, _) in enumerate(members):
            lx, top = place_of(order, i)
            add_window(spread.at[g], taps[i], total, block_of(lx), top)
        return carry

    begin, end = order[BOUND + first], order[BOUND + last]
    over_frames(begin, end, BACK_GROUP, step, 0)


def slot_readers(slots_ref, order, taps):
    def image_of(i):
        return slots_ref[order[SLOT + i], 0:BLOCK]

    def build(i):
        build_back(slots_ref[order[SLOT + i], BLOCK:SLOT_ROWS].astype(F32), taps.at[i])

    return image_of, build


def side_block(lx):
    return lx & 4


def middle_block(lx):
    return (lx >> 1) & 4


def only_block(lx):
    return 0


def sides_kernel(
    cells, place, slots_ref, order, total, taps, first_ref, second_ref,
    turned, spread, columns, left, right,
):
    list_frames(cells, order)
    image_of, build = slot_readers(slots_ref, order, taps)
    add_frames(order, 0, 2, image_of, taps, total, side_block, turned, spread, build)
    left_rim((total, 0), columns, left)
    right_rim((total, 7), columns, right)
    order_rims(place, left, right, first_ref, second_ref)


def side_blocks(side_total, total):
    sides = [(side_total, b) for b in range(8)]
    return sides[:4] + [(total, b) for b in range(8)] + sides[4:]


def column_blocks(*totals):
    return [(total, b) for total in totals for b in range(4)]


def middle_kernel(
    order, slots_ref, side_total, total, top_ref, bottom_ref, taps, turned, spread
):
    image_of, build = slot_readers(slots_ref, order, taps)
    add_frames(order, 2, 4, image_of, taps, total, middle_block, turned, spread, build)
    blocks = side_blocks(side_total, total)
    fold_rows(blocks, 0, top_ref, 0)
    fold_rows(blocks, TILE, bottom_ref, 0)


def first_fold_kernel(order, slots_ref, side_total, total, after, own_ref, taps):
    blocks = side_blocks(side_total, total)
    for r in range(0, EXT, 32):
        fold_rows(blocks, r, own_ref, r)

    def build(members, carry):
        for i, _ in members:
            build_ahead(slots_ref[order[SLOT + i], BLOCK:SLOT_ROWS].astype(F32), taps.at[i])
        return carry

    over_frames(0, order[BOUND + 4], BACK_GROUP, build, 0)


def fold_kernel(total_0, total_1, total_2, total_3, after, own_ref):
    blocks = column_blocks(total_0, total_1, total_2, total_3)
    for r in range(0, EXT, 32):
        fold_rows(blocks, r, own_ref, r)


def forward_pass(order, taps, field, images, scratch):
    stack, copies, doubled, product, paired = scratch
    unfold(field, copies, doubled, stack)

    def step(members, sums):
        for g, (i, _) in enumerate(members):
            lx, top = place_of(order, i)
            window = stack[pl.ds(lx, 4), pl.ds(pl.multiple_of(top, 128), WIN), :]
            product[g] = jnp.dot(
                window.reshape(4 * WIN, 256), taps[i], preferred_element_type=F32
            ).reshape(4, WIN, 256)
        for g, (i, counts) in enumerate(members):
            for xb in range(4):
                paired[g, xb] = product[g, xb, 0:144, 0:128] + product[g, xb, 16:160, 128:256]
            lane = iota((BLOCK, 128), 1)
            modelled = None
            for d in range(4):
                parts = [paired[g, (j + d) % 4, 4 * j : 4 * j + BLOCK] for j in range(4)]
                moved = by_group(lane, parts)
                moved = moved if d == 0 else pltpu.roll(moved, 32 * d, 1)
                modelled = moved if d == 0 else modelled + moved
            image = modelled.astype(BF16)
            images[i] = image
            square = jnp.sum(modelled * image.astype(F32), axis=0, keepdims=True)
            sums = sums + jnp.where(counts, square, 0.0)
        return sums

    return over_frames(0, order[BOUND + 4], GROUP, step, jnp.zeros((1, 128), F32))


def column_kernels():
    def add(k, order, images, taps, total, turned, spread):
        add_frames(order, k, k + 1, lambda i: images[i], taps, total, only_block, turned, spread)

    def left(order, images, taps, total, rim, turned, spread, columns):
        add(0, order, images, taps, total, turned, spread)
        left_rim((total, 0), columns, rim)

    def right(
        order, place, images, taps, left_ref, ahead, total, first_ref, second_ref,
        turned, spread, columns, rim,
    ):
        add(1, order, images, taps, total, turned, spread)
        right_rim((total, 3), columns, rim)
        order_rims(place, left_ref, rim, first_ref, second_ref)

    def inner(order, images, taps, ahead, total, turned, spread):
        add(2, order, images, taps, total, turned, spread)

    def last(
        order, images, taps, total_0, total_3, total_1, ahead, total, top_ref, bottom_ref,
        turned, spread,
    ):
        add(3, order, images, taps, total, turned, spread)
        blocks = column_blocks(total_0, total_1, total, total_3)
        fold_rows(blocks, 0, top_ref, 0)
        fold_rows(blocks, TILE, bottom_ref, 0)

    return left, right, inner, last


def first_forward_kernel(
    order, place, own_in, rim_l, rim_r, rim_a, rim_b, taps,
    images, residual_ref, sums_ref, field, *scratch,
):
    complete(place, own_in, (rim_l, rim_r, rim_a, rim_b), field)
    residual_ref[...] = field[0:EXT, :]
    square = inner_sum(lambda r, n: field[r : r + n, :] * field[r : r + n, :])
    curve = forward_pass(order, taps, field, images, scratch)
    sums_ref[...] = jnp.zeros_like(sums_ref)
    sums_ref[0:1] = square
    sums_ref[1:2] = curve


def first_step(sums):
    square = jnp.sum(sums[0:1], axis=1, keepdims=True)
    curve = jnp.sum(sums[1:2], axis=1, keepdims=True) + DAMPING * square
    return square, curve, square / curve


def second_forward_kernel(
    order, place, sums_in, own_in, rim_l, rim_r, rim_a, rim_b, start_ref, taps,
    images, residual_ref, applied_ref, sums_ref, field, *scratch,
):
    complete(place, own_in, (rim_l, rim_r, rim_a, rim_b), field)
    step = first_step(sums_in[...])[2]
    for r in range(0, EXT, 32):
        start = start_ref[r : r + 32]
        applied = field[r : r + 32, :] + DAMPING * start
        residual = start - step * applied
        applied_ref[r : r + 32] = applied
        residual_ref[r : r + 32] = residual
        field[r : r + 32, :] = residual
    square = inner_sum(lambda r, n: field[r : r + n, :] * field[r : r + n, :])
    cross = inner_sum(lambda r, n: field[r : r + n, :] * applied_ref[r : r + n, :])
    curve = forward_pass(order, taps, field, images, scratch)
    sums_ref[...] = jnp.zeros_like(sums_ref)
    sums_ref[0:1] = square
    sums_ref[1:2] = cross
    sums_ref[2:3] = curve


def last_kernel(
    place, sums_one, sums_two, own_in, rim_l, rim_r, rim_a, rim_b, start_ref, applied_ref,
    residual_ref, solution_out, residual_out, field,
):
    complete(place, own_in, (rim_l, rim_r, rim_a, rim_b), field)
    square_one, curve_one, step_one = first_step(sums_one[...])
    sums = sums_two[...]
    square_two = jnp.sum(sums[0:1], axis=1, keepdims=True)
    cross = jnp.sum(sums[1:2], axis=1, keepdims=True)
    curve = jnp.sum(sums[2:3], axis=1, keepdims=True) + DAMPING * square_two
    ratio = square_two / square_one
    curve_two = curve + 2.0 * ratio * cross + ratio * ratio * curve_one
    step_two = square_two / curve_two
    lane = iota((32, 128), 1)
    for r in range(0, TILE, 32):
        rows = slice(r + HALO, r + HALO + 32)
        start, residual = start_ref[rows], residual_ref[rows]
        applied = field[rows, :] + DAMPING * residual + ratio * applied_ref[rows]
        total = step_one * start + step_two * (residual + ratio * start)
        left = residual - step_two * applied
        for value, out in ((total, solution_out), (left, residual_out)):
            parts = [
                pltpu.roll(value[:, x : x + 128], 128 - HALO, 1) for x in range(0, LANES, 128)
            ]
            for x in range(TILE // 128):
                out[r : r + 32, 128 * x : 128 * x + 128] = jnp.where(
                    lane < 128 - HALO, parts[x], parts[x + 1]
                )


def corner_kernel(place, top_ref, bottom_ref, first_in, second_in, *rest):
    first_out, second_out, top, bottom = rest[-4:]
    top[...] = top_ref[...]
    bottom[...] = bottom_ref[...]
    left, right = neighbours(place[1], N_TX, first_in[...], second_in[...])
    for rim, at in ((left, 0), (right, TILE)):
        top[:, at : at + RIM] += rim[:, 0:128].T[0:RIM]
        bottom[:, at : at + RIM] += rim[:, TILE:LANES].T[0:RIM]
    even = (place[0] & 1) == 0
    first_out[...] = jnp.where(even, bottom[...], top[...])
    second_out[...] = jnp.where(even, top[...], bottom[...])


def call(kernel, outs, spaces, operands, scratch, name, vmem=VMEM_BYTES, out_spaces=None):
    specs = {
        "s": pl.BlockSpec(memory_space=pltpu.SMEM),
        "v": pl.BlockSpec(memory_space=pltpu.VMEM),
        "a": pl.BlockSpec(memory_space=pl.ANY),
        "h": pl.BlockSpec(memory_space=pltpu.HBM),
    }
    return pl.pallas_call(
        kernel,
        out_shape=[jax.ShapeDtypeStruct(shape, kind) for shape, kind in outs],
        in_specs=[specs[space] for space in spaces],
        out_specs=[specs[space] for space in out_spaces or "v" * len(outs)],
        scratch_shapes=scratch,
        compiler_params=pltpu.CompilerParams(vmem_limit_bytes=vmem),
        cost_estimate=pl.CostEstimate(flops=FLOPS, bytes_accessed=BYTES, transcendentals=0),
        name=name,
    )(*operands)


FIELD = ((EXT, LANES), F32)
RIM_ARRAY = ((RIM, LANES), F32)
SUMS = ((8, 128), F32)
ORDER = ((BOUND + 8,), jnp.int32)
ALL_TAPS = ((SLOTS, 256, 256), BF16)
TURNED = pltpu.VMEM((BACK_GROUP, 4, WIN, 128), F32)
SPREAD = pltpu.VMEM((BACK_GROUP, 4, WIN + 16, 128), BF16)
FIELD_SCRATCH = pltpu.VMEM((EXT + 8, LANES), F32)
IMAGES = ((SLOTS, BLOCK, BLOCK), BF16)
FORWARD_SCRATCH = [
    FIELD_SCRATCH,
    pltpu.VMEM((TILE // 32, EXT, 256), BF16),
    pltpu.VMEM((256, 512), BF16),
    pltpu.VMEM((4, EXT + 8, 128), F32),
    pltpu.VMEM((GROUP, 4, WIN, 256), F32),
    pltpu.VMEM((GROUP, 4, 144, 128), F32),
]
ADD_SCRATCH = [TURNED, SPREAD]
RIM_COLUMNS = pltpu.VMEM((EXT, 128), F32)
RIM_SCRATCH = pltpu.VMEM((RIM, LANES), F32)


def totals(blocks):
    return ((blocks, 8 + EXT, 256), F32)


def trade(first, second, axes, size):
    near = [(i, i ^ 1) for i in range(size)]
    far = [(i, ((i + 1) ^ 1) - 1) for i in range(1, size - 1)] + [(0, size - 1), (size - 1, 0)]
    return lax.ppermute(first, axes, near), lax.ppermute(second, axes, far)


def meet(value, axis):
    return value + lax.ppermute(value, axis, [(0, 1), (1, 0), (2, 3), (3, 2)])


def cross(value, axis):
    return value + lax.ppermute(value, axis, [(1, 2), (2, 1), (3, 0), (0, 3)])


def trade_rows(place, rims, top, bottom, beside, sums=None):
    ahead = () if sums is None else (sums,)
    rows = call(
        corner_kernel,
        [RIM_ARRAY, RIM_ARRAY],
        "svvvv" + "a" * len(ahead),
        (place, top, bottom, *rims, *ahead),
        [pltpu.VMEM((RIM, LANES), F32)] * 2,
        "corners",
    )
    if sums is not None:
        sums, *rows = lax.optimization_barrier((sums, *rows))
    rims = (*rims, *trade(*rows, TY, N_TY))
    if sums is not None:
        sums = sums + lax.ppermute(sums, "ty_1", [(0, 1), (1, 0)])
    result = beside(rows[0])
    if sums is not None:
        sums, result = lax.optimization_barrier((sums, result))
        sums = cross(meet(sums, "ty_0"), "ty_0")
    return result, rims, sums


def apply_back(order, place, images, taps, sums):
    left, right, inner, last = column_kernels()
    side_taps, middle_taps = taps
    sums = meet(sums, "tx_1")
    total_0, rim = call(
        left,
        [totals(4), RIM_ARRAY],
        "svv",
        (order, images, side_taps),
        ADD_SCRATCH + [RIM_COLUMNS],
        "left_column",
    )
    sums, rim = lax.optimization_barrier((sums, rim))
    next_sums = cross(sums, "tx_1")
    total_3, first, second = call(
        right,
        [totals(4), RIM_ARRAY, RIM_ARRAY],
        "ssvvva",
        (order, place, images, side_taps, rim, sums),
        ADD_SCRATCH + [RIM_COLUMNS, RIM_SCRATCH],
        "right_column",
    )
    sums, first, second = lax.optimization_barrier((next_sums, first, second))
    rims = trade(first, second, TX, N_TX)
    next_sums = meet(sums, "tx_0")
    (total_1,) = call(
        inner, [totals(4)], "svva", (order, images, middle_taps, sums), ADD_SCRATCH, "inner_column"
    )
    sums, total_1 = lax.optimization_barrier((next_sums, total_1))
    next_sums = cross(sums, "tx_0")
    total_2, top, bottom = call(
        last,
        [totals(4), RIM_ARRAY, RIM_ARRAY],
        "svvvvva",
        (order, images, middle_taps, total_0, total_3, total_1, sums),
        ADD_SCRATCH,
        "last_column",
    )
    sums, top, bottom = lax.optimization_barrier((next_sums, top, bottom))

    def beside(rim):
        operands = (total_0, total_1, total_2, total_3, rim)
        return call(fold_kernel, [FIELD], "vvvva", operands, [], "fold")[0]

    return trade_rows(place, rims, top, bottom, beside, sums)


def body(exposures, point_spread, warp_steps, column, block_cell):
    place = jnp.stack([lax.axis_index(TY), lax.axis_index(TX)]).astype(jnp.int32)
    names = (warp_steps.T, column[:, 0], block_cell)
    (sent,) = call(
        pack_kernel,
        [((SLOTS, SLOT_ROWS, 128), BF16)],
        "ssshh",
        (*names, point_spread.transpose(1, 0, 2), exposures),
        [
            pltpu.VMEM((PSF, FB, PSF), F32),
            pltpu.VMEM((FB, BLOCK, BLOCK), F32),
            pltpu.VMEM((TAPS, FB, 128), F32),
            pltpu.VMEM((TAPS * FB, 128), F32),
            pltpu.SemaphoreType.DMA((2,)),
        ],
        "pack",
        60 << 20,
    )
    slots = lax.all_to_all(
        sent.reshape(N_TX, CAP, SLOT_ROWS, 128), TX, split_axis=0, concat_axis=0, tiled=True
    ).reshape(SLOTS, SLOT_ROWS, 128)
    cells = slots[:, SLOT_ROWS - 8, 0].astype(jnp.int32)

    order, total, side_taps, first, second = call(
        sides_kernel,
        [ORDER, totals(8), ALL_TAPS, RIM_ARRAY, RIM_ARRAY],
        "ssv",
        (cells, place, slots),
        ADD_SCRATCH + [RIM_COLUMNS, RIM_SCRATCH, RIM_SCRATCH],
        "right_side_sides",
        out_spaces="svvvv",
    )
    rims = trade(first, second, TX, N_TX)
    inner, top, bottom, middle_taps = call(
        middle_kernel,
        [totals(8), RIM_ARRAY, RIM_ARRAY, ALL_TAPS],
        "svv",
        (order, slots, total),
        ADD_SCRATCH,
        "right_side_middle",
    )

    def beside(rim):
        return call(
            first_fold_kernel,
            [FIELD, ALL_TAPS],
            "svvva",
            (order, slots, total, inner, rim),
            [],
            "right_side_fold",
        )

    (own, ahead), rims, _ = trade_rows(place, rims, top, bottom, beside)
    back = (side_taps, middle_taps)
    images, start, sums_one = call(
        first_forward_kernel,
        [IMAGES, FIELD, SUMS],
        "ssvvvvvv",
        (order, place, own, *rims, ahead),
        FORWARD_SCRATCH,
        "first_forward",
    )
    own, rims, sums_one = apply_back(order, place, images, back, sums_one)
    images, residual, applied, sums_two = call(
        second_forward_kernel,
        [IMAGES, FIELD, FIELD, SUMS],
        "ssvvvvvvvv",
        (order, place, sums_one, own, *rims, start, ahead),
        FORWARD_SCRATCH,
        "second_forward",
    )
    own, rims, sums_two = apply_back(order, place, images, back, sums_two)
    tile = ((TILE, TILE), F32)
    return tuple(
        call(
            last_kernel,
            [tile, tile],
            "svvvvvvvvvv",
            (place, sums_one, sums_two, own, *rims, start, applied, residual),
            [FIELD_SCRATCH],
            "finish",
        )
    )


def solution(mesh):
    torus = Mesh(mesh.devices.reshape(4, 2, 4, 4), TY_TX)
    in_specs = (
        P(TY_TX, None, None),
        P(TY_TX, None, None),
        P(TY_TX, None),
        P(TY_TX, None),
        P(TY_TX),
    )
    out_specs = (P(TY, TX), P(TY, TX))
    return jax.shard_map(body, mesh=torus, in_specs=in_specs, out_specs=out_specs, check_vma=False)
```

```python
import jax
import jax.numpy as jnp
from jax import lax
from jax.experimental import pallas as pl
from jax.experimental.pallas import tpu as pltpu
from jax.sharding import Mesh
from jax.sharding import PartitionSpec as P

TX = ("tx_0", "tx_1")
TY = ("ty_0", "ty_1")
TY_TX = TY + TX
N_TY, N_TX = 8, 16

SUB = 4
DAMPING = 0.05
FB = 8
CAP = 2
SLOTS = N_TX * CAP
TILE, BLOCK, HALO, TAPS, PSF = 512, 128, 16, 32, 31
EXT = TILE + 2 * HALO
LANES = 640
RIM = 2 * HALO
WIN = BLOCK + 2 * HALO
SLOT_ROWS = 160
GROUP = 8
BACK_GROUP = 4
COLUMNS = (0, 3, 1, 2)
CELL, SLOT, BOUND = 0, SLOTS + 1, 2 * SLOTS + 2
F32, BF16 = jnp.float32, jnp.bfloat16
FLOPS, BYTES = 3 * 10**9, 10**7
VMEM_BYTES = 26 << 20


def iota(shape, axis):
    return lax.broadcasted_iota(jnp.int32, shape, axis)


def by_group(lane, parts):
    low = jnp.where(lane < 32, parts[0], parts[1])
    high = jnp.where(lane < 96, parts[2], parts[3])
    return jnp.where(lane < 64, low, high)


def pack_kernel(warp, column, cell, spread_hbm, exposures_hbm, out_ref, points, images, pad, kern, sems):
    copies = [
        pltpu.make_async_copy(spread_hbm, points, sems.at[0]),
        pltpu.make_async_copy(exposures_hbm, images, sems.at[1]),
    ]
    for copy in copies:
        copy.start()
    for s in range(SLOTS):
        out_ref[s, 128:SLOT_ROWS, :] = jnp.zeros((SLOT_ROWS - 128, 128), BF16)
    pad[...] = jnp.zeros_like(pad)
    frame = iota((FB, 128), 0)
    row_frac, col_frac = jnp.zeros((FB, 128), F32), jnp.zeros((FB, 128), F32)
    for f in range(FB):
        row_frac = jnp.where(frame == f, warp[0, f].astype(F32) / SUB, row_frac)
        col_frac = jnp.where(frame == f, warp[1, f].astype(F32) / SUB, col_frac)
    copies[0].wait()
    pad[0:PSF, :, 0:PSF] = points[...]
    total = jnp.sum(jnp.sum(pad[...], axis=0), axis=1, keepdims=True)
    before = jnp.zeros((FB, 128), F32)
    for a in range(TAPS):
        point = pad[a] / total
        blended = (1.0 - col_frac) * point + col_frac * pltpu.roll(point, 1, 1)
        kern[FB * a : FB * a + FB, :] = (1.0 - row_frac) * blended + row_frac * before
        before = blended
    taps = kern[...].astype(BF16)
    row, lane = iota((128, 128), 0), iota((128, 128), 1)
    tall, wide = iota((32 * FB, 128), 0), iota((32 * FB, 128), 1)
    tap = tall >> 3
    place = jnp.where((lane & 31) == 31 - row, 1.0, 0.0).astype(BF16)
    spread = jnp.dot(taps, place, preferred_element_type=F32)
    spread = jnp.where((wide >> 5) == ((tap >> 2) & 3), spread, 0.0).astype(BF16)
    target, source = iota((8 * FB, 32 * FB), 0), iota((8 * FB, 32 * FB), 1)
    s_tap = source >> 3
    pick = ((source & 7) == (target >> 3)) & (
        (target & 7) == 2 * (s_tap & 3) + (s_tap >> 4)
    )
    backward = jnp.dot(
        jnp.where(pick, 1.0, 0.0).astype(BF16), spread, preferred_element_type=F32
    )
    place = jnp.where((lane & 63) == row, 1.0, 0.0).astype(BF16)
    spread = jnp.dot(taps, place, preferred_element_type=F32)
    spread = jnp.where((wide >> 6) == (tap & 1), spread, 0.0).astype(BF16)
    target, source = iota((16 * FB, 32 * FB), 0), iota((16 * FB, 32 * FB), 1)
    pick = ((source & 7) == (target >> 4)) & ((target & 15) == (source >> 4))
    ahead = jnp.dot(
        jnp.where(pick, 1.0, 0.0).astype(BF16), spread, preferred_element_type=F32
    )
    copies[1].wait()
    for f in range(FB):
        standing = jnp.int32(0)
        for g in range(f):
            standing = standing + jnp.where(column[g] == column[f], 1, 0)
        slot = CAP * column[f] + jnp.minimum(standing, CAP - 1)
        out_ref[slot, 0:BLOCK, :] = images[f].astype(BF16)
        tail = jnp.concatenate(
            [
                backward[8 * f : 8 * f + 8],
                ahead[16 * f : 16 * f + 16],
                jnp.broadcast_to((cell[f] + 1).astype(F32), (8, 128)),
            ],
            axis=0,
        )
        out_ref[slot, 128:SLOT_ROWS, :] = tail.astype(BF16)


def list_frames(cells, order):
    count = jnp.int32(0)
    order[BOUND] = count
    for k, column in enumerate(COLUMNS):
        for s in range(SLOTS):
            cell = cells[s] - 1
            order[CELL + count] = cell
            order[SLOT + count] = s
            listed = (cell >= 0) & ((cell & 3) == column)
            count = count + jnp.where(listed, 1, 0)
        order[BOUND + k + 1] = count


def build_ahead(taps, out):
    row, lane = iota((64, 128), 0), iota((64, 128), 1)
    offset = (lane & 31) + 31 - row
    inside = (offset >= 0) & (offset < 32)
    for a2 in range(4):
        for h in range(2):
            line = jnp.broadcast_to(taps[2 * a2 + h : 2 * a2 + h + 1], (64, 128))
            line = pltpu.roll(line, 97, 1, stride=1, stride_axis=0)
            out[64 * a2 : 64 * a2 + 64, 128 * h : 128 * h + 128] = jnp.where(
                inside, line, 0.0
            ).astype(BF16)


def build_back(taps, out):
    for a1 in range(8):
        for half in range(2):
            at = 8 + 2 * a1 + half
            line = jnp.broadcast_to(taps[at : at + 1], (32, 128))
            line = pltpu.roll(line, 0, 1, stride=1, stride_axis=0)
            out[32 * a1 : 32 * a1 + 32, 128 * half : 128 * half + 128] = line.astype(BF16)


def unfold(field, copies, doubled, stack):
    rows = 32
    source, target = iota((256, 512), 0), iota((256, 512), 1)
    copies[...] = jnp.where(source == 32 * (target >> 7) + (target & 63), 1.0, 0.0).astype(BF16)

    def columns(at, carry):
        both = pl.ds(pl.multiple_of(128 * at, 128), 256)
        wide = jnp.dot(field[:, both].astype(BF16), copies[...], preferred_element_type=F32)
        for k in range(4):
            doubled[k] = wide[:, 128 * k : 128 * k + 128]
        lane = iota((rows, 128), 1)
        for k in range(4):
            for r in range(0, EXT, rows):
                part = [doubled[k, r + a : r + a + rows] for a in range(4)]
                stack[4 * at + k, r : r + rows, 0:128] = jnp.where(
                    lane < 64, part[0], part[1]
                ).astype(BF16)
                stack[4 * at + k, r : r + rows, 128:256] = jnp.where(
                    lane < 64, part[2], part[3]
                ).astype(BF16)
        return carry

    lax.fori_loop(0, TILE // 128, columns, 0)


def folded_block(place, r):
    total, b = place
    lane = iota((32, 128), 1)
    even = total[b, r + 8 : r + 40, 0:128] + total[b, r + 6 : r + 38, 128:256]
    odd = total[b, r + 7 : r + 39, 0:128] + total[b, r + 5 : r + 37, 128:256]
    return jnp.where(lane < 64, even, odd)


def last_columns(place, r):
    before = folded_block(place, r)
    return pltpu.roll(before, 32, 1) + pltpu.roll(before, 96, 1)


def fold_rows(blocks, r, field, to):
    lane = iota((32, 128), 1)
    for at in range(TILE // 128):
        b0, b1, b2, b3 = [folded_block(blocks[4 * at + k], r) for k in range(4)]
        before = folded_block(blocks[4 * at - 1], r) if at else jnp.zeros_like(b3)
        even = jnp.where(lane < 64, b0, b2) + pltpu.roll(jnp.where(lane < 64, b2, b0), 64, 1)
        direct = jnp.where(lane < 64, b1, jnp.where(lane < 96, b3, before))
        turned = jnp.where(lane < 64, jnp.where(lane < 32, b3, before), b1)
        odd = pltpu.roll(direct, 32, 1) + pltpu.roll(turned, 96, 1)
        field[to : to + 32, 128 * at : 128 * at + 128] = even + odd
    field[to : to + 32, TILE:LANES] = jnp.where(lane < RIM, last_columns(blocks[-1], r), 0.0)


def left_rim(place, columns, rim):
    for r in range(0, EXT, 32):
        block = folded_block(place, r)
        columns[r : r + 32] = block + pltpu.roll(block, 64, 1)
    rim[...] = jnp.zeros_like(rim)
    for r in range(0, EXT, 128):
        n = min(128, EXT - r)
        rim[:, r : r + n] = columns[r : r + n].T[0:RIM]


def right_rim(place, columns, rim):
    for r in range(0, EXT, 32):
        columns[r : r + 32] = last_columns(place, r)
    rim[...] = jnp.zeros_like(rim)
    for r in range(0, EXT, 128):
        n = min(128, EXT - r)
        rim[:, r : r + n] = columns[r : r + n].T[0:RIM]


def order_rims(place, left, right, first_ref, second_ref):
    even = (place[1] & 1) == 0
    left, right = left[...], right[...]
    first_ref[...] = jnp.where(even, right, left)
    second_ref[...] = jnp.where(even, left, right)


def clear_total(total):
    def clear(b, carry):
        total[b] = jnp.zeros(total.shape[1:], F32)
        return carry

    lax.fori_loop(0, total.shape[0], clear, 0)


def expand(image, turned, spread):
    for d in range(4):
        turned[d, 16:144] = image if d == 0 else pltpu.roll(image, 32 * d, 1)
    lane = iota((144, 128), 1)
    for xb in range(4):
        parts = [turned[(j - xb) % 4, 16 - 4 * j : 160 - 4 * j] for j in range(4)]
        spread[xb, 16:160] = by_group(lane, parts).astype(BF16)


def add_window(spread, taps, total, block, top):
    both = jnp.concatenate([spread[:, 16:176], spread[:, 0:160]], axis=2).reshape(640, 256)
    window = jnp.dot(both, taps, preferred_element_type=F32).reshape(4, WIN, 256)
    at = pl.ds(pl.multiple_of(8 + top, 8), WIN)
    total[pl.ds(block, 4), at, :] += window


def clear_margins(turned, spread):
    for g in range(BACK_GROUP):
        turned[g, :, 0:16] = jnp.zeros((4, 16, 128), F32)
        turned[g, :, 144:160] = jnp.zeros((4, 16, 128), F32)
        spread[g, :, 0:16] = jnp.zeros((4, 16, 128), BF16)
        spread[g, :, 160:176] = jnp.zeros((4, 16, 128), BF16)


def over_frames(begin, end, size, step, carry):
    def group(k, carry):
        wanted = [begin + size * k + g for g in range(size)]
        return step([(jnp.minimum(i, end - 1), i < end) for i in wanted], carry)

    return lax.fori_loop(0, (end - begin + size - 1) // size, group, carry)


def place_of(order, i):
    cell = order[CELL + i]
    return 4 * (cell & 3), BLOCK * (cell >> 2)


def neighbours(index, size, first, second):
    even = (index & 1) == 0
    before = jnp.where(even, second, first)
    after = jnp.where(even, first, second)
    before = jnp.where(index > 0, before, 0.0)
    after = jnp.where(index < size - 1, after, 0.0)
    return before, after


def complete(place, own, rims, field):
    field[0:EXT, :] = own[...]
    field[EXT:, :] = jnp.zeros((field.shape[0] - EXT, LANES), F32)
    for r in range(0, EXT, 128):
        n = min(128, EXT - r)
        lanes = slice(r, r + 128)
        left, right = neighbours(place[1], N_TX, rims[0][:, lanes], rims[1][:, lanes])
        field[r : r + n, 0:RIM] += left.T[0:n]
        field[r : r + n, TILE:EXT] += right.T[0:n]
    above, below = neighbours(place[0], N_TY, rims[2][...], rims[3][...])
    field[0:RIM, :] += above
    field[TILE:EXT, :] += below

    @pl.when(place[0] == 0)
    def _():
        field[0:HALO, :] = jnp.zeros((HALO, LANES), F32)

    @pl.when(place[0] == N_TY - 1)
    def _():
        field[EXT - HALO : EXT, :] = jnp.zeros((HALO, LANES), F32)

    @pl.when(place[1] == 0)
    def _():
        field[0:EXT, 0:HALO] = jnp.zeros((EXT, HALO), F32)

    @pl.when(place[1] == N_TX - 1)
    def _():
        field[0:EXT, EXT - HALO : EXT] = jnp.zeros((EXT, HALO), F32)


def inner_sum(chunk_of):
    sums = jnp.zeros((1, 128), F32)
    lane = iota((32, LANES), 1)
    inside = (lane >= HALO) & (lane < HALO + TILE)
    for r in range(HALO, HALO + TILE, 32):
        chunk = jnp.where(inside, chunk_of(r, 32), 0.0)
        by_lane = jnp.sum(chunk, axis=0, keepdims=True)
        for x in range(0, LANES, 128):
            sums = sums + by_lane[:, x : x + 128]
    return sums


def add_frames(order, first, last, image_of, taps, total, block_of, turned, spread, build=None):
    clear_total(total)
    clear_margins(turned, spread)

    def step(members, carry):
        if build is not None:
            for i, _ in members:
                build(i)
        for g, (i, counts) in enumerate(members):
            image = jnp.where(counts, image_of(i).astype(F32), 0.0)
            expand(image, turned.at[g], spread.at[g])
        for g, (i, _) in enumerate(members):
            lx, top = place_of(order, i)
            add_window(spread.at[g], taps[i], total, block_of(lx), top)
        return carry

    begin, end = order[BOUND + first], order[BOUND + last]
    over_frames(begin, end, BACK_GROUP, step, 0)


def slot_readers(slots_ref, order, taps):
    def image_of(i):
        return slots_ref[order[SLOT + i], 0:BLOCK]

    def build(i):
        build_back(slots_ref[order[SLOT + i], BLOCK:SLOT_ROWS].astype(F32), taps.at[i])

    return image_of, build


def side_block(lx):
    return lx & 4


def middle_block(lx):
    return (lx >> 1) & 4


def only_block(lx):
    return 0


def sides_kernel(
    cells, place, slots_ref, order, total, taps, first_ref, second_ref,
    turned, spread, columns, left, right,
):
    list_frames(cells, order)
    image_of, build = slot_readers(slots_ref, order, taps)
    add_frames(order, 0, 2, image_of, taps, total, side_block, turned, spread, build)
    left_rim((total, 0), columns, left)
    right_rim((total, 7), columns, right)
    order_rims(place, left, right, first_ref, second_ref)


def side_blocks(side_total, total):
    sides = [(side_total, b) for b in range(8)]
    return sides[:4] + [(total, b) for b in range(8)] + sides[4:]


def column_blocks(*totals):
    return [(total, b) for total in totals for b in range(4)]


def middle_kernel(
    order, slots_ref, side_total, total, top_ref, bottom_ref, taps, turned, spread
):
    image_of, build = slot_readers(slots_ref, order, taps)
    add_frames(order, 2, 4, image_of, taps, total, middle_block, turned, spread, build)
    blocks = side_blocks(side_total, total)
    fold_rows(blocks, 0, top_ref, 0)
    fold_rows(blocks, TILE, bottom_ref, 0)


def first_fold_kernel(order, slots_ref, side_total, total, after, own_ref, taps):
    blocks = side_blocks(side_total, total)
    for r in range(0, EXT, 32):
        fold_rows(blocks, r, own_ref, r)

    def build(members, carry):
        for i, _ in members:
            build_ahead(slots_ref[order[SLOT + i], BLOCK:SLOT_ROWS].astype(F32), taps.at[i])
        return carry

    over_frames(0, order[BOUND + 4], BACK_GROUP, build, 0)


def fold_kernel(total_0, total_1, total_2, total_3, after, own_ref):
    blocks = column_blocks(total_0, total_1, total_2, total_3)
    for r in range(0, EXT, 32):
        fold_rows(blocks, r, own_ref, r)


def forward_pass(order, taps, field, images, scratch):
    stack, copies, doubled, product, paired = scratch
    unfold(field, copies, doubled, stack)

    def step(members, sums):
        for g, (i, _) in enumerate(members):
            lx, top = place_of(order, i)
            window = stack[pl.ds(lx, 4), pl.ds(pl.multiple_of(top, 128), WIN), :]
            product[g] = jnp.dot(
                window.reshape(4 * WIN, 256), taps[i], preferred_element_type=F32
            ).reshape(4, WIN, 256)
        for g, (i, counts) in enumerate(members):
            for xb in range(4):
                paired[g, xb] = product[g, xb, 0:144, 0:128] + product[g, xb, 16:160, 128:256]
            lane = iota((BLOCK, 128), 1)
            modelled = None
            for d in range(4):
                parts = [paired[g, (j + d) % 4, 4 * j : 4 * j + BLOCK] for j in range(4)]
                moved = by_group(lane, parts)
                moved = moved if d == 0 else pltpu.roll(moved, 32 * d, 1)
                modelled = moved if d == 0 else modelled + moved
            image = modelled.astype(BF16)
            images[i] = image
            square = jnp.sum(modelled * image.astype(F32), axis=0, keepdims=True)
            sums = sums + jnp.where(counts, square, 0.0)
        return sums

    return over_frames(0, order[BOUND + 4], GROUP, step, jnp.zeros((1, 128), F32))


def column_kernels():
    def add(k, order, images, taps, total, turned, spread):
        add_frames(order, k, k + 1, lambda i: images[i], taps, total, only_block, turned, spread)

    def left(order, images, taps, total, rim, turned, spread, columns):
        add(0, order, images, taps, total, turned, spread)
        left_rim((total, 0), columns, rim)

    def right(
        order, place, images, taps, left_ref, ahead, total, first_ref, second_ref,
        turned, spread, columns, rim,
    ):
        add(1, order, images, taps, total, turned, spread)
        right_rim((total, 3), columns, rim)
        order_rims(place, left_ref, rim, first_ref, second_ref)

    def inner(order, images, taps, ahead, total, turned, spread):
        add(2, order, images, taps, total, turned, spread)

    def last(
        order, images, taps, total_0, total_3, total_1, ahead, total, top_ref, bottom_ref,
        turned, spread,
    ):
        add(3, order, images, taps, total, turned, spread)
        blocks = column_blocks(total_0, total_1, total, total_3)
        fold_rows(blocks, 0, top_ref, 0)
        fold_rows(blocks, TILE, bottom_ref, 0)

    return left, right, inner, last


def first_forward_kernel(
    order, place, own_in, rim_l, rim_r, rim_a, rim_b, taps,
    images, residual_ref, sums_ref, field, *scratch,
):
    complete(place, own_in, (rim_l, rim_r, rim_a, rim_b), field)
    residual_ref[...] = field[0:EXT, :]
    square = inner_sum(lambda r, n: field[r : r + n, :] * field[r : r + n, :])
    curve = forward_pass(order, taps, field, images, scratch)
    sums_ref[...] = jnp.zeros_like(sums_ref)
    sums_ref[0:1] = square
    sums_ref[1:2] = curve


def first_step(sums):
    square = jnp.sum(sums[0:1], axis=1, keepdims=True)
    curve = jnp.sum(sums[1:2], axis=1, keepdims=True) + DAMPING * square
    return square, curve, square / curve


def second_forward_kernel(
    order, place, sums_in, own_in, rim_l, rim_r, rim_a, rim_b, start_ref, taps,
    images, residual_ref, applied_ref, sums_ref, field, *scratch,
):
    complete(place, own_in, (rim_l, rim_r, rim_a, rim_b), field)
    step = first_step(sums_in[...])[2]
    for r in range(0, EXT, 32):
        start = start_ref[r : r + 32]
        applied = field[r : r + 32, :] + DAMPING * start
        residual = start - step * applied
        applied_ref[r : r + 32] = applied
        residual_ref[r : r + 32] = residual
        field[r : r + 32, :] = residual
    square = inner_sum(lambda r, n: field[r : r + n, :] * field[r : r + n, :])
    cross = inner_sum(lambda r, n: field[r : r + n, :] * applied_ref[r : r + n, :])
    curve = forward_pass(order, taps, field, images, scratch)
    sums_ref[...] = jnp.zeros_like(sums_ref)
    sums_ref[0:1] = square
    sums_ref[1:2] = cross
    sums_ref[2:3] = curve


def last_kernel(
    place, sums_one, sums_two, own_in, rim_l, rim_r, rim_a, rim_b, start_ref, applied_ref,
    residual_ref, solution_out, residual_out, field,
):
    complete(place, own_in, (rim_l, rim_r, rim_a, rim_b), field)
    square_one, curve_one, step_one = first_step(sums_one[...])
    sums = sums_two[...]
    square_two = jnp.sum(sums[0:1], axis=1, keepdims=True)
    cross = jnp.sum(sums[1:2], axis=1, keepdims=True)
    curve = jnp.sum(sums[2:3], axis=1, keepdims=True) + DAMPING * square_two
    ratio = square_two / square_one
    curve_two = curve + 2.0 * ratio * cross + ratio * ratio * curve_one
    step_two = square_two / curve_two
    lane = iota((32, 128), 1)
    for r in range(0, TILE, 32):
        rows = slice(r + HALO, r + HALO + 32)
        start, residual = start_ref[rows], residual_ref[rows]
        applied = field[rows, :] + DAMPING * residual + ratio * applied_ref[rows]
        total = step_one * start + step_two * (residual + ratio * start)
        left = residual - step_two * applied
        for value, out in ((total, solution_out), (left, residual_out)):
            parts = [
                pltpu.roll(value[:, x : x + 128], 128 - HALO, 1) for x in range(0, LANES, 128)
            ]
            for x in range(TILE // 128):
                out[r : r + 32, 128 * x : 128 * x + 128] = jnp.where(
                    lane < 128 - HALO, parts[x], parts[x + 1]
                )


def corner_kernel(place, top_ref, bottom_ref, first_in, second_in, *rest):
    first_out, second_out, top, bottom = rest[-4:]
    top[...] = top_ref[...]
    bottom[...] = bottom_ref[...]
    left, right = neighbours(place[1], N_TX, first_in[...], second_in[...])
    for rim, at in ((left, 0), (right, TILE)):
        top[:, at : at + RIM] += rim[:, 0:128].T[0:RIM]
        bottom[:, at : at + RIM] += rim[:, TILE:LANES].T[0:RIM]
    even = (place[0] & 1) == 0
    first_out[...] = jnp.where(even, bottom[...], top[...])
    second_out[...] = jnp.where(even, top[...], bottom[...])


def call(kernel, outs, spaces, operands, scratch, name, vmem=VMEM_BYTES, out_spaces=None):
    specs = {
        "s": pl.BlockSpec(memory_space=pltpu.SMEM),
        "v": pl.BlockSpec(memory_space=pltpu.VMEM),
        "a": pl.BlockSpec(memory_space=pl.ANY),
        "h": pl.BlockSpec(memory_space=pltpu.HBM),
    }
    return pl.pallas_call(
        kernel,
        out_shape=[jax.ShapeDtypeStruct(shape, kind) for shape, kind in outs],
        in_specs=[specs[space] for space in spaces],
        out_specs=[specs[space] for space in out_spaces or "v" * len(outs)],
        scratch_shapes=scratch,
        compiler_params=pltpu.CompilerParams(vmem_limit_bytes=vmem),
        cost_estimate=pl.CostEstimate(flops=FLOPS, bytes_accessed=BYTES, transcendentals=0),
        name=name,
    )(*operands)


FIELD = ((EXT, LANES), F32)
RIM_ARRAY = ((RIM, LANES), F32)
SUMS = ((8, 128), F32)
ORDER = ((BOUND + 8,), jnp.int32)
ALL_TAPS = ((SLOTS, 256, 256), BF16)
TURNED = pltpu.VMEM((BACK_GROUP, 4, WIN, 128), F32)
SPREAD = pltpu.VMEM((BACK_GROUP, 4, WIN + 16, 128), BF16)
FIELD_SCRATCH = pltpu.VMEM((EXT + 8, LANES), F32)
IMAGES = ((SLOTS, BLOCK, BLOCK), BF16)
FORWARD_SCRATCH = [
    FIELD_SCRATCH,
    pltpu.VMEM((TILE // 32, EXT, 256), BF16),
    pltpu.VMEM((256, 512), BF16),
    pltpu.VMEM((4, EXT + 8, 128), F32),
    pltpu.VMEM((GROUP, 4, WIN, 256), F32),
    pltpu.VMEM((GROUP, 4, 144, 128), F32),
]
ADD_SCRATCH = [TURNED, SPREAD]
RIM_COLUMNS = pltpu.VMEM((EXT, 128), F32)
RIM_SCRATCH = pltpu.VMEM((RIM, LANES), F32)


def totals(blocks):
    return ((blocks, 8 + EXT, 256), F32)


def trade(first, second, axes, size):
    near = [(i, i ^ 1) for i in range(size)]
    far = [(i, ((i + 1) ^ 1) - 1) for i in range(1, size - 1)] + [(0, size - 1), (size - 1, 0)]
    return lax.ppermute(first, axes, near), lax.ppermute(second, axes, far)


def meet(value, axis):
    return value + lax.ppermute(value, axis, [(0, 1), (1, 0), (2, 3), (3, 2)])


def cross(value, axis):
    return value + lax.ppermute(value, axis, [(1, 2), (2, 1), (3, 0), (0, 3)])


def trade_rows(place, rims, top, bottom, beside, sums=None):
    ahead = () if sums is None else (sums,)
    rows = call(
        corner_kernel,
        [RIM_ARRAY, RIM_ARRAY],
        "svvvv" + "a" * len(ahead),
        (place, top, bottom, *rims, *ahead),
        [pltpu.VMEM((RIM, LANES), F32)] * 2,
        "corners",
    )
    if sums is not None:
        sums, *rows = lax.optimization_barrier((sums, *rows))
    rims = (*rims, *trade(*rows, TY, N_TY))
    if sums is not None:
        sums = sums + lax.ppermute(sums, "ty_1", [(0, 1), (1, 0)])
    result = beside(rows[0])
    if sums is not None:
        sums, result = lax.optimization_barrier((sums, result))
        sums = cross(meet(sums, "ty_0"), "ty_0")
    return result, rims, sums


def apply_back(order, place, images, taps, sums):
    left, right, inner, last = column_kernels()
    side_taps, middle_taps = taps
    sums = meet(sums, "tx_1")
    total_0, rim = call(
        left,
        [totals(4), RIM_ARRAY],
        "svv",
        (order, images, side_taps),
        ADD_SCRATCH + [RIM_COLUMNS],
        "left_column",
    )
    sums, rim = lax.optimization_barrier((sums, rim))
    next_sums = cross(sums, "tx_1")
    total_3, first, second = call(
        right,
        [totals(4), RIM_ARRAY, RIM_ARRAY],
        "ssvvva",
        (order, place, images, side_taps, rim, sums),
        ADD_SCRATCH + [RIM_COLUMNS, RIM_SCRATCH],
        "right_column",
    )
    sums, first, second = lax.optimization_barrier((next_sums, first, second))
    rims = trade(first, second, TX, N_TX)
    next_sums = meet(sums, "tx_0")
    (total_1,) = call(
        inner, [totals(4)], "svva", (order, images, middle_taps, sums), ADD_SCRATCH, "inner_column"
    )
    sums, total_1 = lax.optimization_barrier((next_sums, total_1))
    next_sums = cross(sums, "tx_0")
    total_2, top, bottom = call(
        last,
        [totals(4), RIM_ARRAY, RIM_ARRAY],
        "svvvvva",
        (order, images, middle_taps, total_0, total_3, total_1, sums),
        ADD_SCRATCH,
        "last_column",
        16 << 20,
    )
    sums, top, bottom = lax.optimization_barrier((next_sums, top, bottom))

    def beside(rim):
        operands = (total_0, total_1, total_2, total_3, rim)
        return call(fold_kernel, [FIELD], "vvvva", operands, [], "fold", 16 << 20)[0]

    return trade_rows(place, rims, top, bottom, beside, sums)


def body(exposures, point_spread, warp_steps, column, block_cell):
    place = jnp.stack([lax.axis_index(TY), lax.axis_index(TX)]).astype(jnp.int32)
    names = (warp_steps.T, column[:, 0], block_cell)
    (sent,) = call(
        pack_kernel,
        [((SLOTS, SLOT_ROWS, 128), BF16)],
        "ssshh",
        (*names, point_spread.transpose(1, 0, 2), exposures),
        [
            pltpu.VMEM((PSF, FB, PSF), F32),
            pltpu.VMEM((FB, BLOCK, BLOCK), F32),
            pltpu.VMEM((TAPS, FB, 128), F32),
            pltpu.VMEM((TAPS * FB, 128), F32),
            pltpu.SemaphoreType.DMA((2,)),
        ],
        "pack",
        60 << 20,
    )
    slots = lax.all_to_all(
        sent.reshape(N_TX, CAP, SLOT_ROWS, 128), TX, split_axis=0, concat_axis=0, tiled=True
    ).reshape(SLOTS, SLOT_ROWS, 128)
    cells = slots[:, SLOT_ROWS - 8, 0].astype(jnp.int32)

    order, total, side_taps, first, second = call(
        sides_kernel,
        [ORDER, totals(8), ALL_TAPS, RIM_ARRAY, RIM_ARRAY],
        "ssv",
        (cells, place, slots),
        ADD_SCRATCH + [RIM_COLUMNS, RIM_SCRATCH, RIM_SCRATCH],
        "right_side_sides",
        out_spaces="svvvv",
    )
    rims = trade(first, second, TX, N_TX)
    inner, top, bottom, middle_taps = call(
        middle_kernel,
        [totals(8), RIM_ARRAY, RIM_ARRAY, ALL_TAPS],
        "svv",
        (order, slots, total),
        ADD_SCRATCH,
        "right_side_middle",
    )

    def beside(rim):
        return call(
            first_fold_kernel,
            [FIELD, ALL_TAPS],
            "svvva",
            (order, slots, total, inner, rim),
            [],
            "right_side_fold",
        )

    (own, ahead), rims, _ = trade_rows(place, rims, top, bottom, beside)
    back = (side_taps, middle_taps)
    images, start, sums_one = call(
        first_forward_kernel,
        [IMAGES, FIELD, SUMS],
        "ssvvvvvv",
        (order, place, own, *rims, ahead),
        FORWARD_SCRATCH,
        "first_forward",
    )
    own, rims, sums_one = apply_back(order, place, images, back, sums_one)
    images, residual, applied, sums_two = call(
        second_forward_kernel,
        [IMAGES, FIELD, FIELD, SUMS],
        "ssvvvvvvvv",
        (order, place, sums_one, own, *rims, start, ahead),
        FORWARD_SCRATCH,
        "second_forward",
    )
    own, rims, sums_two = apply_back(order, place, images, back, sums_two)
    tile = ((TILE, TILE), F32)
    return tuple(
        call(
            last_kernel,
            [tile, tile],
            "svvvvvvvvvv",
            (place, sums_one, sums_two, own, *rims, start, applied, residual),
            [FIELD_SCRATCH],
            "finish",
            12 << 20,
        )
    )


def solution(mesh):
    torus = Mesh(mesh.devices.reshape(4, 2, 4, 4), TY_TX)
    in_specs = (
        P(TY_TX, None, None),
        P(TY_TX, None, None),
        P(TY_TX, None),
        P(TY_TX, None),
        P(TY_TX),
    )
    out_specs = (P(TY, TX), P(TY, TX))
    return jax.shard_map(body, mesh=torus, in_specs=in_specs, out_specs=out_specs, check_vma=False)
```
